32 devices in a mesh: seq: 8 (over y, x, core), head: 4 (over z).
Axes of the slice: x: 2, y: 2, z: 4, core: 2. Of those that a mesh axis runs over, the one named last changes fastest.
Arguments:
- tokens: bfloat16 [2048, 2048], P('seq'), may hold values from -6 to 6
- w_query: bfloat16 [2048, 2048], P(None, 'head'), may hold values from -0.125 to 0.125
- w_key: bfloat16 [2048, 2048], P(None, 'head'), may hold values from -0.125 to 0.125
- w_value: bfloat16 [2048, 2048], P(None, 'head'), may hold values from -0.125 to 0.125
- w_beta: bfloat16 [2048, 16], P(None, 'head'), may hold values from -0.125 to 0.125
- b_beta: float32 [16], P('head'), may hold values from -6 to 1
- d_out: bfloat16 [2048, 2048], P('seq', 'head'), may hold values from -6 to 6
Outputs:
- d_x: bfloat16 [2048, 2048], P('seq', 'head')
- grad_query: float32 [2048, 2048], P('seq', 'head')
- grad_key: float32 [2048, 2048], P('seq', 'head')
- grad_value: float32 [2048, 2048], P('seq', 'head')
- grad_wbeta: float32 [2048, 16], P('seq', 'head')
- grad_bbeta: float32 [16], P('head')
The draws below stay inside these ranges and needn't reach their ends.
All inputs are finite; a program needn't handle non-finite values.
Results may differ from the reference program's by a relative error of at most 0.012.
Values may be sent and summed in bfloat16 or wider, within the bound.
A program may use at most 128 MiB of HBM per device.

```python
import jax
import jax.numpy as jnp
from jax import lax

H = 16
DK = 128
D = 2048
SPAN = 64
TOKENS = 2048


def with_spikes(result, key, source, target, parts, factor):
    owner, partner = [(jnp.arange(result.shape[dim]) // (result.shape[dim] // parts)).reshape([-1 if axis == dim else 1 for axis in range(result.ndim)]) for dim in (source, target)]
    chosen = jax.random.permutation(key, parts)[partner]
    strong = (owner == chosen) | (owner == (partner + parts // 2) % parts)
    return jnp.where(strong, factor * result, result)


def levels(own_key, dims, cuts, low, top_value):
    def one(position, blocks):
        draws = jax.random.uniform(jax.random.fold_in(jax.random.fold_in(own_key, 6), position), (blocks,), jnp.float32, low / len(cuts), top_value / len(cuts))
        return jnp.repeat(jnp.exp(draws), dims[position] // blocks).reshape((-1,) + (1,) * (len(dims) - position - 1))

    gain = one(*cuts[0])
    for cut in cuts[1:]:
        gain = gain * one(*cut)
    return gain


def centred(stream_key, extent, width, bound, cuts=(), held_as=jnp.bfloat16):
    values = jax.random.normal(stream_key, extent, jnp.float32) * width
    if len(cuts) > 0:
        values = levels(stream_key, extent, cuts, -0.22, 0.18) * values
    return jnp.clip(values, min=-bound, max=bound).astype(held_as)


def bell_draw_with(stream_key, extent, deviation, limit, cuts, heavy, kind=jnp.bfloat16):
    values = deviation * jax.random.normal(stream_key, extent, jnp.float32)
    if cuts:
        values = values * levels(stream_key, extent, cuts, -0.22, 0.18)
    return jnp.clip(with_spikes(values, jax.random.fold_in(stream_key, 3), *heavy), -limit, limit).astype(kind)


def setup_inputs(seed: int = 0) -> dict:
    key_list = jax.random.split(jax.random.key(seed), 8)
    tokens = bell_draw_with(key_list[0], (TOKENS, D), 1.0, 6.0, ((0, 8),), (0, 1, 8, 2.0))
    w_query = centred(key_list[1], (D, D), D ** -0.5, 0.125, ((1, 4),))
    w_key = centred(key_list[2], (D, D), D ** -0.5, 0.125, ((1, 4),))
    w_value = centred(key_list[3], (D, D), D ** -0.5, 0.125, ((1, 4),))
    w_beta = centred(key_list[4], (D, H), D ** -0.5, 0.125, ((1, 4),))
    b_beta = jnp.clip(-6.0 + 7.0 * jax.random.uniform(key_list[5], (H,), jnp.float32) ** levels(key_list[5], (H,), ((0, 4),), -0.2, 0.2), -6.0, 1.0)
    d_out = centred(key_list[6], (TOKENS, D), 1.0, 6.0, ((0, 8), (1, 4)))
    return {"tokens": tokens, "w_query": w_query, "w_key": w_key, "w_value": w_value, "w_beta": w_beta, "b_beta": b_beta, "d_out": d_out}


highest = lax.Precision.HIGHEST
epsilon = 1e-06

def delta_block(carry_state, query_block, key_block, value_block, beta_block):
    block_len = key_block.shape[1]
    strict_lower = jnp.tril(jnp.ones((block_len, block_len), key_block.dtype), -1)
    with_diagonal = jnp.tril(jnp.ones((block_len, block_len), key_block.dtype))
    weighted = beta_block[..., None] * key_block
    gram_matrix = jnp.einsum('hcd,hed->hce', weighted, key_block, precision=highest)
    system = jnp.eye(block_len, dtype=key_block.dtype) + gram_matrix * strict_lower
    w_block = lax.linalg.triangular_solve(system, weighted, left_side=True, lower=True, unit_diagonal=True)
    u_block = lax.linalg.triangular_solve(system, beta_block[..., None] * value_block, left_side=True, lower=True, unit_diagonal=True)
    updates = u_block - jnp.einsum('hcd,hvd->hcv', w_block, carry_state, precision=highest)
    scores = jnp.einsum('hcd,hed->hce', query_block, key_block, precision=highest) * with_diagonal
    outputs = jnp.einsum('hcd,hvd->hcv', query_block, carry_state, precision=highest)
    outputs = outputs + jnp.einsum('hce,hev->hcv', scores, updates, precision=highest)
    carry_state = carry_state + jnp.einsum('hcv,hcd->hvd', updates, key_block, precision=highest)
    return (carry_state, outputs, w_block)

def arrange(tensor):
    blocks_count = tensor.shape[0] // SPAN
    shaped = tensor.reshape((blocks_count, SPAN) + tensor.shape[1:])
    return jnp.swapaxes(shaped, 1, 2)

def prepare(query_raw, key_raw, value_raw, logits):
    query_norm = query_raw * lax.rsqrt(lax.optimization_barrier(jnp.sum(query_raw * query_raw, -1, keepdims=True)) + epsilon)
    key_norm = key_raw * lax.rsqrt(lax.optimization_barrier(jnp.sum(key_raw * key_raw, -1, keepdims=True)) + epsilon)
    beta_gate = 2.0 * jax.nn.sigmoid(logits)
    return (arrange(query_norm), arrange(key_norm), arrange(value_raw), arrange(beta_gate))

def delta_layer(query_raw, key_raw, value_raw, logits, initial):
    token_count, head_count, head_width = query_raw.shape
    arranged = prepare(query_raw, key_raw, value_raw, logits)

    def advance(carry_state, pieces):
        carry_state, outputs, unused = delta_block(carry_state, pieces[0], pieces[1], pieces[2], pieces[3])
        return (carry_state, outputs)
    last_state, outputs = lax.scan(jax.checkpoint(advance), initial, arranged)
    outputs = jnp.swapaxes(outputs, 1, 2).reshape(token_count, head_count, head_width)
    return (outputs, last_state)

def reference(tokens, w_query, w_key, w_value, w_beta, b_beta, d_out):
    token_count = tokens.shape[0]
    query_raw = jnp.dot(tokens.astype(jnp.float32), w_query.astype(jnp.float32), preferred_element_type=jnp.float32).reshape(token_count, H, DK)
    key_raw = jnp.dot(tokens.astype(jnp.float32), w_key.astype(jnp.float32), preferred_element_type=jnp.float32).reshape(token_count, H, DK)
    value_raw = jnp.dot(tokens.astype(jnp.float32), w_value.astype(jnp.float32), preferred_element_type=jnp.float32).reshape(token_count, H, DK)
    logits = jnp.dot(tokens.astype(jnp.float32), w_beta.astype(jnp.float32), preferred_element_type=jnp.float32) + b_beta
    initial = jnp.zeros((H, DK, DK), jnp.float32)

    def forward(first_in, second_in, third_in, fourth_in):
        return delta_layer(first_in, second_in, third_in, fourth_in, initial)[0]
    unused, pull_back = jax.vjp(forward, query_raw, key_raw, value_raw, logits)
    cotangent = d_out.astype(jnp.float32).reshape(token_count, H, DK)
    grad_q, grad_k, grad_v, grad_z = pull_back(cotangent)
    query_b = grad_q.reshape(token_count, D).astype(jnp.bfloat16)
    key_b = grad_k.reshape(token_count, D).astype(jnp.bfloat16)
    value_b = grad_v.reshape(token_count, D).astype(jnp.bfloat16)
    logit_b = grad_z.astype(jnp.bfloat16)
    input_grad = jnp.dot(query_b.astype(jnp.float32), w_query.T.astype(jnp.float32), preferred_element_type=jnp.float32)
    input_grad = input_grad + jnp.dot(key_b.astype(jnp.float32), w_key.T.astype(jnp.float32), preferred_element_type=jnp.float32)
    input_grad = input_grad + jnp.dot(value_b.astype(jnp.float32), w_value.T.astype(jnp.float32), preferred_element_type=jnp.float32)
    input_grad = input_grad + jnp.dot(logit_b.astype(jnp.float32), w_beta.T.astype(jnp.float32), preferred_element_type=jnp.float32)
    d_x = input_grad.astype(jnp.bfloat16)
    grad_query = jnp.dot(tokens.T.astype(jnp.float32), query_b.astype(jnp.float32), preferred_element_type=jnp.float32)
    grad_key = jnp.dot(tokens.T.astype(jnp.float32), key_b.astype(jnp.float32), preferred_element_type=jnp.float32)
    grad_value = jnp.dot(tokens.T.astype(jnp.float32), value_b.astype(jnp.float32), preferred_element_type=jnp.float32)
    grad_wbeta = jnp.dot(tokens.T.astype(jnp.float32), logit_b.astype(jnp.float32), preferred_element_type=jnp.float32)
    grad_bbeta = lax.optimization_barrier(jnp.sum(grad_z, 0))
    return (d_x, grad_query, grad_key, grad_value, grad_wbeta, grad_bbeta)
```

```python
import functools

import jax
import jax.numpy as jnp
from jax import lax
from jax.experimental import pallas as pl
from jax.experimental.pallas import tpu as pltpu
from jax.sharding import PartitionSpec as P

epsilon = 1e-06
LANES = 128
MESH = pl.DeviceIdType.MESH
highest = lax.Precision.HIGHEST


def split(a):
    high = a.astype(jnp.bfloat16)
    return high, (a - high.astype(jnp.float32)).astype(jnp.bfloat16)


def only(a):
    return a.astype(jnp.bfloat16), None


def mm(a, b, dims=(1, 0)):
    numbers = (((dims[0],), (dims[1],)), ((), ()))
    dot = functools.partial(
        lax.dot_general, dimension_numbers=numbers, preferred_element_type=jnp.float32
    )
    total = dot(a[0], b[0])
    if b[1] is not None:
        total = total + dot(a[0], b[1])
    if a[1] is not None:
        total = total + dot(a[1], b[0])
    return total


def iotas(rows, cols):
    return (
        lax.broadcasted_iota(jnp.int32, (rows, cols), 0),
        lax.broadcasted_iota(jnp.int32, (rows, cols), 1),
    )


def invert_unit_lower(systems):
    size = systems[0].shape[0]
    base = min(size, LANES)
    row, col = iotas(base, base)
    eye = jnp.where(row == col, 1.0, 0.0).astype(jnp.float32)

    def step_mask(s):
        return (row // (2 * s) == col // (2 * s)) & (row % (2 * s) >= s) & (col % (2 * s) < s)

    count = size // base
    diagonals = [
        n[i * base : (i + 1) * base, i * base : (i + 1) * base] for n in systems for i in range(count)
    ]
    inverses = [eye - jnp.where(step_mask(1), n, 0.0) for n in diagonals]
    s = 2
    while s < base:
        mask = step_mask(s)
        parts = [split(x) for x in inverses]
        inner = [mm(split(jnp.where(mask, n, 0.0)), x) for n, x in zip(diagonals, parts)]
        outer = [mm(x, split(y)) for x, y in zip(parts, inner)]
        inverses = [x - y for x, y in zip(inverses, outer)]
        s *= 2
    grouped = [inverses[i * count : (i + 1) * count] for i in range(len(systems))]
    width = base
    while width < size:
        merged = []
        for n, blocks in zip(systems, grouped):
            joined = []
            for i in range(0, len(blocks), 2):
                first, second = blocks[i], blocks[i + 1]
                low = n[(i + 1) * width : (i + 2) * width, i * width : (i + 1) * width]
                corner = mm(split(second), split(mm(split(low), split(first))))
                joined.append(
                    jnp.concatenate(
                        [
                            jnp.concatenate([first, jnp.zeros_like(first)], 1),
                            jnp.concatenate([-corner, second], 1),
                        ],
                        0,
                    )
                )
            merged.append(joined)
        grouped = merged
        width *= 2
    return [g[0] for g in grouped]


def normalise(raw):
    scale = lax.rsqrt(jnp.sum(raw * raw, -1, keepdims=True) + epsilon)
    return raw * scale, scale


def dot(a, b, dims=(1, 0)):
    return lax.dot_general(
        a, b, (((dims[0],), (dims[1],)), ((), ())), preferred_element_type=jnp.float32
    )


def summarise(heads, dim, q_ref, k_ref, v_ref, z_ref, g_ref, put_map):
    count = q_ref.shape[0]
    row, col = iotas(count, count)
    strict, inclusive = row > col, row >= col
    every = range(heads)
    cols = [slice(h * dim, (h + 1) * dim) for h in every]
    beta_all = 2.0 * jax.nn.sigmoid(z_ref[...])
    beta = [beta_all[:, h : h + 1] for h in every]
    qn = [normalise(q_ref[:, c])[0] for c in cols]
    kn = [normalise(k_ref[:, c])[0] for c in cols]
    ks = [split(x) for x in kn]
    qs = [split(x) for x in qn]
    gs = [(g_ref[:, c], None) for c in cols]
    gram = [jnp.where(strict, mm(x, x, (1, 1)), 0.0) for x in ks]
    inverse = [split(t) for t in invert_unit_lower([b * n for b, n in zip(beta, gram)])]
    gram = [split(n) for n in gram]
    scores = [split(jnp.where(inclusive, mm(a, b, (1, 1)), 0.0)) for a, b in zip(qs, ks)]
    back = [mm(p, g, (0, 0)) for p, g in zip(scores, gs)]
    forth_in = [jnp.concatenate([v_ref[:, c], k], 1) for c, k in zip(cols, kn)]
    forth = [split(mm(t, split(b * x))) for t, b, x in zip(inverse, beta, forth_in)]
    adjoint = [
        mm(t, split(jnp.concatenate([p, k], 1)), (0, 0)) for t, p, k in zip(inverse, back, kn)
    ]
    ends = [mm(f, k, (0, 0)) for f, k in zip(forth, ks)]
    tails = [mm(split(a), split(b * k), (0, 0)) for a, b, k in zip(adjoint, beta, kn)]
    direct = [mm(g, q, (0, 0)) for g, q in zip(gs, qs)]
    for h in every:
        put_map(h, ends[h][dim:], ends[h][:dim])
        put_map(heads + h, tails[h][dim:], direct[h] - tails[h][:dim])

    def put_mid(mid_ref):
        for h in every:
            mid_ref[h, :, : 2 * dim] = forth_in[h] - mm(gram[h], forth[h])
            mid_ref[h, :, 2 * dim :] = adjoint[h]

    return put_mid


def summary_kernel(heads, dim, q_ref, k_ref, v_ref, z_ref, g_ref, map_ref, mid_ref):
    def put_map(unit, factor, offset):
        map_ref[unit, 0] = factor.astype(map_ref.dtype)
        map_ref[unit, 1] = offset.astype(map_ref.dtype)

    summarise(heads, dim, q_ref, k_ref, v_ref, z_ref, g_ref, put_map)(mid_ref)


def gradients(heads, dim, every, q_ref, k_ref, z_ref, g_ref, mid_ref, state, put):
    count = q_ref.shape[0]
    row, col = iotas(count, count)
    strict, inclusive = row > col, row >= col
    beta_all = 2.0 * jax.nn.sigmoid(z_ref[...])
    cols = [slice(h * dim, (h + 1) * dim) for h in every]
    beta = [beta_all[:, h : h + 1] for h in every]
    qp = [normalise(q_ref[:, c]) for c in cols]
    kp = [normalise(k_ref[:, c]) for c in cols]
    ks = [split(x[0]) for x in kp]
    qs = [split(x[0]) for x in qp]
    gs = [(g_ref[:, c], None) for c in cols]
    ss = [(state(h), None) for h in every]
    ds = [(state(heads + h), None) for h in every]
    plain = [
        mid_ref[h, :, :dim] - mm(split(mid_ref[h, :, dim : 2 * dim]), s, (1, 1))
        for h, s in zip(every, ss)
    ]
    dx = [
        mid_ref[h, :, 2 * dim : 3 * dim] + mm(split(mid_ref[h, :, 3 * dim :]), d, (1, 1))
        for h, d in zip(every, ds)
    ]
    us = [split(b * x) for b, x in zip(beta, plain)]
    dv = [b * x for b, x in zip(beta, dx)]
    dvs = [split(x) for x in dv]
    inner = [split(jnp.where(inclusive, mm(g, u, (1, 1)), 0.0)) for g, u in zip(gs, us)]
    pair = [jnp.where(strict, mm(d, u, (1, 1)), 0.0) for d, u in zip(dvs, us)]
    both = [split(e + e.T) for e in pair]
    dqn = [mm(g, s) + mm(i, k) for g, s, i, k in zip(gs, ss, inner, ks)]
    dkn = [
        mm(i, q, (0, 0)) + mm(u, d) - mm(x, s) - mm(e, k)
        for i, q, u, d, x, s, e, k in zip(inner, qs, us, ds, dvs, ss, both, ks)
    ]

    def through(grad, pair):
        unit, scale = pair
        return scale * (grad - unit * jnp.sum(unit * grad, -1, keepdims=True))

    dz = []
    for i, h in enumerate(every):
        put(0, h, through(dqn[i], qp[i]).astype(jnp.bfloat16))
        put(1, h, through(dkn[i], kp[i]).astype(jnp.bfloat16))
        put(2, h, dv[i].astype(jnp.bfloat16))
        dz.append(jnp.sum(dx[i] * plain[i], -1, keepdims=True) * beta[i] * (1.0 - 0.5 * beta[i]))
    return dz


def strength_lanes(heads, dz):
    lane = lax.broadcasted_iota(jnp.int32, (dz[0].shape[0], LANES), 1)
    last = jnp.zeros((dz[0].shape[0], LANES), jnp.float32)
    for h in range(heads):
        high, low = split(dz[h])
        last = jnp.where(lane == h, high.astype(jnp.float32), last)
        last = jnp.where(lane == heads + h, low.astype(jnp.float32), last)
    return last.astype(jnp.bfloat16)


def gradient_kernel(heads, dim, q_ref, k_ref, z_ref, g_ref, mid_ref, state_ref, out_ref):
    width = heads * dim

    def put(i, h, value):
        out_ref[:, i * width + h * dim : i * width + (h + 1) * dim] = value

    dz = gradients(
        heads, dim, range(heads), q_ref, k_ref, z_ref, g_ref, mid_ref,
        lambda unit: state_ref[unit], put,
    )
    out_ref[:, 3 * width :] = strength_lanes(heads, dz)


def gathered_states(maps, heads):
    count = lax.axis_size("seq")
    place = lax.axis_index("seq")
    gathered = lax.all_gather(maps, "seq").astype(jnp.float32)

    def walk(steps, pick, rows):
        def one(lap, state):
            pair = lax.dynamic_index_in_dim(gathered, pick(lap), 0, False)[rows]
            moved = jnp.einsum("hij,hjk->hik", state, pair[:, 0], precision=highest)
            return state - moved + pair[:, 1]

        return lax.fori_loop(0, steps, one, jnp.zeros((heads,) + maps.shape[2:], jnp.float32))

    first = walk(place, lambda lap: lap, slice(0, heads))
    second = walk(count - 1 - place, lambda lap: count - 1 - lap, slice(heads, None))
    return jnp.concatenate([first, second]).astype(maps.dtype)


def layer_kernel(
    groups, heads, dim,
    x_hbm, wq_hbm, wk_hbm, wv_hbm, g_hbm, wb_ref, b_ref,
    dx_ref, gq_ref, gk_ref, gv_ref, tail_ref,
    x, w, wb, g, qkv, z, mid, maps, x_out, x_in, y_out, y_in, state,
    cols, cols_t, mine, blocks, tails, part_out, part_in, tail_out, tail_in,
    own, piece, landed, relay,
    load, tok_send, tok_recv, map_send, map_recv, x_send, x_recv, f_send, f_recv,
    y_send, y_recv, far_send, far_recv, sib_send, sib_recv, fwd_send, fwd_recv,
    part_send, part_recv, z_send, z_recv, relay_recv,
):
    me = lax.axis_index("seq")
    group = lax.axis_index("head")
    core, across, upper = me % 2, (me // 2) % 2, me // 4
    rows, width = g.shape
    part = cols.shape[-1]
    half = heads // 2
    f32, bf16 = jnp.float32, jnp.bfloat16

    def seq(o):
        index = me
        for bit in (1, 2, 4):
            if o & bit:
                index = index + bit - 2 * bit * ((me // bit) % 2)
        return index

    def remote(source, target, send, recv, device):
        return pltpu.make_async_remote_copy(
            src_ref=source,
            dst_ref=target,
            send_sem=send,
            recv_sem=recv,
            device_id=device if isinstance(device, dict) else {"seq": seq(device)},
            device_id_type=MESH,
        )

    pairs = ((x_hbm, x), (wq_hbm, w.at[0]), (wk_hbm, w.at[1]), (wv_hbm, w.at[2]), (g_hbm, g))
    loads = [pltpu.make_async_copy(s, t, load.at[i]) for i, (s, t) in enumerate(pairs)]
    for copy in loads:
        copy.start()
    barrier = pltpu.get_barrier_semaphore()
    others = [{"seq": seq(o)} for o in range(1, 8)]
    others += [{"head": lax.rem(group + r, groups)} for r in range(1, groups)]
    for peer in others:
        pl.semaphore_signal(barrier, inc=1, device_id=peer, device_id_type=MESH)
    wb[...] = jnp.zeros_like(wb)
    wb[pl.ds(0, heads), :] = wb_ref[...]
    loads[0].wait()
    loads[1].wait()
    qkv[0] = dot(x[...], w[0])
    pl.semaphore_wait(barrier, len(others))

    fars, partners = (2, 4), (4, 2)
    slots = [(0, 1, far, far ^ 1) for far in fars]

    def columns(index):
        return pl.ds(pl.multiple_of(index * part, part), part)

    tokens = []
    for a in range(2):
        for s in range(1, 4):
            for b in range(2):
                if (a, s, b) != (1, 1, 0):
                    owner = seq(slots[a][s] ^ (partners[a] if b else 0))
                    i = len(tokens)
                    tokens.append(
                        remote(
                            x.at[:, columns(owner)], cols.at[a, s, b],
                            tok_send.at[i], tok_recv.at[i], slots[a][s],
                        )
                    )
                    tokens[i].start()

    loads[2].wait()
    qkv[1] = dot(x[...], w[1])
    loads[3].wait()
    qkv[2] = dot(x[...], w[2])
    z[...] = dot(x[...], wb[...], (1, 1))
    z[:, :heads] = z[:, :heads] + b_ref[...]
    loads[4].wait()

    def put_map(unit, factor, offset):
        maps[core, unit, 0] = factor.astype(bf16)
        maps[core, unit, 1] = offset.astype(bf16)

    put_mid = summarise(heads, dim, qkv.at[0], qkv.at[1], qkv.at[2], z, g, put_map)
    sibling = remote(maps.at[core], maps.at[core], map_send, map_recv, 1)
    sibling.start()
    put_mid(mid)
    sibling.wait_recv()

    passed, taken = across, 1 - across
    kept = pl.ds(core * half, half)

    def chip_total(way, n):
        unit = way * heads + core * half + n
        first = jnp.concatenate([maps[way, unit, 0], maps[way, unit, 1]], 0)
        factor = maps[1 - way, unit, 0]
        moved = dot(first, factor)
        both = first.astype(f32) - moved
        return both[:dim] + factor.astype(f32), both[dim:] + maps[1 - way, unit, 1].astype(f32)

    for n in range(half):
        factor, offset = chip_total(passed, n)
        x_out[0, n] = offset.astype(bf16)
        x_out[1, n] = factor.astype(bf16)
    over = [remote(x_out.at[j], x_in.at[j, kept], x_send.at[j], x_recv.at[j], 2) for j in range(2)]
    for copy in over:
        copy.start()
    totals = [chip_total(taken, n) for n in range(half)]
    forward = [
        remote(x_in.at[j, kept], x_in.at[j, kept], f_send.at[j], f_recv.at[j], 1) for j in range(2)
    ]

    def turn(a):
        far, partner = fars[a], partners[a]
        for s in range(4):
            for b in range(2):
                if s == 0:
                    block = x[:, columns(seq(partner) if b else me)]
                else:
                    block = cols[0, 1, 0] if (a, s, b) == (1, 1, 0) else cols[a, s, b]
                cols_t[a, b * part : (b + 1) * part, s * rows : (s + 1) * rows] = block.T

    for copy in tokens:
        copy.wait_recv()
    turn(0)
    over[0].wait_recv()
    for n, (factor, offset) in enumerate(totals):
        entering = x_in[0, core * half + n]
        y_out[n] = (entering.astype(f32) - mm((entering, None), split(factor)) + offset).astype(bf16)
    up = [
        remote(y_out, y_in.at[kept], y_send.at[j], y_recv.at[core], 4 + j) for j in range(4)
    ]

    @pl.when(upper == taken)
    def _():
        for copy in up:
            copy.start()

    forward[0].start()
    over[1].wait_recv()
    forward[1].start()
    turn(1)
    for copy in forward:
        copy.wait_recv()
    for c in range(2):
        remote(
            y_out, y_in.at[pl.ds(c * half, half)], y_send.at[0], y_recv.at[c], 4
        ).wait_recv()
    state[...] = jnp.zeros_like(state)
    for h in range(heads):
        state[(1 - upper) * heads + h] = y_in[h].astype(f32)

    def advance(unit, factor, offset):
        before = state[unit]
        state[unit] = before - mm(split(before), (factor, None)) + offset.astype(f32)

    for h in range(heads):
        advance(taken * heads + h, x_in[1, h], x_in[0, h])
    for h in range(heads):
        unit = (1 - core) * heads + h
        advance(unit, maps[1 - core, unit, 0], maps[1 - core, unit, 1])

    def put(i, h, value):
        a, n = h // half, h % half
        mine[:, i * width + h * dim : i * width + (h + 1) * dim] = value
        blocks[a, i, :rows, n * dim : (n + 1) * dim] = value

    def spread(a, i):
        held = blocks.at[a, i] if i < 3 else tails
        slot = [pl.ds(s * rows, rows) for s in range(4)]
        return (
            remote(held.at[slot[0]], held.at[slot[2]], far_send.at[a, i], far_recv.at[a, i], fars[a]),
            remote(held.at[slot[0]], held.at[slot[1]], sib_send.at[a, i], sib_recv.at[a, i], 1),
            remote(held.at[slot[2]], held.at[slot[3]], fwd_send.at[a, i], fwd_recv.at[a, i], 1),
        )

    def unit_state(unit):
        return state[unit].astype(bf16)

    spreads = {(a, i): spread(a, i) for a in range(2) for i in range(3)}
    spreads[0, 3] = spread(0, 3)
    dz = []
    for a in range(2):
        dz += gradients(
            heads, dim, range(a * half, (a + 1) * half),
            qkv.at[0], qkv.at[1], z, g, mid, unit_state, put,
        )
        for i in range(3):
            for copy in spreads[a, i][:2]:
                copy.start()
    last = strength_lanes(heads, dz)
    mine[:, 3 * width :] = last
    tails[:rows] = last
    for copy in spreads[0, 3][:2]:
        copy.start()

    def input_part(index):
        span = pl.ds(pl.multiple_of(index * width, width), width)
        total = dot(mine[:, 3 * width :], wb[:, span])
        for i in range(3):
            total = total + dot(mine[:, i * width : (i + 1) * width], w[i, span, :], (1, 1))
        return total

    side = 1 - 2 * (group // 2)
    edge = (group == 0) | (group == groups - 1)
    rim = jnp.where(edge, 1, 0)
    targets = [
        group + side * (1 + 2 * rim),
        group + side * (3 * rim - 1),
        group + side * (2 - rim),
    ]

    def landing(n):
        return remote(
            piece.at[n], landed.at[group], z_send.at[n], z_recv.at[group], {"head": targets[n]}
        )

    to_relay = remote(piece.at[0], relay, z_send.at[0], relay_recv, {"head": group + side})
    piece[0] = input_part(targets[0]).astype(bf16)

    @pl.when(edge)
    def _():
        to_relay.start()

    @pl.when(jnp.logical_not(edge))
    def _():
        landing(0).start()

    piece[1] = input_part(targets[1]).astype(bf16)

    @pl.when(jnp.logical_not(edge))
    def _():
        landing(1).start()

    piece[2] = input_part(targets[2]).astype(bf16)

    @pl.when(edge)
    def _():
        to_relay.wait_send()
        landing(1).start()
        landing(2).start()

    own[...] = input_part(group)

    grads = (gq_ref, gk_ref, gv_ref)
    order = [(a, i) for i in range(3) for a in range(2)] + [(0, 3)]
    trades = {
        (a, i): remote(
            part_out.at[a, i], part_in.at[a, i], part_send.at[a, i], part_recv.at[a, i], partners[a]
        )
        for a in range(2)
        for i in range(3)
    }
    tail_trade = remote(tail_out, tail_in, part_send.at[0, 3], part_recv.at[0, 3], partners[0])

    def process(a, i):
        spreads[a, i][1].wait_recv()
        spreads[a, i][2].wait_recv()
        if i < 3:
            value = dot(cols_t[a], blocks[a, i])
            part_out[a, i] = value[part:].astype(bf16)
            trades[a, i].start()
            grads[i][:, a * half * dim : (a + 1) * half * dim] = value[:part]
        else:
            value = dot(cols_t[a], tails[...]).T[:8]
            total = jnp.sum(tails[...].astype(f32), 0, keepdims=True)
            total = jnp.concatenate([total] * (part // LANES), 1)
            zero = jnp.zeros((7, part), f32)
            tail_out[...] = jnp.concatenate([value[:, part:], total, zero], 0)
            tail_trade.start()
            tail_ref[...] = jnp.concatenate([value[:, :part], total, zero], 0)

    for n, key in enumerate(order):
        spreads[key][0].wait_recv()
        spreads[key][2].start()
        if n > 0:
            process(*order[n - 1])
        if n == 3:

            @pl.when(jnp.logical_not(edge))
            def _():
                to_relay.wait_recv()
                piece[2] = (piece[2].astype(f32) + relay[...].astype(f32)).astype(bf16)
                landing(2).start()

    process(*order[-1])
    for a, i in order:
        if i < 3:
            trades[a, i].wait_recv()
            span = slice(a * half * dim, (a + 1) * half * dim)
            grads[i][:, span] = grads[i][:, span] + part_in[a, i].astype(f32)
    tail_trade.wait_recv()
    tail_ref[...] = tail_ref[...] + tail_in[...]

    def arrived(sender):
        remote(
            piece.at[0], landed.at[sender], z_send.at[0], z_recv.at[sender], {"head": targets[0]}
        ).wait_recv()
        return landed[sender].astype(f32)

    @pl.when(jnp.logical_not(edge))
    def _():
        own[...] = own[...] + arrived(group - side)

    dx_ref[...] = (own[...] + arrived(group + side) + arrived(group + 2 * side)).astype(bf16)
    sibling.wait_send()

    @pl.when(upper == taken)
    def _():
        for copy in up:
            copy.wait_send()

    @pl.when(jnp.logical_not(edge))
    def _():
        landing(0).wait_send()

    for n in (1, 2):
        landing(n).wait_send()
    for copy in tokens + over + forward + [tail_trade] + list(trades.values()):
        copy.wait_send()
    for copies in spreads.values():
        for copy in copies:
            copy.wait_send()


def place_kernel(count, heads, *refs):
    sems = refs[-1]
    tail_ref, bias_ref = refs[count], refs[2 * count + 2]
    copies = [
        pltpu.make_async_copy(refs[i], refs[count + 1 + i], sems.at[i]) for i in range(count)
    ]
    for copy in copies:
        copy.start()
    refs[2 * count + 1][...] = tail_ref[:heads, :]
    bias_ref[...] = tail_ref[8:9, :heads] + tail_ref[8:9, heads : 2 * heads]
    for copy in copies:
        copy.wait()


def place(arrays, tail, heads):
    count = len(arrays)
    vmem = pl.BlockSpec(memory_space=pltpu.VMEM)
    return pl.pallas_call(
        functools.partial(place_kernel, count, heads),
        out_shape=tuple(jax.ShapeDtypeStruct(a.shape, a.dtype) for a in arrays)
        + (
            jax.ShapeDtypeStruct((heads, tail.shape[1]), tail.dtype),
            jax.ShapeDtypeStruct((1, heads), tail.dtype),
        ),
        in_specs=[vmem] * (count + 1),
        out_specs=(pl.BlockSpec(memory_space=pltpu.HBM),) * count + (vmem,) * 2,
        scratch_shapes=[pltpu.SemaphoreType.DMA((count,))],
        name="place",
    )(*arrays, tail)


def whole_layer(tokens, weights, w_beta, b_beta, d_out):
    shards, groups = lax.axis_size("seq"), lax.axis_size("head")
    rows, features = tokens.shape
    heads = w_beta.shape[1]
    width = weights[0].shape[1]
    dim = width // heads
    half = heads // 2
    part = features // shards
    f32, bf16 = jnp.float32, jnp.bfloat16
    vmem = pl.BlockSpec(memory_space=pltpu.VMEM)
    hbm = pl.BlockSpec(memory_space=pl.ANY)
    square = jax.ShapeDtypeStruct((part, width), f32)
    dma = pltpu.SemaphoreType.DMA
    outs = pl.pallas_call(
        functools.partial(layer_kernel, groups, heads, dim),
        out_shape=(
            jax.ShapeDtypeStruct((rows, features // groups), tokens.dtype),
            square,
            square,
            square,
            jax.ShapeDtypeStruct((16, part), f32),
        ),
        in_specs=[hbm] * 5 + [vmem] * 2,
        out_specs=(vmem,) * 5,
        scratch_shapes=[
            pltpu.VMEM((rows, features), bf16),
            pltpu.VMEM((3, features, width), bf16),
            pltpu.VMEM((LANES, features), bf16),
            pltpu.VMEM((rows, width), bf16),
            pltpu.VMEM((3, rows, width), f32),
            pltpu.VMEM((rows, LANES), f32),
            pltpu.VMEM((heads, rows, 4 * dim), f32),
            pltpu.VMEM((2, 2 * heads, 2, dim, dim), bf16),
            pltpu.VMEM((2, half, dim, dim), bf16),
            pltpu.VMEM((2, heads, dim, dim), bf16),
            pltpu.VMEM((half, dim, dim), bf16),
            pltpu.VMEM((heads, dim, dim), bf16),
            pltpu.VMEM((2 * heads, dim, dim), f32),
            pltpu.VMEM((2, 4, 2, rows, part), bf16),
            pltpu.VMEM((2, 2 * part, 4 * rows), bf16),
            pltpu.VMEM((rows, 3 * width + LANES), bf16),
            pltpu.VMEM((2, 3, 4 * rows, width // 2), bf16),
            pltpu.VMEM((4 * rows, LANES), bf16),
            pltpu.VMEM((2, 3, part, width // 2), bf16),
            pltpu.VMEM((2, 3, part, width // 2), bf16),
            pltpu.VMEM((16, part), f32),
            pltpu.VMEM((16, part), f32),
            pltpu.VMEM((rows, features // groups), f32),
            pltpu.VMEM((3, rows, features // groups), bf16),
            pltpu.VMEM((groups, rows, features // groups), bf16),
            pltpu.VMEM((rows, features // groups), bf16),
            dma((5,)),
            dma((11,)),
            dma((11,)),
            dma,
            dma,
            dma((2,)),
            dma((2,)),
            dma((2,)),
            dma((2,)),
            dma((4,)),
            dma((2,)),
            dma((2, 4)),
            dma((2, 4)),
            dma((2, 4)),
            dma((2, 4)),
            dma((2, 4)),
            dma((2, 4)),
            dma((2, 4)),
            dma((2, 4)),
            dma((3,)),
            dma((groups,)),
            dma,
        ],
        compiler_params=pltpu.CompilerParams(
            vmem_limit_bytes=52 * 1024 * 1024, collective_id=1, has_side_effects=True
        ),
        name="layer",
    )(tokens, *weights, d_out, w_beta.T, b_beta.reshape(1, heads))
    d_x, grad_q, grad_k, grad_v, tail, bias = place(outs[:4], outs[4], heads)
    return d_x, grad_q, grad_k, grad_v, tail.T, bias.reshape(heads)


def per_device(tokens, w_query, w_key, w_value, w_beta, b_beta, d_out):
    token_count, features = tokens.shape
    heads = w_beta.shape[1]
    width = w_query.shape[1]
    dim = width // heads
    f32 = jnp.float32
    shards, groups = lax.axis_size("seq"), lax.axis_size("head")
    weights = (w_query, w_key, w_value)
    fits = heads % 2 == 0 and 2 * heads <= 8 and width * groups == features and dim == LANES
    if shards == 8 and groups == 4 and fits and features // shards == token_count:
        return whole_layer(tokens, weights, w_beta, b_beta, d_out)
    q, k, v = (jnp.dot(tokens, w, preferred_element_type=f32) for w in weights)
    w_last = jnp.pad(w_beta, ((0, 0), (0, LANES - heads)))
    z = jnp.dot(tokens, w_last, preferred_element_type=f32) + jnp.pad(b_beta, (0, LANES - heads))
    params = pltpu.CompilerParams(vmem_limit_bytes=60 * 1024 * 1024)
    columns = lax.all_to_all(tokens, "seq", split_axis=1, concat_axis=0, tiled=True)
    maps, mid = pl.pallas_call(
        functools.partial(summary_kernel, heads, dim),
        out_shape=(
            jax.ShapeDtypeStruct((2 * heads, 2, dim, dim), jnp.bfloat16),
            jax.ShapeDtypeStruct((heads, token_count, 4 * dim), f32),
        ),
        compiler_params=params,
        name="summary",
    )(q, k, v, z, d_out)
    states = gathered_states(maps, heads)
    grads = pl.pallas_call(
        functools.partial(gradient_kernel, heads, dim),
        out_shape=jax.ShapeDtypeStruct((token_count, 3 * width + LANES), jnp.bfloat16),
        compiler_params=params,
        name="gradient",
    )(q, k, z, d_out, mid, states)
    whole = lax.all_gather(grads, "seq", axis=0, tiled=True)
    partial = jnp.dot(grads[:, 3 * width : 3 * width + heads], w_beta.T, preferred_element_type=f32)
    for i, w in enumerate(weights):
        partial = partial + jnp.dot(
            grads[:, i * width : (i + 1) * width], w.T, preferred_element_type=f32
        )
    d_x = lax.psum_scatter(
        partial.astype(jnp.bfloat16), "head", scatter_dimension=1, tiled=True
    )

    def weight_grad(block):
        return lax.dot_general(
            columns, block, (((0,), (0,)), ((), ())), preferred_element_type=f32
        )

    found = [weight_grad(whole[:, i * width : (i + 1) * width]) for i in range(3)]
    tail = whole[:, 3 * width :]
    grad_wbeta = weight_grad(tail)[:, :heads]
    sums = jnp.sum(tail.astype(f32), 0)
    return (d_x, *found, grad_wbeta, sums[:heads] + sums[heads : 2 * heads])


def solution(mesh):
    in_specs = (
        P("seq", None),
        P(None, "head"),
        P(None, "head"),
        P(None, "head"),
        P(None, "head"),
        P("head"),
        P("seq", "head"),
    )
    out_specs = (
        P("seq", "head"),
        P("seq", "head"),
        P("seq", "head"),
        P("seq", "head"),
        P("seq", "head"),
        P("head"),
    )
    return jax.shard_map(
        per_device, mesh=mesh, in_specs=in_specs, out_specs=out_specs, check_vma=False
    )
```

```python
import functools

import jax
import jax.numpy as jnp
from jax import lax
from jax.experimental import pallas as pl
from jax.experimental.pallas import tpu as pltpu
from jax.sharding import PartitionSpec as P

epsilon = 1e-06
LANES = 128
MESH = pl.DeviceIdType.MESH
highest = lax.Precision.HIGHEST


def split(a):
    high = a.astype(jnp.bfloat16)
    return high, (a - high.astype(jnp.float32)).astype(jnp.bfloat16)


def only(a):
    return a.astype(jnp.bfloat16), None


def mm(a, b, dims=(1, 0)):
    numbers = (((dims[0],), (dims[1],)), ((), ()))
    dot = functools.partial(
        lax.dot_general, dimension_numbers=numbers, preferred_element_type=jnp.float32
    )
    total = dot(a[0], b[0])
    if b[1] is not None:
        total = total + dot(a[0], b[1])
    if a[1] is not None:
        total = total + dot(a[1], b[0])
    return total


def iotas(rows, cols):
    return (
        lax.broadcasted_iota(jnp.int32, (rows, cols), 0),
        lax.broadcasted_iota(jnp.int32, (rows, cols), 1),
    )


def invert_unit_lower(systems):
    size = systems[0].shape[0]
    base = min(size, LANES)
    row, col = iotas(base, base)
    eye = jnp.where(row == col, 1.0, 0.0).astype(jnp.float32)

    def step_mask(s):
        return (row // (2 * s) == col // (2 * s)) & (row % (2 * s) >= s) & (col % (2 * s) < s)

    count = size // base
    diagonals = [
        n[i * base : (i + 1) * base, i * base : (i + 1) * base] for n in systems for i in range(count)
    ]
    inverses = [eye - jnp.where(step_mask(1), n, 0.0) for n in diagonals]
    s = 2
    while s < base:
        mask = step_mask(s)
        parts = [split(x) for x in inverses]
        inner = [mm(split(jnp.where(mask, n, 0.0)), x) for n, x in zip(diagonals, parts)]
        outer = [mm(x, split(y)) for x, y in zip(parts, inner)]
        inverses = [x - y for x, y in zip(inverses, outer)]
        s *= 2
    grouped = [inverses[i * count : (i + 1) * count] for i in range(len(systems))]
    width = base
    while width < size:
        merged = []
        for n, blocks in zip(systems, grouped):
            joined = []
            for i in range(0, len(blocks), 2):
                first, second = blocks[i], blocks[i + 1]
                low = n[(i + 1) * width : (i + 2) * width, i * width : (i + 1) * width]
                corner = mm(split(second), split(mm(split(low), split(first))))
                joined.append(
                    jnp.concatenate(
                        [
                            jnp.concatenate([first, jnp.zeros_like(first)], 1),
                            jnp.concatenate([-corner, second], 1),
                        ],
                        0,
                    )
                )
            merged.append(joined)
        grouped = merged
        width *= 2
    return [g[0] for g in grouped]


def normalise(raw):
    scale = lax.rsqrt(jnp.sum(raw * raw, -1, keepdims=True) + epsilon)
    return raw * scale, scale


def dot(a, b, dims=(1, 0)):
    return lax.dot_general(
        a, b, (((dims[0],), (dims[1],)), ((), ())), preferred_element_type=jnp.float32
    )


def summarise(heads, dim, q_ref, k_ref, v_ref, z_ref, g_ref, put_map):
    count = q_ref.shape[0]
    row, col = iotas(count, count)
    strict, inclusive = row > col, row >= col
    every = range(heads)
    cols = [slice(h * dim, (h + 1) * dim) for h in every]
    beta_all = 2.0 * jax.nn.sigmoid(z_ref[...])
    beta = [beta_all[:, h : h + 1] for h in every]
    qn = [normalise(q_ref[:, c])[0] for c in cols]
    kn = [normalise(k_ref[:, c])[0] for c in cols]
    ks = [split(x) for x in kn]
    qs = [split(x) for x in qn]
    gs = [(g_ref[:, c], None) for c in cols]
    gram = [jnp.where(strict, mm(x, x, (1, 1)), 0.0) for x in ks]
    inverse = [split(t) for t in invert_unit_lower([b * n for b, n in zip(beta, gram)])]
    gram = [split(n) for n in gram]
    scores = [split(jnp.where(inclusive, mm(a, b, (1, 1)), 0.0)) for a, b in zip(qs, ks)]
    back = [mm(p, g, (0, 0)) for p, g in zip(scores, gs)]
    forth_in = [jnp.concatenate([v_ref[:, c], k], 1) for c, k in zip(cols, kn)]
    forth = [split(mm(t, split(b * x))) for t, b, x in zip(inverse, beta, forth_in)]
    adjoint = [
        mm(t, split(jnp.concatenate([p, k], 1)), (0, 0)) for t, p, k in zip(inverse, back, kn)
    ]
    ends = [mm(f, k, (0, 0)) for f, k in zip(forth, ks)]
    tails = [mm(split(a), split(b * k), (0, 0)) for a, b, k in zip(adjoint, beta, kn)]
    direct = [mm(g, q, (0, 0)) for g, q in zip(gs, qs)]
    for h in every:
        put_map(h, ends[h][dim:], ends[h][:dim])
        put_map(heads + h, tails[h][dim:], direct[h] - tails[h][:dim])

    def put_mid(mid_ref):
        for h in every:
            mid_ref[h, :, : 2 * dim] = forth_in[h] - mm(gram[h], forth[h])
            mid_ref[h, :, 2 * dim :] = adjoint[h]

    return put_mid


def summary_kernel(heads, dim, q_ref, k_ref, v_ref, z_ref, g_ref, map_ref, mid_ref):
    def put_map(unit, factor, offset):
        map_ref[unit, 0] = factor.astype(map_ref.dtype)
        map_ref[unit, 1] = offset.astype(map_ref.dtype)

    summarise(heads, dim, q_ref, k_ref, v_ref, z_ref, g_ref, put_map)(mid_ref)


def value_gradients(heads, dim, q_ref, k_ref, z_ref, g_ref, mid_ref, state):
    every = range(heads)
    beta_all = 2.0 * jax.nn.sigmoid(z_ref[...])
    cols = [slice(h * dim, (h + 1) * dim) for h in every]
    beta = [beta_all[:, h : h + 1] for h in every]
    ds = [(state(heads + h), None) for h in every]
    ss = [(state(h), None) for h in every]
    dx = [
        mid_ref[h, :, 2 * dim : 3 * dim] + mm(split(mid_ref[h, :, 3 * dim :]), d, (1, 1))
        for h, d in zip(every, ds)
    ]
    dv = [b * x for b, x in zip(beta, dx)]
    plain = [
        mid_ref[h, :, :dim] - mm(split(mid_ref[h, :, dim : 2 * dim]), s, (1, 1))
        for h, s in zip(every, ss)
    ]
    us = [split(b * x) for b, x in zip(beta, plain)]
    dz = [
        jnp.sum(x * p, -1, keepdims=True) * b * (1.0 - 0.5 * b) for x, p, b in zip(dx, plain, beta)
    ]
    return dv, us, dz


def key_gradients(heads, dim, q_ref, k_ref, g_ref, state, dv, us, put, between):
    every = range(heads)
    count = q_ref.shape[0] // 2
    row, col = iotas(count, count)
    strict, inclusive = row > col, row >= col
    cols = [slice(h * dim, (h + 1) * dim) for h in every]
    qp = [normalise(q_ref[:, c]) for c in cols]
    kp = [normalise(k_ref[:, c]) for c in cols]
    ks = [split(x[0]) for x in kp]
    qs = [split(x[0]) for x in qp]
    gs = [(g_ref[:, c], None) for c in cols]
    ss = [(state(h), None) for h in every]
    ds = [(state(heads + h), None) for h in every]
    dvs = [split(x) for x in dv]

    def top(x):
        return tuple(None if y is None else y[:count] for y in x)

    def low(x):
        return tuple(None if y is None else y[count:] for y in x)

    def masked(mask, x):
        return jnp.concatenate([x[:, :count], jnp.where(mask, x[:, count:], 0.0)], 1)

    inner_top = [split(jnp.where(inclusive, mm(top(g), top(u), (1, 1)), 0.0)) for g, u in zip(gs, us)]
    pair_top = [jnp.where(strict, mm(top(d), top(u), (1, 1)), 0.0) for d, u in zip(dvs, us)]
    inner_low = [split(masked(inclusive, mm(low(g), u, (1, 1)))) for g, u in zip(gs, us)]
    pair_low = [masked(strict, mm(low(d), u, (1, 1))) for d, u in zip(dvs, us)]
    both_top = [
        split(jnp.concatenate([e + e.T, f[:, :count].T], 1)) for e, f in zip(pair_top, pair_low)
    ]
    both_low = [
        split(jnp.concatenate([f[:, :count], f[:, count:] + f[:, count:].T], 1)) for f in pair_low
    ]

    def through(grad, pair, rows):
        unit, scale = pair[0][rows], pair[1][rows]
        return scale * (grad - unit * jnp.sum(unit * grad, -1, keepdims=True))

    def finish(rows, dqn, dkn):
        for h in every:
            put(0, h, rows, through(dqn[h], qp[h], rows).astype(jnp.bfloat16))
            put(1, h, rows, through(dkn[h], kp[h], rows).astype(jnp.bfloat16))

    def left(x):
        return tuple(y[:, :count] for y in x)

    def right(x):
        return tuple(y[:, count:] for y in x)

    dqn = [mm(top(g), s) + mm(i, top(k)) for g, s, i, k in zip(gs, ss, inner_top, ks)]
    dkn = [
        mm(i, top(q), (0, 0)) + mm(left(j), low(q), (0, 0)) + mm(top(u), d) - mm(top(x), s) - mm(e, k)
        for i, j, q, u, d, x, s, e, k in zip(inner_top, inner_low, qs, us, ds, dvs, ss, both_top, ks)
    ]
    finish(slice(0, count), dqn, dkn)
    between()
    dqn = [mm(low(g), s) + mm(j, k) for g, s, j, k in zip(gs, ss, inner_low, ks)]
    dkn = [
        mm(right(j), low(q), (0, 0)) + mm(low(u), d) - mm(low(x), s) - mm(e, k)
        for j, q, u, d, x, s, e, k in zip(inner_low, qs, us, ds, dvs, ss, both_low, ks)
    ]
    finish(slice(count, 2 * count), dqn, dkn)


def strength_lanes(heads, dz):
    lane = lax.broadcasted_iota(jnp.int32, (dz[0].shape[0], LANES), 1)
    last = jnp.zeros((dz[0].shape[0], LANES), jnp.float32)
    for h in range(heads):
        high, low = split(dz[h])
        last = jnp.where(lane == h, high.astype(jnp.float32), last)
        last = jnp.where(lane == heads + h, low.astype(jnp.float32), last)
    return last


def gradient_kernel(heads, dim, q_ref, k_ref, z_ref, g_ref, mid_ref, state_ref, out_ref):
    width = heads * dim

    def put(i, h, rows, value):
        out_ref[rows, i * width + h * dim : i * width + (h + 1) * dim] = value

    def state(unit):
        return state_ref[unit]

    dv, us, dz = value_gradients(heads, dim, q_ref, k_ref, z_ref, g_ref, mid_ref, state)
    for h in range(heads):
        put(2, h, slice(None), dv[h].astype(jnp.bfloat16))
    key_gradients(heads, dim, q_ref, k_ref, g_ref, state, dv, us, put, lambda: None)
    out_ref[:, 3 * width :] = strength_lanes(heads, dz).astype(jnp.bfloat16)


def gathered_states(maps, heads):
    count = lax.axis_size("seq")
    place = lax.axis_index("seq")
    gathered = lax.all_gather(maps, "seq").astype(jnp.float32)

    def walk(steps, pick, rows):
        def one(lap, state):
            pair = lax.dynamic_index_in_dim(gathered, pick(lap), 0, False)[rows]
            moved = jnp.einsum("hij,hjk->hik", state, pair[:, 0], precision=highest)
            return state - moved + pair[:, 1]

        return lax.fori_loop(0, steps, one, jnp.zeros((heads,) + maps.shape[2:], jnp.float32))

    first = walk(place, lambda lap: lap, slice(0, heads))
    second = walk(count - 1 - place, lambda lap: count - 1 - lap, slice(heads, None))
    return jnp.concatenate([first, second]).astype(maps.dtype)


def layer_kernel(
    groups, heads, dim,
    x_hbm, wq_hbm, wk_hbm, wv_hbm, g_hbm, wb_hbm, b_hbm,
    dx_hbm, gq_hbm, gk_hbm, gv_hbm, tail_hbm,
    dx_ref, grads, tail_ref, x, w, wb, g, wb_ref, b_ref, qkv, z, mid, maps, x_out, x_in, y_out, y_in, state,
    cols, cols_t, mine, blocks, tails, part_out, part_in, tail_out, tail_in,
    own, piece, landed,
    load, tok_send, tok_recv, map_send, map_recv, x_send, x_recv, f_send, f_recv,
    y_send, y_recv, s_recv, far_send, far_recv, sib_send, sib_recv, fwd_send, fwd_recv,
    part_send, part_recv, z_send, z_recv, save,
):
    me = lax.axis_index("seq")
    group = lax.axis_index("head")
    core, across, upper = me % 2, (me // 2) % 2, me // 4
    rows, width = g.shape
    part = cols.shape[-1]
    half = heads // 2
    f32, bf16 = jnp.float32, jnp.bfloat16

    def seq(o):
        index = me
        for bit in (1, 2, 4):
            if o & bit:
                index = index + bit - 2 * bit * ((me // bit) % 2)
        return index

    def remote(source, target, send, recv, device):
        return pltpu.make_async_remote_copy(
            src_ref=source,
            dst_ref=target,
            send_sem=send,
            recv_sem=recv,
            device_id=device if isinstance(device, dict) else {"seq": seq(device)},
            device_id_type=MESH,
        )

    pairs = (
        (x_hbm, x), (wk_hbm, w.at[1]), (wb_hbm, wb_ref), (b_hbm, b_ref), (g_hbm, g),
        (wq_hbm, w.at[0]), (wv_hbm, w.at[2]),
    )
    loads = [pltpu.make_async_copy(s, t, load.at[i]) for i, (s, t) in enumerate(pairs)]
    for copy in loads:
        copy.start()
    barrier = pltpu.get_barrier_semaphore()
    others = [{"seq": seq(o)} for o in range(1, 8)]
    others += [{"head": lax.rem(group + r, groups)} for r in range(1, groups)]
    for peer in others:
        pl.semaphore_signal(barrier, inc=1, device_id=peer, device_id_type=MESH)
    wb[...] = jnp.zeros_like(wb)
    pl.semaphore_wait(barrier, len(others))

    fars, partners = (2, 4), (4, 2)
    slots = [(0, 1, far, far ^ 1) for far in fars]

    def columns(index):
        return pl.ds(pl.multiple_of(index * part, part), part)

    tokens = []
    for a in range(2):
        for s in range(1, 4):
            for b in range(2):
                if (a, s, b) != (1, 1, 0):
                    owner = seq(slots[a][s] ^ (partners[a] if b else 0))
                    i = len(tokens)
                    tokens.append(
                        remote(
                            x_hbm.at[:, columns(owner)], cols.at[a, s, b],
                            tok_send.at[i], tok_recv.at[i], slots[a][s],
                        )
                    )
                    tokens[i].start()

    loads[0].wait()
    loads[1].wait()
    qkv[1] = dot(x[...], w[1])
    for copy in loads[2:]:
        copy.wait()
    wb[pl.ds(0, heads), :] = wb_ref[...]
    z[...] = dot(x[...], wb[...], (1, 1))
    z[:, :heads] = z[:, :heads] + b_ref[...]
    qkv[0] = dot(x[...], w[0])
    qkv[2] = dot(x[...], w[2])

    def put_map(unit, factor, offset):
        maps[core, unit, 0] = factor.astype(bf16)
        maps[core, unit, 1] = offset.astype(bf16)

    put_mid = summarise(heads, dim, qkv.at[0], qkv.at[1], qkv.at[2], z, g, put_map)
    passed, taken = across, 1 - across
    kept, other = pl.ds(core * half, half), pl.ds((1 - core) * half, half)
    urgent = [
        (way * heads + n * half, j)
        for j, (way, n) in enumerate(
            [(passed, 1 - core), (taken, 1 - core), (passed, core), (taken, core)]
        )
    ]
    sibling = [
        remote(
            maps.at[core, pl.ds(unit, half)], maps.at[core, pl.ds(unit, half)],
            map_send.at[j], map_recv.at[j], 1,
        )
        for unit, j in urgent
    ]
    arriving = [
        remote(
            maps.at[1 - core, pl.ds(way * heads + n * half, half)],
            maps.at[1 - core, pl.ds(way * heads + n * half, half)],
            map_send.at[j], map_recv.at[j], 1,
        )
        for j, (way, n) in enumerate([(passed, core), (taken, core), (passed, 1 - core), (taken, 1 - core)])
    ]
    for copy in sibling:
        copy.start()
    put_mid(mid)
    arriving[0].wait_recv()

    def chip_total(way, n):
        unit = way * heads + core * half + n
        first = jnp.concatenate([maps[way, unit, 0], maps[way, unit, 1]], 0)
        factor = maps[1 - way, unit, 0]
        moved = dot(first, factor)
        both = first.astype(f32) - moved
        return both[:dim] + factor.astype(f32), both[dim:] + maps[1 - way, unit, 1].astype(f32)

    for n in range(half):
        factor, offset = chip_total(passed, n)
        x_out[0, n] = offset.astype(bf16)
        x_out[1, n] = factor.astype(bf16)
    over = [remote(x_out.at[j], x_in.at[j, kept], x_send.at[j], x_recv.at[j], 2) for j in range(2)]
    for copy in over:
        copy.start()
    arriving[1].wait_recv()
    totals = [chip_total(taken, n) for n in range(half)]
    forward = [
        remote(x_in.at[j, kept], x_in.at[j, kept], f_send.at[j], f_recv.at[j], 1) for j in range(2)
    ]

    def own_columns(a, b):
        return x[:, columns(seq(partners[a]) if b else me)]

    def turn(a):
        for s in range(4):
            for b in range(2):
                if s == 0:
                    block = own_columns(a, b)
                else:
                    block = cols[0, 1, 0] if (a, s, b) == (1, 1, 0) else cols[a, s, b]
                cols_t[a, b * part : (b + 1) * part, s * rows : (s + 1) * rows] = block.T

    for copy in tokens:
        copy.wait_recv()
    turn(0)
    over[0].wait_recv()
    for n, (factor, offset) in enumerate(totals):
        entering = x_in[0, core * half + n]
        y_out[n] = (entering.astype(f32) - mm((entering, None), split(factor)) + offset).astype(bf16)
    up = [remote(y_out, y_in.at[kept], y_send.at[j], y_recv, 4 + 2 * j) for j in range(2)]
    share = remote(y_in.at[kept], y_in.at[kept], y_send.at[2], s_recv, 1)

    @pl.when(upper == taken)
    def _():
        for copy in up:
            copy.start()

    forward[0].start()
    over[1].wait_recv()
    forward[1].start()
    turn(1)
    for copy in forward + arriving[2:]:
        copy.wait_recv()
    state[...] = jnp.zeros_like(state)
    for h in range(heads):
        state[taken * heads + h] = x_in[0, h].astype(f32)
    bridge = []
    lead, inside = 1 - upper, 1 - core
    for h in range(heads):
        unit = inside * heads + h
        factor = maps[inside, unit, 0]
        before = state[unit]
        state[unit] = before - mm(split(before), (factor, None)) + maps[inside, unit, 1].astype(f32)
        first = jnp.where(taken == lead, x_in[1, h].astype(f32), 0.0).astype(bf16)
        second = jnp.where(inside == lead, factor.astype(f32), 0.0).astype(bf16)
        bridge.append(split(first.astype(f32) + second.astype(f32) - dot(first, second)))
    up[0].wait_recv()
    share.start()
    share.wait_recv()
    for h in range(heads):
        unit = lead * heads + h
        state[unit] = state[unit] + (y_in[h].astype(f32) - mm((y_in[h], None), bridge[h]))

    def put(i, h, span, value):
        a, n = h // half, h % half
        mine[span, i * width + h * dim : i * width + (h + 1) * dim] = value
        blocks[a, i, span, n * dim : (n + 1) * dim] = value

    def spread(a, i):
        if i < 3:
            slot = [blocks.at[a, i, pl.ds(s * rows, rows)] for s in range(4)]
        else:
            slot = [tails.at[s] for s in range(4)]
        return (
            remote(slot[0], slot[2], far_send.at[a, i], far_recv.at[a, i], fars[a]),
            remote(slot[0], slot[1], sib_send.at[a, i], sib_recv.at[a, i], 1),
            remote(slot[2], slot[3], fwd_send.at[a, i], fwd_recv.at[a, i], 1),
        )

    def unit_state(unit):
        return state[unit].astype(bf16)

    spreads = {(a, i): spread(a, i) for a in range(2) for i in range(3)}
    spreads[0, 3] = spread(0, 3)

    def send(key):
        for copy in spreads[key][:2]:
            copy.start()

    dv, us, dz = value_gradients(heads, dim, qkv.at[0], qkv.at[1], z, g, mid, unit_state)
    for h in range(heads):
        put(2, h, slice(0, rows), dv[h].astype(bf16))
    send((0, 2))
    send((1, 2))
    last = strength_lanes(heads, dz)
    mine[:, 3 * width :] = last.astype(bf16)
    tails[0] = last.T[:16].astype(bf16)
    send((0, 3))
    halves = [slice(0, rows // 2), slice(rows // 2, rows)]

    def input_part(index, rows):
        span = pl.ds(pl.multiple_of(index * width, width), width)
        total = dot(mine[rows, 3 * width :], wb[:, span])
        for i in range(3):
            total = total + dot(mine[rows, i * width : (i + 1) * width], w[i, span, :], (1, 1))
        return total

    side = 1 - 2 * (group // 2)
    edge = (group == 0) | (group == groups - 1)
    rim = jnp.where(edge, 1, 0)
    targets = [
        group + side * (1 + 2 * rim),
        group + side * (3 * rim - 1),
        group + side * (2 - rim),
    ]

    def landing(n, h):
        slot = jnp.where(edge, groups, group) if n == 0 else group
        device = group + side if n == 0 else targets[n]
        return remote(
            piece.at[n, halves[h]], landed.at[slot, halves[h]],
            z_send.at[n, h], z_recv.at[slot, h], {"head": device},
        )

    def first_piece(h):
        piece[0, halves[h]] = input_part(targets[0], halves[h]).astype(bf16)
        landing(0, h).start()

    key_gradients(
        heads, dim, qkv.at[0], qkv.at[1], g, unit_state, dv, us, put, lambda: first_piece(0)
    )
    for key in ((0, 0), (1, 0), (0, 1), (1, 1)):
        send(key)
    first_piece(1)
    piece[1] = input_part(targets[1], slice(0, rows)).astype(bf16)
    for h in range(2):
        landing(1, h).start()
    piece[2] = input_part(targets[2], slice(0, rows)).astype(bf16)

    @pl.when(edge)
    def _():
        for h in range(2):
            landing(2, h).start()

    own[...] = input_part(group, slice(0, rows))

    def arrived(slot, h):
        remote(
            piece.at[0, halves[h]], landed.at[slot, halves[h]],
            z_send.at[0, h], z_recv.at[slot, h], {"head": targets[0]},
        ).wait_recv()
        return landed[slot, halves[h]].astype(f32)

    def pass_on(h):
        @pl.when(jnp.logical_not(edge))
        def _():
            piece[2, halves[h]] = (piece[2, halves[h]].astype(f32) + arrived(groups, h)).astype(bf16)
            landing(2, h).start()

    order = [(0, 2), (1, 2), (0, 3), (0, 0), (1, 0), (0, 1), (1, 1)]
    trades = {
        (a, i): remote(
            part_out.at[a, i], part_in.at[a, i], part_send.at[a, i], part_recv.at[a, i], partners[a]
        )
        for a in range(2)
        for i in range(3)
    }
    tail_trade = remote(tail_out, tail_in, part_send.at[0, 3], part_recv.at[0, 3], partners[0])

    def process(a, i):
        spreads[a, i][1].wait_recv()
        spreads[a, i][2].wait_recv()
        if i < 3:
            value = dot(cols_t[a], blocks[a, i])
            part_out[a, i] = value[part:].astype(bf16)
            trades[a, i].start()
            grads[i, :, a * half * dim : (a + 1) * half * dim] = value[:part]
        else:
            sums = [dot(tails[0], own_columns(0, b)) for b in range(2)]
            for s in range(1, 4):
                sums = [t + dot(tails[s], cols[0, s, b]) for b, t in enumerate(sums)]
            held = jnp.sum(tails[...].astype(f32), 0)
            held = jnp.sum(held, -1, keepdims=True)
            row, col = iotas(16, part)
            held = jnp.sum(jnp.where(row == col, held, 0.0), 0, keepdims=True)
            row = lax.broadcasted_iota(jnp.int32, (16, part), 0)
            tail_out[...] = jnp.where(row == 8, held, sums[1])
            tail_trade.start()
            tail_ref[...] = jnp.where(row == 8, held, sums[0])

    for n, key in enumerate(order):
        spreads[key][0].wait_recv()
        spreads[key][2].start()
        if n > 0:
            process(*order[n - 1])
        if n == 2:
            pass_on(0)
        if n == 4:
            pass_on(1)

    process(*order[-1])
    saves = []

    def keep(source, target):
        copy = pltpu.make_async_copy(source, target, save.at[len(saves)])
        copy.start()
        saves.append(copy)

    targets_hbm = (gq_hbm, gk_hbm, gv_hbm)
    for a, i in order:
        if i < 3:
            trades[a, i].wait_recv()
            span = slice(a * half * dim, (a + 1) * half * dim)
            grads[i, :, span] = grads[i, :, span] + part_in[a, i].astype(f32)
            keep(grads.at[i, :, span], targets_hbm[i].at[:, span])
        else:
            tail_trade.wait_recv()
            tail_ref[...] = tail_ref[...] + tail_in[...]
            keep(tail_ref, tail_hbm)

    for h in range(2):

        @pl.when(jnp.logical_not(edge))
        def _():
            own[halves[h]] = own[halves[h]] + arrived(group - side, h)

        total = own[halves[h]] + arrived(group + side, h) + arrived(group + 2 * side, h)
        dx_ref[halves[h]] = total.astype(bf16)
        keep(dx_ref.at[halves[h]], dx_hbm.at[halves[h]])

    share.wait_send()

    @pl.when(upper == taken)
    def _():
        for copy in up:
            copy.wait_send()

    for n in range(3):
        for h in range(2):
            landing(n, h).wait_send()
    for copy in sibling + tokens + over + forward + [tail_trade] + list(trades.values()):
        copy.wait_send()
    for copies in spreads.values():
        for copy in copies:
            copy.wait_send()
    for copy in saves:
        copy.wait()


def place_kernel(count, heads, *refs):
    sources, outs = refs[: count + 1], refs[count + 1 : 2 * count + 3]
    held, sems = refs[2 * count + 3 : -1], refs[-1]
    fetch = [
        pltpu.make_async_copy(sources[i], held[i], sems.at[0, i]) for i in range(count + 1)
    ]
    store = [pltpu.make_async_copy(held[i], outs[i], sems.at[1, i]) for i in range(count)]
    for copy in fetch:
        copy.start()
    for i in range(count):
        fetch[i].wait()
        store[i].start()
    fetch[count].wait()
    outs[count][...] = held[count][:heads, :]
    outs[count + 1][...] = held[count][8:9, :heads] + held[count][8:9, heads : 2 * heads]
    for copy in store:
        copy.wait()


def place(arrays, tail, heads):
    count = len(arrays)
    vmem = pl.BlockSpec(memory_space=pltpu.VMEM)
    hbm = pl.BlockSpec(memory_space=pltpu.HBM)
    return pl.pallas_call(
        functools.partial(place_kernel, count, heads),
        out_shape=tuple(jax.ShapeDtypeStruct(a.shape, a.dtype) for a in arrays)
        + (
            jax.ShapeDtypeStruct((heads, tail.shape[1]), tail.dtype),
            jax.ShapeDtypeStruct((1, heads), tail.dtype),
        ),
        in_specs=[hbm] * (count + 1),
        out_specs=(hbm,) * count + (vmem,) * 2,
        scratch_shapes=[pltpu.VMEM(a.shape, a.dtype) for a in (*arrays, tail)]
        + [pltpu.SemaphoreType.DMA((2, count + 1))],
        compiler_params=pltpu.CompilerParams(vmem_limit_bytes=60 * 1024 * 1024),
        name="place",
    )(*arrays, tail)


def whole_layer(tokens, weights, w_beta, b_beta, d_out):
    shards, groups = lax.axis_size("seq"), lax.axis_size("head")
    rows, features = tokens.shape
    heads = w_beta.shape[1]
    width = weights[0].shape[1]
    dim = width // heads
    half = heads // 2
    part = features // shards
    f32, bf16 = jnp.float32, jnp.bfloat16
    hbm = pl.BlockSpec(memory_space=pltpu.HBM)
    square = jax.ShapeDtypeStruct((part, width), f32)
    dma = pltpu.SemaphoreType.DMA
    outs = pl.pallas_call(
        functools.partial(layer_kernel, groups, heads, dim),
        out_shape=(
            jax.ShapeDtypeStruct((rows, features // groups), tokens.dtype),
            square,
            square,
            square,
            jax.ShapeDtypeStruct((16, part), f32),
        ),
        in_specs=[hbm] * 7,
        out_specs=(hbm,) * 5,
        scratch_shapes=[
            pltpu.VMEM((rows, features // groups), bf16),
            pltpu.VMEM((3, part, width), f32),
            pltpu.VMEM((16, part), f32),
            pltpu.VMEM((rows, features), bf16),
            pltpu.VMEM((3, features, width), bf16),
            pltpu.VMEM((LANES, features), bf16),
            pltpu.VMEM((rows, width), bf16),
            pltpu.VMEM((heads, features), bf16),
            pltpu.VMEM((1, heads), f32),
            pltpu.VMEM((3, rows, width), f32),
            pltpu.VMEM((rows, LANES), f32),
            pltpu.VMEM((heads, rows, 4 * dim), f32),
            pltpu.VMEM((2, 2 * heads, 2, dim, dim), bf16),
            pltpu.VMEM((2, half, dim, dim), bf16),
            pltpu.VMEM((2, heads, dim, dim), bf16),
            pltpu.VMEM((half, dim, dim), bf16),
            pltpu.VMEM((heads, dim, dim), bf16),
            pltpu.VMEM((2 * heads, dim, dim), f32),
            pltpu.VMEM((2, 4, 2, rows, part), bf16),
            pltpu.VMEM((2, 2 * part, 4 * rows), bf16),
            pltpu.VMEM((rows, 3 * width + LANES), bf16),
            pltpu.VMEM((2, 3, 4 * rows, width // 2), bf16),
            pltpu.VMEM((4, 16, rows), bf16),
            pltpu.VMEM((2, 3, part, width // 2), bf16),
            pltpu.VMEM((2, 3, part, width // 2), bf16),
            pltpu.VMEM((16, part), f32),
            pltpu.VMEM((16, part), f32),
            pltpu.VMEM((rows, features // groups), f32),
            pltpu.VMEM((3, rows, features // groups), bf16),
            pltpu.VMEM((groups + 1, rows, features // groups), bf16),
            dma((7,)),
            dma((11,)),
            dma((11,)),
            dma((4,)),
            dma((4,)),
            dma((2,)),
            dma((2,)),
            dma((2,)),
            dma((2,)),
            dma((3,)),
            dma,
            dma,
            dma((2, 4)),
            dma((2, 4)),
            dma((2, 4)),
            dma((2, 4)),
            dma((2, 4)),
            dma((2, 4)),
            dma((2, 4)),
            dma((2, 4)),
            dma((3, 2)),
            dma((groups + 1, 2)),
            dma((9,)),
        ],
        compiler_params=pltpu.CompilerParams(
            vmem_limit_bytes=60 * 1024 * 1024, collective_id=1, has_side_effects=True
        ),
        name="layer",
    )(tokens, *weights, d_out, w_beta.T, b_beta.reshape(1, heads))
    d_x, grad_q, grad_k, grad_v, tail, bias = place(outs[:4], outs[4], heads)
    return d_x, grad_q, grad_k, grad_v, tail.T, bias.reshape(heads)


def per_device(tokens, w_query, w_key, w_value, w_beta, b_beta, d_out):
    token_count, features = tokens.shape
    heads = w_beta.shape[1]
    width = w_query.shape[1]
    dim = width // heads
    f32 = jnp.float32
    shards, groups = lax.axis_size("seq"), lax.axis_size("head")
    weights = (w_query, w_key, w_value)
    fits = heads % 2 == 0 and 2 * heads <= 8 and width * groups == features and dim == LANES
    if shards == 8 and groups == 4 and fits and features // shards == token_count:
        return whole_layer(tokens, weights, w_beta, b_beta, d_out)
    q, k, v = (jnp.dot(tokens, w, preferred_element_type=f32) for w in weights)
    w_last = jnp.pad(w_beta, ((0, 0), (0, LANES - heads)))
    z = jnp.dot(tokens, w_last, preferred_element_type=f32) + jnp.pad(b_beta, (0, LANES - heads))
    params = pltpu.CompilerParams(vmem_limit_bytes=60 * 1024 * 1024)
    columns = lax.all_to_all(tokens, "seq", split_axis=1, concat_axis=0, tiled=True)
    maps, mid = pl.pallas_call(
        functools.partial(summary_kernel, heads, dim),
        out_shape=(
            jax.ShapeDtypeStruct((2 * heads, 2, dim, dim), jnp.bfloat16),
            jax.ShapeDtypeStruct((heads, token_count, 4 * dim), f32),
        ),
        compiler_params=params,
        name="summary",
    )(q, k, v, z, d_out)
    states = gathered_states(maps, heads)
    grads = pl.pallas_call(
        functools.partial(gradient_kernel, heads, dim),
        out_shape=jax.ShapeDtypeStruct((token_count, 3 * width + LANES), jnp.bfloat16),
        compiler_params=params,
        name="gradient",
    )(q, k, z, d_out, mid, states)
    whole = lax.all_gather(grads, "seq", axis=0, tiled=True)
    partial = jnp.dot(grads[:, 3 * width : 3 * width + heads], w_beta.T, preferred_element_type=f32)
    for i, w in enumerate(weights):
        partial = partial + jnp.dot(
            grads[:, i * width : (i + 1) * width], w.T, preferred_element_type=f32
        )
    d_x = lax.psum_scatter(
        partial.astype(jnp.bfloat16), "head", scatter_dimension=1, tiled=True
    )

    def weight_grad(block):
        return lax.dot_general(
            columns, block, (((0,), (0,)), ((), ())), preferred_element_type=f32
        )

    found = [weight_grad(whole[:, i * width : (i + 1) * width]) for i in range(3)]
    tail = whole[:, 3 * width :]
    grad_wbeta = weight_grad(tail)[:, :heads]
    sums = jnp.sum(tail.astype(f32), 0)
    return (d_x, *found, grad_wbeta, sums[:heads] + sums[heads : 2 * heads])


def solution(mesh):
    in_specs = (
        P("seq", None),
        P(None, "head"),
        P(None, "head"),
        P(None, "head"),
        P(None, "head"),
        P("head"),
        P("seq", "head"),
    )
    out_specs = (
        P("seq", "head"),
        P("seq", "head"),
        P("seq", "head"),
        P("seq", "head"),
        P("seq", "head"),
        P("head"),
    )
    return jax.shard_map(
        per_device, mesh=mesh, in_specs=in_specs, out_specs=out_specs, check_vma=False
    )
```

```python
import functools

import jax
import jax.numpy as jnp
from jax import lax
from jax.experimental import pallas as pl
from jax.experimental.pallas import tpu as pltpu
from jax.sharding import PartitionSpec as P

epsilon = 1e-06
LANES = 128
MESH = pl.DeviceIdType.MESH
highest = lax.Precision.HIGHEST


def split(a):
    high = a.astype(jnp.bfloat16)
    return high, (a - high.astype(jnp.float32)).astype(jnp.bfloat16)


def only(a):
    return a.astype(jnp.bfloat16), None


def mm(a, b, dims=(1, 0)):
    numbers = (((dims[0],), (dims[1],)), ((), ()))
    dot = functools.partial(
        lax.dot_general, dimension_numbers=numbers, preferred_element_type=jnp.float32
    )
    total = dot(a[0], b[0])
    if b[1] is not None:
        total = total + dot(a[0], b[1])
    if a[1] is not None:
        total = total + dot(a[1], b[0])
    return total


def square_mm(a, b):
    size = a[0].shape[0]
    left = jnp.concatenate(a, 1)
    right = jnp.concatenate(
        [jnp.concatenate(b, 1), jnp.concatenate([b[0], jnp.zeros_like(b[0])], 1)], 0
    )
    both = lax.dot_general(left, right, (((1,), (0,)), ((), ())), preferred_element_type=jnp.float32)
    return both[:, :size] + both[:, size:]


def tight_mm(a, b, dims=(1, 0)):
    inner, outer = dims[1], 1 - dims[1]
    size = b[0].shape[outer]
    left = a[0] if a[1] is None else jnp.concatenate(a, dims[0])
    right = b[0] if b[1] is None else jnp.concatenate(b, outer)
    if a[1] is not None:
        again = b[0]
        if b[1] is not None:
            again = jnp.concatenate([b[0], jnp.zeros_like(b[0])], outer)
        right = jnp.concatenate([right, again], inner)
    both = lax.dot_general(
        left, right, (((dims[0],), (dims[1],)), ((), ())), preferred_element_type=jnp.float32
    )
    return both if b[1] is None else both[:, :size] + both[:, size:]


def iotas(rows, cols):
    return (
        lax.broadcasted_iota(jnp.int32, (rows, cols), 0),
        lax.broadcasted_iota(jnp.int32, (rows, cols), 1),
    )


def invert_unit_lower(systems, fillers=()):
    fillers = list(fillers)
    size = systems[0].shape[0]
    base = min(size, LANES)
    row, col = iotas(base, base)
    eye = jnp.where(row == col, 1.0, 0.0).astype(jnp.float32)

    def step_mask(s):
        return (row // (2 * s) == col // (2 * s)) & (row % (2 * s) >= s) & (col % (2 * s) < s)

    count = size // base
    diagonals = [
        n[i * base : (i + 1) * base, i * base : (i + 1) * base] for n in systems for i in range(count)
    ]
    inverses = [eye - jnp.where(step_mask(1), n, 0.0) for n in diagonals]
    pairs = [split(n) for n in diagonals]
    s = 2
    while s < base:
        mask = jnp.where(step_mask(s), 1.0, 0.0).astype(jnp.bfloat16)
        parts = [split(x) for x in inverses]
        inner = [square_mm((mask * n[0], mask * n[1]), x) for n, x in zip(pairs, parts)]
        if fillers:
            fillers.pop(0)()
        outer = [square_mm(x, split(y)) for x, y in zip(parts, inner)]
        inverses = [x - y for x, y in zip(inverses, outer)]
        s *= 2
    for filler in fillers:
        filler()
    grouped = [inverses[i * count : (i + 1) * count] for i in range(len(systems))]
    width = base
    while width < size:
        merged = []
        for n, blocks in zip(systems, grouped):
            joined = []
            for i in range(0, len(blocks), 2):
                first, second = blocks[i], blocks[i + 1]
                low = n[(i + 1) * width : (i + 2) * width, i * width : (i + 1) * width]
                corner = square_mm(split(second), split(square_mm(split(low), split(first))))
                joined.append(
                    jnp.concatenate(
                        [
                            jnp.concatenate([first, jnp.zeros_like(first)], 1),
                            jnp.concatenate([-corner, second], 1),
                        ],
                        0,
                    )
                )
            merged.append(joined)
        grouped = merged
        width *= 2
    return [g[0] for g in grouped]


def normalise(raw):
    scale = lax.rsqrt(jnp.sum(raw * raw, -1, keepdims=True) + epsilon)
    return raw * scale, scale


def dot(a, b, dims=(1, 0)):
    return lax.dot_general(
        a, b, (((dims[0],), (dims[1],)), ((), ())), preferred_element_type=jnp.float32
    )


def summarise(heads, dim, q_ref, k_ref, v_ref, z_ref, g_ref, put_map, fillers=(), put_unit=None):
    count = q_ref.shape[0]
    row, col = iotas(count, count)
    strict, inclusive = row > col, row >= col
    every = range(heads)
    cols = [slice(h * dim, (h + 1) * dim) for h in every]
    beta_all = 2.0 * jax.nn.sigmoid(z_ref[:, :heads])
    beta = [beta_all[:, h : h + 1] for h in every]
    kp = [normalise(k_ref[:, c]) for c in cols]
    kn = [x[0] for x in kp]
    ks = [split(x) for x in kn]
    gs = [(g_ref[:, c], None) for c in cols]
    gram = [jnp.where(strict, mm(x, x, (1, 1)), 0.0) for x in ks]
    systems = [b * n for b, n in zip(beta, gram)]
    inverse = [split(t) for t in invert_unit_lower(systems, fillers)]
    qp = [normalise(q_ref[:, c]) for c in cols]
    qs = [split(x[0]) for x in qp]
    if put_unit is not None:
        put_unit(qp, kp)
    gram = [split(n) for n in gram]
    scores = [split(jnp.where(inclusive, mm(a, b, (1, 1)), 0.0)) for a, b in zip(qs, ks)]
    back = [mm(p, g, (0, 0)) for p, g in zip(scores, gs)]
    forth_in = [jnp.concatenate([v_ref[:, c], k], 1) for c, k in zip(cols, kn)]
    forth = [split(mm(t, split(b * x))) for t, b, x in zip(inverse, beta, forth_in)]
    adjoint = [
        mm(t, split(jnp.concatenate([p, k], 1)), (0, 0)) for t, p, k in zip(inverse, back, kn)
    ]
    ends = [mm(f, k, (0, 0)) for f, k in zip(forth, ks)]
    tails = [mm(split(a), split(b * k), (0, 0)) for a, b, k in zip(adjoint, beta, kn)]
    direct = [mm(g, q, (0, 0)) for g, q in zip(gs, qs)]
    for h in every:
        put_map(h, ends[h][dim:], ends[h][:dim])
        put_map(heads + h, tails[h][dim:], direct[h] - tails[h][:dim])

    def put_mid(mid_ref):
        for h in every:
            mid_ref[h, :, : 2 * dim] = forth_in[h] - mm(gram[h], forth[h])
            mid_ref[h, :, 2 * dim :] = adjoint[h]

    return put_mid


def summary_kernel(heads, dim, q_ref, k_ref, v_ref, z_ref, g_ref, map_ref, mid_ref):
    def put_map(unit, factor, offset):
        map_ref[unit, 0] = factor.astype(map_ref.dtype)
        map_ref[unit, 1] = offset.astype(map_ref.dtype)

    summarise(heads, dim, q_ref, k_ref, v_ref, z_ref, g_ref, put_map)(mid_ref)


def gradients(heads, dim, qp, kp, z_ref, g_ref, mid_ref, state, put, strength, valued, between):
    every = range(heads)
    count = z_ref.shape[0] // 2
    halves = (slice(0, count), slice(count, 2 * count))
    row, col = iotas(count, count)
    strict, inclusive = row > col, row >= col
    beta_all = 2.0 * jax.nn.sigmoid(z_ref[:, :heads])
    beta = [beta_all[:, h : h + 1] for h in every]
    ss = [(state(h), None) for h in every]
    ds = [(state(heads + h), None) for h in every]
    dx = [
        mid_ref[h, :, 2 * dim : 3 * dim] + mm(split(mid_ref[h, :, 3 * dim :]), d, (1, 1))
        for h, d in zip(every, ds)
    ]
    dv = [b * x for b, x in zip(beta, dx)]
    for h in every:
        put(2, h, slice(0, 2 * count), dv[h].astype(jnp.bfloat16))
    valued()

    def pick(x, rows):
        return tuple(None if y is None else y[rows] for y in x)

    def part(rows):
        ks = [split(x[0][rows]) for x in kp]
        qs = [split(x[0][rows]) for x in qp]
        gs = [(g_ref[rows, h * dim : (h + 1) * dim], None) for h in every]
        plain = [
            mid_ref[h, rows, :dim] - mm(split(mid_ref[h, rows, dim : 2 * dim]), s, (1, 1))
            for h, s in zip(every, ss)
        ]
        us = [split(b[rows] * x) for b, x in zip(beta, plain)]
        dz = [
            jnp.sum(x[rows] * p, -1, keepdims=True) * b[rows] * (1.0 - 0.5 * b[rows])
            for x, p, b in zip(dx, plain, beta)
        ]
        return ks, qs, gs, us, dz

    def through(grad, pair, rows):
        unit, scale = pair[0][rows], pair[1][rows]
        return scale * (grad - unit * jnp.sum(unit * grad, -1, keepdims=True))

    def finish(rows, dqn, dkn):
        for h in every:
            put(0, h, rows, through(dqn[h], qp[h], rows).astype(jnp.bfloat16))
            put(1, h, rows, through(dkn[h], kp[h], rows).astype(jnp.bfloat16))

    def below(a, b, mask):
        found = [tight_mm(x, y, (1, 1)) for x, y in zip(a, b)]
        return found if mask is None else [jnp.where(mask, x, 0.0) for x in found]

    dvs = [[split(x[rows]) for x in dv] for rows in halves]
    k0, q0, g0, u0, dz = part(halves[0])
    strength(halves[0], dz)
    k1 = [split(x[0][halves[1]]) for x in kp]
    q1 = [split(x[0][halves[1]]) for x in qp]
    g1 = [(g_ref[halves[1], h * dim : (h + 1) * dim], None) for h in every]
    inner0 = [split(x) for x in below(g0, u0, inclusive)]
    pair0 = below(dvs[0], u0, strict)
    inner1 = [split(x) for x in below(g1, u0, None)]
    pair1 = below(dvs[1], u0, None)
    dqn = [tight_mm(g, s) + tight_mm(i, k) for g, s, i, k in zip(g0, ss, inner0, k0)]
    dkn = [
        tight_mm(i, q, (0, 0)) + tight_mm(j, r, (0, 0)) + tight_mm(u, d) - tight_mm(x, s)
        - tight_mm(split(e + e.T), k) - tight_mm(split(f.T), l)
        for i, q, j, r, u, d, x, s, e, k, f, l in zip(
            inner0, q0, inner1, q1, u0, ds, dvs[0], ss, pair0, k0, pair1, k1
        )
    ]
    finish(halves[0], dqn, dkn)
    between()
    k1, q1, g1, u1, dz = part(halves[1])
    strength(halves[1], dz)
    inner2 = [split(x) for x in below(g1, u1, inclusive)]
    pair2 = below(dvs[1], u1, strict)
    dqn = [
        tight_mm(g, s) + tight_mm(j, k) + tight_mm(i, l)
        for g, s, j, k, i, l in zip(g1, ss, inner1, k0, inner2, k1)
    ]
    dkn = [
        tight_mm(i, q, (0, 0)) + tight_mm(u, d) - tight_mm(x, s) - tight_mm(split(f), k) - tight_mm(split(e + e.T), l)
        for i, q, u, d, x, s, f, k, e, l in zip(
            inner2, q1, u1, ds, dvs[1], ss, pair1, k0, pair2, k1
        )
    ]
    finish(halves[1], dqn, dkn)


def strength_lanes(heads, dz):
    lane = lax.broadcasted_iota(jnp.int32, (dz[0].shape[0], LANES), 1)
    last = jnp.zeros((dz[0].shape[0], LANES), jnp.float32)
    for h in range(heads):
        high, low = split(dz[h])
        last = jnp.where(lane == h, high.astype(jnp.float32), last)
        last = jnp.where(lane == heads + h, low.astype(jnp.float32), last)
    return last


def gradient_kernel(heads, dim, q_ref, k_ref, z_ref, g_ref, mid_ref, state_ref, out_ref):
    width = heads * dim

    def put(i, h, rows, value):
        out_ref[rows, i * width + h * dim : i * width + (h + 1) * dim] = value

    def state(unit):
        return state_ref[unit]

    def strength(rows, dz):
        out_ref[rows, 3 * width :] = strength_lanes(heads, dz).astype(jnp.bfloat16)

    cols = [slice(h * dim, (h + 1) * dim) for h in range(heads)]
    qp = [normalise(q_ref[:, c]) for c in cols]
    kp = [normalise(k_ref[:, c]) for c in cols]
    gradients(
        heads, dim, qp, kp, z_ref, g_ref, mid_ref, state, put, strength,
        lambda: None, lambda: None,
    )


def gathered_states(maps, heads):
    count = lax.axis_size("seq")
    place = lax.axis_index("seq")
    gathered = lax.all_gather(maps, "seq").astype(jnp.float32)

    def walk(steps, pick, rows):
        def one(lap, state):
            pair = lax.dynamic_index_in_dim(gathered, pick(lap), 0, False)[rows]
            moved = jnp.einsum("hij,hjk->hik", state, pair[:, 0], precision=highest)
            return state - moved + pair[:, 1]

        return lax.fori_loop(0, steps, one, jnp.zeros((heads,) + maps.shape[2:], jnp.float32))

    first = walk(place, lambda lap: lap, slice(0, heads))
    second = walk(count - 1 - place, lambda lap: count - 1 - lap, slice(heads, None))
    return jnp.concatenate([first, second]).astype(maps.dtype)


def layer_kernel(
    groups, heads, dim,
    x_hbm, wq_hbm, wk_hbm, wv_hbm, g_hbm, wb_hbm, b_hbm,
    dx_hbm, gq_hbm, gk_hbm, gv_hbm, tail_hbm,
    dx_ref, grads, tail_ref, x, w, wb, g, wb_ref, b_ref, qkv, units, scales, z, mid, maps, x_out, x_in, y_out, y_in, state,
    cols, cols_t, mine, blocks, tails, part_out, part_in, tail_out, tail_in,
    own, piece, landed,
    load, tok_send, tok_recv, map_send, map_recv, x_send, x_recv, f_send, f_recv,
    y_send, y_recv, s_recv, far_send, far_recv, sib_send, sib_recv, fwd_send, fwd_recv,
    part_send, part_recv, z_send, z_recv, save,
):
    me = lax.axis_index("seq")
    group = lax.axis_index("head")
    core, across, upper = me % 2, (me // 2) % 2, me // 4
    rows, width = g.shape
    part = cols.shape[-1]
    half = heads // 2
    f32, bf16 = jnp.float32, jnp.bfloat16

    def seq(o):
        index = me
        for bit in (1, 2, 4):
            if o & bit:
                index = index + bit - 2 * bit * ((me // bit) % 2)
        return index

    def remote(source, target, send, recv, device):
        return pltpu.make_async_remote_copy(
            src_ref=source,
            dst_ref=target,
            send_sem=send,
            recv_sem=recv,
            device_id=device if isinstance(device, dict) else {"seq": seq(device)},
            device_id_type=MESH,
        )

    pairs = (
        (x_hbm, x), (wk_hbm, w.at[1]), (wb_hbm, wb_ref), (b_hbm, b_ref), (g_hbm, g),
        (wq_hbm, w.at[0]), (wv_hbm, w.at[2]),
    )
    loads = [pltpu.make_async_copy(s, t, load.at[i]) for i, (s, t) in enumerate(pairs)]
    for copy in loads:
        copy.start()
    barrier = pltpu.get_barrier_semaphore()
    others = [{"seq": seq(o)} for o in range(1, 8)]
    others += [{"head": lax.rem(group + r, groups)} for r in range(1, groups)]
    for peer in others:
        pl.semaphore_signal(barrier, inc=1, device_id=peer, device_id_type=MESH)
    wb[...] = jnp.zeros_like(wb)
    pl.semaphore_wait(barrier, len(others))

    fars, partners = (2, 4), (4, 2)
    slots = [(0, 1, far, far ^ 1) for far in fars]

    def columns(index):
        return pl.ds(pl.multiple_of(index * part, part), part)

    tokens, later = {}, [(0, 3, 1), (1, 3, 1)]
    for s in (2, 3, 1):
        for b in range(2):
            for a in range(2):
                if (a, s, b) != (1, 1, 0):
                    owner = seq(slots[a][s] ^ (partners[a] if b else 0))
                    i = len(tokens)
                    tokens[a, s, b] = remote(
                        x_hbm.at[:, columns(owner)], cols.at[a, s, b],
                        tok_send.at[i], tok_recv.at[i], slots[a][s],
                    )
                    if (a, s, b) not in later:
                        tokens[a, s, b].start()

    loads[0].wait()
    loads[1].wait()
    qkv[1] = dot(x[...], w[1])
    for copy in loads[2:]:
        copy.wait()
    wb[pl.ds(0, heads), :] = wb_ref[...]
    z[:, :heads] = dot(x[...], wb[:16], (1, 1))[:, :heads] + b_ref[...]
    def put_map(unit, factor, offset):
        maps[core, unit, 0] = factor.astype(bf16)
        maps[core, unit, 1] = offset.astype(bf16)

    def project(i, n):
        def run():
            span = slice(n * width // 2, (n + 1) * width // 2)
            qkv[i, :, span] = dot(x[...], w[i, :, span])

        return run

    def put_unit(qp, kp):
        for i, pairs in enumerate((qp, kp)):
            for h, (unit, scale) in enumerate(pairs):
                units[i, :, h * dim : (h + 1) * dim] = unit
                scales[:, i * heads + h : i * heads + h + 1] = scale

    fillers = [project(i, n) for i in (0, 2) for n in range(2)]
    put_mid = summarise(
        heads, dim, qkv.at[0], qkv.at[1], qkv.at[2], z, g, put_map, fillers, put_unit
    )
    passed, taken = across, 1 - across
    kept, other = pl.ds(core * half, half), pl.ds((1 - core) * half, half)
    urgent = [
        (way * heads + n * half, j)
        for j, (way, n) in enumerate(
            [(passed, 1 - core), (taken, 1 - core), (passed, core), (taken, core)]
        )
    ]
    sibling = [
        remote(
            maps.at[core, pl.ds(unit, half)], maps.at[core, pl.ds(unit, half)],
            map_send.at[j], map_recv.at[j], 1,
        )
        for unit, j in urgent
    ]
    arriving = [
        remote(
            maps.at[1 - core, pl.ds(way * heads + n * half, half)],
            maps.at[1 - core, pl.ds(way * heads + n * half, half)],
            map_send.at[j], map_recv.at[j], 1,
        )
        for j, (way, n) in enumerate([(passed, core), (taken, core), (passed, 1 - core), (taken, 1 - core)])
    ]
    for copy in sibling:
        copy.start()
    put_mid(mid)
    arriving[0].wait_recv()

    def chip_total(way, n):
        unit = way * heads + core * half + n
        first = jnp.concatenate([maps[way, unit, 0], maps[way, unit, 1]], 0)
        factor = maps[1 - way, unit, 0]
        moved = dot(first, factor)
        both = first.astype(f32) - moved
        return both[:dim] + factor.astype(f32), both[dim:] + maps[1 - way, unit, 1].astype(f32)

    for n in range(half):
        factor, offset = chip_total(passed, n)
        x_out[0, n] = offset.astype(bf16)
        x_out[1, n] = factor.astype(bf16)
    over = [remote(x_out.at[j], x_in.at[j, kept], x_send.at[j], x_recv.at[j], 2) for j in range(2)]
    for copy in over:
        copy.start()
    arriving[1].wait_recv()
    totals = [chip_total(taken, n) for n in range(half)]
    forward = [
        remote(x_in.at[j, kept], x_in.at[j, kept], f_send.at[j], f_recv.at[j], 1) for j in range(2)
    ]

    def own_columns(a, b):
        return x[:, columns(seq(partners[a]) if b else me)]

    def turn_block(a, s, b):
        if s == 0:
            block = own_columns(a, b)
        else:
            block = cols[0, 1, 0] if (a, s, b) == (1, 1, 0) else cols[a, s, b]
        cols_t[a, b * part : (b + 1) * part, s * rows : (s + 1) * rows] = block.T

    def turn(a):
        for s in range(4):
            for b in range(2):
                if (a, s, b) not in later:
                    turn_block(a, s, b)

    for key, copy in tokens.items():
        if key[0] == 0 and key not in later:
            copy.wait_recv()
    turn(0)
    over[0].wait_recv()
    for n, (factor, offset) in enumerate(totals):
        entering = x_in[0, core * half + n]
        y_out[n] = (entering.astype(f32) - mm((entering, None), split(factor)) + offset).astype(bf16)
    up = [remote(y_out, y_in.at[kept], y_send.at[j], y_recv, 4 + 2 * j) for j in range(2)]
    share = remote(y_in.at[kept], y_in.at[kept], y_send.at[2], s_recv, 1)

    @pl.when(upper == taken)
    def _():
        for copy in up:
            copy.start()

    forward[0].start()
    over[1].wait_recv()
    forward[1].start()
    for key in later:
        tokens[key].start()
    for key, copy in tokens.items():
        if key[0] == 1 and key not in later:
            copy.wait_recv()
    turn(1)
    for copy in forward + arriving[2:]:
        copy.wait_recv()
    state[...] = jnp.zeros_like(state)
    for h in range(heads):
        state[taken * heads + h] = x_in[0, h].astype(f32)
    bridge = []
    lead, inside = 1 - upper, 1 - core
    for h in range(heads):
        unit = inside * heads + h
        factor = maps[inside, unit, 0]
        before = state[unit]
        state[unit] = before - mm(split(before), (factor, None)) + maps[inside, unit, 1].astype(f32)
        first = jnp.where(taken == lead, x_in[1, h].astype(f32), 0.0).astype(bf16)
        second = jnp.where(inside == lead, factor.astype(f32), 0.0).astype(bf16)
        bridge.append(split(first.astype(f32) + second.astype(f32) - dot(first, second)))
    up[0].wait_recv()
    share.start()
    share.wait_recv()
    for h in range(heads):
        unit = lead * heads + h
        state[unit] = state[unit] + (y_in[h].astype(f32) - mm((y_in[h], None), bridge[h]))

    def put(i, h, span, value):
        a, n = h // half, h % half
        mine[span, i * width + h * dim : i * width + (h + 1) * dim] = value
        blocks[a, i, span, n * dim : (n + 1) * dim] = value

    def spread(a, i):
        if i < 3:
            slot = [blocks.at[a, i, pl.ds(s * rows, rows)] for s in range(4)]
        else:
            slot = [tails.at[s] for s in range(4)]
        return (
            remote(slot[0], slot[2], far_send.at[a, i], far_recv.at[a, i], fars[a]),
            remote(slot[0], slot[1], sib_send.at[a, i], sib_recv.at[a, i], 1),
            remote(slot[2], slot[3], fwd_send.at[a, i], fwd_recv.at[a, i], 1),
        )

    def unit_state(unit):
        return state[unit].astype(bf16)

    spreads = {(a, i): spread(a, i) for a in range(2) for i in range(3)}
    spreads[0, 3] = spread(0, 3)

    def send(key):
        for copy in spreads[key][:2]:
            copy.start()

    def valued():
        send((0, 2))
        send((1, 2))

    def strength(span, dz):
        last = strength_lanes(heads, dz)
        mine[span, 3 * width :] = last.astype(bf16)
        tails[0, :, span] = last.T[:16].astype(bf16)

    def unit_pairs(i):
        return [
            (units[i, :, h * dim : (h + 1) * dim], scales[:, i * heads + h : i * heads + h + 1])
            for h in range(heads)
        ]

    halves = [slice(0, rows // 2), slice(rows // 2, rows)]

    def input_part(index, rows):
        span = pl.ds(pl.multiple_of(index * width, width), width)
        total = dot(mine[rows, 3 * width :], wb[:, span])
        for i in range(3):
            total = total + dot(mine[rows, i * width : (i + 1) * width], w[i, span, :], (1, 1))
        return total

    side = 1 - 2 * (group // 2)
    edge = (group == 0) | (group == groups - 1)
    rim = jnp.where(edge, 1, 0)
    targets = [
        group + side * (1 + 2 * rim),
        group + side * (3 * rim - 1),
        group + side * (2 - rim),
    ]

    def landing(n, h):
        slot = jnp.where(edge, groups, group) if n == 0 else group
        device = group + side if n == 0 else targets[n]
        return remote(
            piece.at[n, halves[h]], landed.at[slot, halves[h]],
            z_send.at[n, h], z_recv.at[slot, h], {"head": device},
        )

    def first_piece(h):
        piece[0, halves[h]] = input_part(targets[0], halves[h]).astype(bf16)
        landing(0, h).start()

    gradients(
        heads, dim, unit_pairs(0), unit_pairs(1), z, g, mid, unit_state, put, strength,
        valued, lambda: first_piece(0),
    )
    for key in ((0, 0), (1, 0), (0, 1), (1, 1), (0, 3)):
        send(key)
    first_piece(1)
    piece[1] = input_part(targets[1], slice(0, rows)).astype(bf16)
    for h in range(2):
        landing(1, h).start()
    piece[2] = input_part(targets[2], slice(0, rows)).astype(bf16)

    @pl.when(edge)
    def _():
        for h in range(2):
            landing(2, h).start()

    own[...] = input_part(group, slice(0, rows))

    def arrived(slot, h):
        remote(
            piece.at[0, halves[h]], landed.at[slot, halves[h]],
            z_send.at[0, h], z_recv.at[slot, h], {"head": targets[0]},
        ).wait_recv()
        return landed[slot, halves[h]].astype(f32)

    def pass_on(h):
        @pl.when(jnp.logical_not(edge))
        def _():
            piece[2, halves[h]] = (piece[2, halves[h]].astype(f32) + arrived(groups, h)).astype(bf16)
            landing(2, h).start()

    order = [(0, 2), (1, 2), (0, 0), (1, 0), (0, 1), (1, 1), (0, 3)]
    trades = {
        (a, i): remote(
            part_out.at[a, i], part_in.at[a, i], part_send.at[a, i], part_recv.at[a, i], partners[a]
        )
        for a in range(2)
        for i in range(3)
    }
    tail_trade = remote(tail_out, tail_in, part_send.at[0, 3], part_recv.at[0, 3], partners[0])

    def process(a, i):
        spreads[a, i][1].wait_recv()
        spreads[a, i][2].wait_recv()
        if i < 3:
            value = dot(cols_t[a], blocks[a, i])
            part_out[a, i] = value[part:].astype(bf16)
            trades[a, i].start()
            grads[i, :, a * half * dim : (a + 1) * half * dim] = value[:part]
        else:
            sums = [dot(tails[0], own_columns(0, b)) for b in range(2)]
            for s in range(1, 4):
                sums = [t + dot(tails[s], cols[0, s, b]) for b, t in enumerate(sums)]
            held = jnp.sum(tails[...].astype(f32), 0)
            held = jnp.sum(held, -1, keepdims=True)
            row, col = iotas(16, part)
            held = jnp.sum(jnp.where(row == col, held, 0.0), 0, keepdims=True)
            row = lax.broadcasted_iota(jnp.int32, (16, part), 0)
            tail_out[...] = jnp.where(row == 8, held, sums[1])
            tail_trade.start()
            tail_ref[...] = jnp.where(row == 8, held, sums[0])

    for key in later:
        tokens[key].wait_recv()
        turn_block(*key)
    for n, key in enumerate(order):
        spreads[key][0].wait_recv()
        spreads[key][2].start()
        if n > 0:
            process(*order[n - 1])
        if n == 1:
            pass_on(0)
        if n == 3:
            pass_on(1)

    process(*order[-1])
    saves = []

    def keep(source, target):
        copy = pltpu.make_async_copy(source, target, save.at[len(saves)])
        copy.start()
        saves.append(copy)

    targets_hbm = (gq_hbm, gk_hbm, gv_hbm)
    for a, i in order:
        if i < 3:
            trades[a, i].wait_recv()
            span = slice(a * half * dim, (a + 1) * half * dim)
            grads[i, :, span] = grads[i, :, span] + part_in[a, i].astype(f32)
            keep(grads.at[i, :, span], targets_hbm[i].at[:, span])
        else:
            tail_trade.wait_recv()
            tail_ref[...] = tail_ref[...] + tail_in[...]
            keep(tail_ref, tail_hbm)

    for h in range(2):

        @pl.when(jnp.logical_not(edge))
        def _():
            own[halves[h]] = own[halves[h]] + arrived(group - side, h)

        total = own[halves[h]] + arrived(group + side, h) + arrived(group + 2 * side, h)
        dx_ref[halves[h]] = total.astype(bf16)
        keep(dx_ref.at[halves[h]], dx_hbm.at[halves[h]])

    share.wait_send()

    @pl.when(upper == taken)
    def _():
        for copy in up:
            copy.wait_send()

    for n in range(3):
        for h in range(2):
            landing(n, h).wait_send()
    for copy in sibling + list(tokens.values()) + over + forward + [tail_trade] + list(trades.values()):
        copy.wait_send()
    for copies in spreads.values():
        for copy in copies:
            copy.wait_send()
    for copy in saves:
        copy.wait()


def place_kernel(count, heads, *refs):
    sources, outs = refs[: count + 1], refs[count + 1 : 2 * count + 3]
    held, sems = refs[2 * count + 3 : -1], refs[-1]
    fetch, store = [], []
    for i in range(count):
        size = sources[i].shape[0] // 2
        for n in range(2):
            span = pl.ds(n * size, size)
            j = 2 * i + n
            fetch.append(
                pltpu.make_async_copy(sources[i].at[span], held[i].at[span], sems.at[0, j])
            )
            store.append(pltpu.make_async_copy(held[i].at[span], outs[i].at[span], sems.at[1, j]))
    small = pltpu.make_async_copy(sources[count], held[count], sems.at[0, 2 * count])
    for copy in fetch:
        copy.start()
    small.start()
    for j in range(2 * count):
        fetch[j].wait()
        store[j].start()
    small.wait()
    outs[count][...] = held[count][:heads, :]
    outs[count + 1][...] = held[count][8:9, :heads] + held[count][8:9, heads : 2 * heads]
    for copy in store:
        copy.wait()


def place(arrays, tail, heads):
    count = len(arrays)
    vmem = pl.BlockSpec(memory_space=pltpu.VMEM)
    hbm = pl.BlockSpec(memory_space=pltpu.HBM)
    return pl.pallas_call(
        functools.partial(place_kernel, count, heads),
        out_shape=tuple(jax.ShapeDtypeStruct(a.shape, a.dtype) for a in arrays)
        + (
            jax.ShapeDtypeStruct((heads, tail.shape[1]), tail.dtype),
            jax.ShapeDtypeStruct((1, heads), tail.dtype),
        ),
        in_specs=[hbm] * (count + 1),
        out_specs=(hbm,) * count + (vmem,) * 2,
        scratch_shapes=[pltpu.VMEM(a.shape, a.dtype) for a in (*arrays, tail)]
        + [pltpu.SemaphoreType.DMA((2, 2 * count + 1))],
        compiler_params=pltpu.CompilerParams(vmem_limit_bytes=60 * 1024 * 1024),
        name="place",
    )(*arrays, tail)


def whole_layer(tokens, weights, w_beta, b_beta, d_out):
    shards, groups = lax.axis_size("seq"), lax.axis_size("head")
    rows, features = tokens.shape
    heads = w_beta.shape[1]
    width = weights[0].shape[1]
    dim = width // heads
    half = heads // 2
    part = features // shards
    f32, bf16 = jnp.float32, jnp.bfloat16
    hbm = pl.BlockSpec(memory_space=pltpu.HBM)
    square = jax.ShapeDtypeStruct((part, width), f32)
    dma = pltpu.SemaphoreType.DMA
    outs = pl.pallas_call(
        functools.partial(layer_kernel, groups, heads, dim),
        out_shape=(
            jax.ShapeDtypeStruct((rows, features // groups), tokens.dtype),
            square,
            square,
            square,
            jax.ShapeDtypeStruct((16, part), f32),
        ),
        in_specs=[hbm] * 7,
        out_specs=(hbm,) * 5,
        scratch_shapes=[
            pltpu.VMEM((rows, features // groups), bf16),
            pltpu.VMEM((3, part, width), f32),
            pltpu.VMEM((16, part), f32),
            pltpu.VMEM((rows, features), bf16),
            pltpu.VMEM((3, features, width), bf16),
            pltpu.VMEM((LANES, features), bf16),
            pltpu.VMEM((rows, width), bf16),
            pltpu.VMEM((heads, features), bf16),
            pltpu.VMEM((1, heads), f32),
            pltpu.VMEM((3, rows, width), f32),
            pltpu.VMEM((2, rows, width), f32),
            pltpu.VMEM((rows, LANES), f32),
            pltpu.VMEM((rows, LANES), f32),
            pltpu.VMEM((heads, rows, 4 * dim), f32),
            pltpu.VMEM((2, 2 * heads, 2, dim, dim), bf16),
            pltpu.VMEM((2, half, dim, dim), bf16),
            pltpu.VMEM((2, heads, dim, dim), bf16),
            pltpu.VMEM((half, dim, dim), bf16),
            pltpu.VMEM((heads, dim, dim), bf16),
            pltpu.VMEM((2 * heads, dim, dim), f32),
            pltpu.VMEM((2, 4, 2, rows, part), bf16),
            pltpu.VMEM((2, 2 * part, 4 * rows), bf16),
            pltpu.VMEM((rows, 3 * width + LANES), bf16),
            pltpu.VMEM((2, 3, 4 * rows, width // 2), bf16),
            pltpu.VMEM((4, 16, rows), bf16),
            pltpu.VMEM((2, 3, part, width // 2), bf16),
            pltpu.VMEM((2, 3, part, width // 2), bf16),
            pltpu.VMEM((16, part), f32),
            pltpu.VMEM((16, part), f32),
            pltpu.VMEM((rows, features // groups), f32),
            pltpu.VMEM((3, rows, features // groups), bf16),
            pltpu.VMEM((groups + 1, rows, features // groups), bf16),
            dma((7,)),
            dma((11,)),
            dma((11,)),
            dma((4,)),
            dma((4,)),
            dma((2,)),
            dma((2,)),
            dma((2,)),
            dma((2,)),
            dma((3,)),
            dma,
            dma,
            dma((2, 4)),
            dma((2, 4)),
            dma((2, 4)),
            dma((2, 4)),
            dma((2, 4)),
            dma((2, 4)),
            dma((2, 4)),
            dma((2, 4)),
            dma((3, 2)),
            dma((groups + 1, 2)),
            dma((9,)),
        ],
        compiler_params=pltpu.CompilerParams(
            vmem_limit_bytes=60 * 1024 * 1024, collective_id=1, has_side_effects=True
        ),
        name="layer",
    )(tokens, *weights, d_out, w_beta.T, b_beta.reshape(1, heads))
    d_x, grad_q, grad_k, grad_v, tail, bias = place(outs[:4], outs[4], heads)
    return d_x, grad_q, grad_k, grad_v, tail.T, bias.reshape(heads)


def per_device(tokens, w_query, w_key, w_value, w_beta, b_beta, d_out):
    token_count, features = tokens.shape
    heads = w_beta.shape[1]
    width = w_query.shape[1]
    dim = width // heads
    f32 = jnp.float32
    shards, groups = lax.axis_size("seq"), lax.axis_size("head")
    weights = (w_query, w_key, w_value)
    fits = heads % 2 == 0 and 2 * heads <= 8 and width * groups == features and dim == LANES
    if shards == 8 and groups == 4 and fits and features // shards == token_count:
        return whole_layer(tokens, weights, w_beta, b_beta, d_out)
    q, k, v = (jnp.dot(tokens, w, preferred_element_type=f32) for w in weights)
    w_last = jnp.pad(w_beta, ((0, 0), (0, LANES - heads)))
    z = jnp.dot(tokens, w_last, preferred_element_type=f32) + jnp.pad(b_beta, (0, LANES - heads))
    params = pltpu.CompilerParams(vmem_limit_bytes=60 * 1024 * 1024)
    columns = lax.all_to_all(tokens, "seq", split_axis=1, concat_axis=0, tiled=True)
    maps, mid = pl.pallas_call(
        functools.partial(summary_kernel, heads, dim),
        out_shape=(
            jax.ShapeDtypeStruct((2 * heads, 2, dim, dim), jnp.bfloat16),
            jax.ShapeDtypeStruct((heads, token_count, 4 * dim), f32),
        ),
        compiler_params=params,
        name="summary",
    )(q, k, v, z, d_out)
    states = gathered_states(maps, heads)
    grads = pl.pallas_call(
        functools.partial(gradient_kernel, heads, dim),
        out_shape=jax.ShapeDtypeStruct((token_count, 3 * width + LANES), jnp.bfloat16),
        compiler_params=params,
        name="gradient",
    )(q, k, z, d_out, mid, states)
    whole = lax.all_gather(grads, "seq", axis=0, tiled=True)
    partial = jnp.dot(grads[:, 3 * width : 3 * width + heads], w_beta.T, preferred_element_type=f32)
    for i, w in enumerate(weights):
        partial = partial + jnp.dot(
            grads[:, i * width : (i + 1) * width], w.T, preferred_element_type=f32
        )
    d_x = lax.psum_scatter(
        partial.astype(jnp.bfloat16), "head", scatter_dimension=1, tiled=True
    )

    def weight_grad(block):
        return lax.dot_general(
            columns, block, (((0,), (0,)), ((), ())), preferred_element_type=f32
        )

    found = [weight_grad(whole[:, i * width : (i + 1) * width]) for i in range(3)]
    tail = whole[:, 3 * width :]
    grad_wbeta = weight_grad(tail)[:, :heads]
    sums = jnp.sum(tail.astype(f32), 0)
    return (d_x, *found, grad_wbeta, sums[:heads] + sums[heads : 2 * heads])


def solution(mesh):
    in_specs = (
        P("seq", None),
        P(None, "head"),
        P(None, "head"),
        P(None, "head"),
        P(None, "head"),
        P("head"),
        P("seq", "head"),
    )
    out_specs = (
        P("seq", "head"),
        P("seq", "head"),
        P("seq", "head"),
        P("seq", "head"),
        P("seq", "head"),
        P("head"),
    )
    return jax.shard_map(
        per_device, mesh=mesh, in_specs=in_specs, out_specs=out_specs, check_vma=False
    )
```

```python
import functools

import jax
import jax.numpy as jnp
from jax import lax
from jax.experimental import pallas as pl
from jax.experimental.pallas import tpu as pltpu
from jax.sharding import PartitionSpec as P

epsilon = 1e-06
LANES = 128
MESH = pl.DeviceIdType.MESH
highest = lax.Precision.HIGHEST


def split(a):
    high = a.astype(jnp.bfloat16)
    return high, (a - high.astype(jnp.float32)).astype(jnp.bfloat16)


def only(a):
    return a.astype(jnp.bfloat16), None


def mm(a, b, dims=(1, 0)):
    numbers = (((dims[0],), (dims[1],)), ((), ()))
    dot = functools.partial(
        lax.dot_general, dimension_numbers=numbers, preferred_element_type=jnp.float32
    )
    total = dot(a[0], b[0])
    if b[1] is not None:
        total = total + dot(a[0], b[1])
    if a[1] is not None:
        total = total + dot(a[1], b[0])
    return total


def square_mm(a, b):
    size = a[0].shape[0]
    left = jnp.concatenate(a, 1)
    right = jnp.concatenate(
        [jnp.concatenate(b, 1), jnp.concatenate([b[0], jnp.zeros_like(b[0])], 1)], 0
    )
    both = lax.dot_general(left, right, (((1,), (0,)), ((), ())), preferred_element_type=jnp.float32)
    return both[:, :size] + both[:, size:]


def tight_mm(a, b, dims=(1, 0)):
    inner, outer = dims[1], 1 - dims[1]
    size = b[0].shape[outer]
    left = a[0] if a[1] is None else jnp.concatenate(a, dims[0])
    right = b[0] if b[1] is None else jnp.concatenate(b, outer)
    if a[1] is not None:
        again = b[0]
        if b[1] is not None:
            again = jnp.concatenate([b[0], jnp.zeros_like(b[0])], outer)
        right = jnp.concatenate([right, again], inner)
    both = lax.dot_general(
        left, right, (((dims[0],), (dims[1],)), ((), ())), preferred_element_type=jnp.float32
    )
    return both if b[1] is None else both[:, :size] + both[:, size:]


def wide_mm(a, b, dims=(1, 0)):
    numbers = (((dims[0],), (dims[1],)), ((), ()))
    size = b[0].shape[1 - dims[1]]
    both = lax.dot_general(
        a[0], jnp.concatenate(b, 1 - dims[1]), numbers, preferred_element_type=jnp.float32
    )
    total = both[:, :size] + both[:, size:]
    if a[1] is not None:
        total = total + lax.dot_general(a[1], b[0], numbers, preferred_element_type=jnp.float32)
    return total


def iotas(rows, cols):
    return (
        lax.broadcasted_iota(jnp.int32, (rows, cols), 0),
        lax.broadcasted_iota(jnp.int32, (rows, cols), 1),
    )


def invert_unit_lower(systems, fillers=()):
    fillers = list(fillers)
    size = systems[0].shape[0]
    base = min(size, LANES)
    row, col = iotas(base, base)
    eye = jnp.where(row == col, 1.0, 0.0).astype(jnp.float32)

    def step_mask(s):
        return (row // (2 * s) == col // (2 * s)) & (row % (2 * s) >= s) & (col % (2 * s) < s)

    count = size // base
    diagonals = [
        n[i * base : (i + 1) * base, i * base : (i + 1) * base] for n in systems for i in range(count)
    ]
    inverses = [eye - jnp.where(step_mask(1), n, 0.0) for n in diagonals]
    pairs = [split(n) for n in diagonals]
    s = 2
    while s < base:
        mask = jnp.where(step_mask(s), 1.0, 0.0).astype(jnp.bfloat16)
        parts = [split(x) for x in inverses]
        inner = [square_mm((mask * n[0], mask * n[1]), x) for n, x in zip(pairs, parts)]
        if fillers:
            fillers.pop(0)()
        outer = [square_mm(x, split(y)) for x, y in zip(parts, inner)]
        inverses = [x - y for x, y in zip(inverses, outer)]
        s *= 2
    for filler in fillers:
        filler()
    grouped = [inverses[i * count : (i + 1) * count] for i in range(len(systems))]
    width = base
    while width < size:
        merged = []
        for n, blocks in zip(systems, grouped):
            joined = []
            for i in range(0, len(blocks), 2):
                first, second = blocks[i], blocks[i + 1]
                low = n[(i + 1) * width : (i + 2) * width, i * width : (i + 1) * width]
                corner = square_mm(split(second), split(square_mm(split(low), split(first))))
                joined.append(
                    jnp.concatenate(
                        [
                            jnp.concatenate([first, jnp.zeros_like(first)], 1),
                            jnp.concatenate([-corner, second], 1),
                        ],
                        0,
                    )
                )
            merged.append(joined)
        grouped = merged
        width *= 2
    return [g[0] for g in grouped]


def normalise(raw):
    scale = lax.rsqrt(jnp.sum(raw * raw, -1, keepdims=True) + epsilon)
    return raw * scale, scale


def dot(a, b, dims=(1, 0)):
    return lax.dot_general(
        a, b, (((dims[0],), (dims[1],)), ((), ())), preferred_element_type=jnp.float32
    )


def summarise(heads, dim, q_ref, k_ref, v_ref, z_ref, g_ref, put_map, fillers=(), put_unit=None):
    count = q_ref.shape[0]
    row, col = iotas(count, count)
    strict, inclusive = row > col, row >= col
    every = range(heads)
    cols = [slice(h * dim, (h + 1) * dim) for h in every]
    beta_all = 2.0 * jax.nn.sigmoid(z_ref[:, :heads])
    beta = [beta_all[:, h : h + 1] for h in every]
    kp = [normalise(k_ref[:, c]) for c in cols]
    kn = [x[0] for x in kp]
    ks = [split(x) for x in kn]
    gs = [(g_ref[:, c], None) for c in cols]
    gram = [jnp.where(strict, mm(x, x, (1, 1)), 0.0) for x in ks]
    systems = [b * n for b, n in zip(beta, gram)]
    inverse = [split(t) for t in invert_unit_lower(systems, fillers)]
    qp = [normalise(q_ref[:, c]) for c in cols]
    qs = [split(x[0]) for x in qp]
    if put_unit is not None:
        put_unit(qp, kp)
    gram = [split(n) for n in gram]
    scores = [split(jnp.where(inclusive, mm(a, b, (1, 1)), 0.0)) for a, b in zip(qs, ks)]
    back = [mm(p, g, (0, 0)) for p, g in zip(scores, gs)]
    forth_in = [jnp.concatenate([v_ref[:, c], k], 1) for c, k in zip(cols, kn)]
    forth = [split(mm(t, split(b * x))) for t, b, x in zip(inverse, beta, forth_in)]
    adjoint = [
        mm(t, split(jnp.concatenate([p, k], 1)), (0, 0)) for t, p, k in zip(inverse, back, kn)
    ]
    ends = [wide_mm(f, k, (0, 0)) for f, k in zip(forth, ks)]
    tails = [wide_mm(split(a), split(b * k), (0, 0)) for a, b, k in zip(adjoint, beta, kn)]
    direct = [wide_mm(g, q, (0, 0)) for g, q in zip(gs, qs)]
    for h in every:
        put_map(h, ends[h][dim:], ends[h][:dim])
        put_map(heads + h, tails[h][dim:], direct[h] - tails[h][:dim])

    def put_mid(mid_ref):
        for h in every:
            mid_ref[h, :, : 2 * dim] = forth_in[h] - mm(gram[h], forth[h])
            mid_ref[h, :, 2 * dim :] = adjoint[h]

    return put_mid


def summary_kernel(heads, dim, q_ref, k_ref, v_ref, z_ref, g_ref, map_ref, mid_ref):
    def put_map(unit, factor, offset):
        map_ref[unit, 0] = factor.astype(map_ref.dtype)
        map_ref[unit, 1] = offset.astype(map_ref.dtype)

    summarise(heads, dim, q_ref, k_ref, v_ref, z_ref, g_ref, put_map)(mid_ref)


def gradients(heads, dim, qp, kp, z_ref, g_ref, mid_ref, state, put, strength, valued, between):
    every = range(heads)
    count = z_ref.shape[0] // 2
    halves = (slice(0, count), slice(count, 2 * count))
    row, col = iotas(count, count)
    strict, inclusive = row > col, row >= col
    beta_all = 2.0 * jax.nn.sigmoid(z_ref[:, :heads])
    beta = [beta_all[:, h : h + 1] for h in every]
    ss = [(state(h), None) for h in every]
    ds = [(state(heads + h), None) for h in every]
    dx = [
        mid_ref[h, :, 2 * dim : 3 * dim] + tight_mm(split(mid_ref[h, :, 3 * dim :]), d, (1, 1))
        for h, d in zip(every, ds)
    ]
    dv = [b * x for b, x in zip(beta, dx)]
    for h in every:
        put(2, h, slice(0, 2 * count), dv[h].astype(jnp.bfloat16))
    valued()

    def pick(x, rows):
        return tuple(None if y is None else y[rows] for y in x)

    def part(rows):
        ks = [split(x[0][rows]) for x in kp]
        qs = [split(x[0][rows]) for x in qp]
        gs = [(g_ref[rows, h * dim : (h + 1) * dim], None) for h in every]
        plain = [
            mid_ref[h, rows, :dim] - tight_mm(split(mid_ref[h, rows, dim : 2 * dim]), s, (1, 1))
            for h, s in zip(every, ss)
        ]
        us = [split(b[rows] * x) for b, x in zip(beta, plain)]
        dz = [
            jnp.sum(x[rows] * p, -1, keepdims=True) * b[rows] * (1.0 - 0.5 * b[rows])
            for x, p, b in zip(dx, plain, beta)
        ]
        return ks, qs, gs, us, dz

    def through(grad, pair, rows):
        unit, scale = pair[0][rows], pair[1][rows]
        return scale * (grad - unit * jnp.sum(unit * grad, -1, keepdims=True))

    def finish(rows, dqn, dkn):
        for h in every:
            put(0, h, rows, through(dqn[h], qp[h], rows).astype(jnp.bfloat16))
            put(1, h, rows, through(dkn[h], kp[h], rows).astype(jnp.bfloat16))

    def below(a, b, mask):
        found = [tight_mm(x, y, (1, 1)) for x, y in zip(a, b)]
        return found if mask is None else [jnp.where(mask, x, 0.0) for x in found]

    dvs = [[split(x[rows]) for x in dv] for rows in halves]
    k0, q0, g0, u0, dz = part(halves[0])
    strength(halves[0], dz)
    k1 = [split(x[0][halves[1]]) for x in kp]
    q1 = [split(x[0][halves[1]]) for x in qp]
    g1 = [(g_ref[halves[1], h * dim : (h + 1) * dim], None) for h in every]
    inner0 = [split(x) for x in below(g0, u0, inclusive)]
    pair0 = below(dvs[0], u0, strict)
    inner1 = [split(x) for x in below(g1, u0, None)]
    pair1 = below(dvs[1], u0, None)
    dqn = [tight_mm(g, s) + tight_mm(i, k) for g, s, i, k in zip(g0, ss, inner0, k0)]
    dkn = [
        tight_mm(i, q, (0, 0)) + tight_mm(j, r, (0, 0)) + tight_mm(u, d) - tight_mm(x, s)
        - tight_mm(split(e + e.T), k) - tight_mm(split(f.T), l)
        for i, q, j, r, u, d, x, s, e, k, f, l in zip(
            inner0, q0, inner1, q1, u0, ds, dvs[0], ss, pair0, k0, pair1, k1
        )
    ]
    finish(halves[0], dqn, dkn)
    between()
    k1, q1, g1, u1, dz = part(halves[1])
    strength(halves[1], dz)
    inner2 = [split(x) for x in below(g1, u1, inclusive)]
    pair2 = below(dvs[1], u1, strict)
    dqn = [
        tight_mm(g, s) + tight_mm(j, k) + tight_mm(i, l)
        for g, s, j, k, i, l in zip(g1, ss, inner1, k0, inner2, k1)
    ]
    dkn = [
        tight_mm(i, q, (0, 0)) + tight_mm(u, d) - tight_mm(x, s) - tight_mm(split(f), k) - tight_mm(split(e + e.T), l)
        for i, q, u, d, x, s, f, k, e, l in zip(
            inner2, q1, u1, ds, dvs[1], ss, pair1, k0, pair2, k1
        )
    ]
    finish(halves[1], dqn, dkn)


def strength_lanes(heads, dz):
    lane = lax.broadcasted_iota(jnp.int32, (dz[0].shape[0], LANES), 1)
    last = jnp.zeros((dz[0].shape[0], LANES), jnp.float32)
    for h in range(heads):
        high, low = split(dz[h])
        last = jnp.where(lane == h, high.astype(jnp.float32), last)
        last = jnp.where(lane == heads + h, low.astype(jnp.float32), last)
    return last


def gradient_kernel(heads, dim, q_ref, k_ref, z_ref, g_ref, mid_ref, state_ref, out_ref):
    width = heads * dim

    def put(i, h, rows, value):
        out_ref[rows, i * width + h * dim : i * width + (h + 1) * dim] = value

    def state(unit):
        return state_ref[unit]

    def strength(rows, dz):
        out_ref[rows, 3 * width :] = strength_lanes(heads, dz).astype(jnp.bfloat16)

    cols = [slice(h * dim, (h + 1) * dim) for h in range(heads)]
    qp = [normalise(q_ref[:, c]) for c in cols]
    kp = [normalise(k_ref[:, c]) for c in cols]
    gradients(
        heads, dim, qp, kp, z_ref, g_ref, mid_ref, state, put, strength,
        lambda: None, lambda: None,
    )


def gathered_states(maps, heads):
    count = lax.axis_size("seq")
    place = lax.axis_index("seq")
    gathered = lax.all_gather(maps, "seq").astype(jnp.float32)

    def walk(steps, pick, rows):
        def one(lap, state):
            pair = lax.dynamic_index_in_dim(gathered, pick(lap), 0, False)[rows]
            moved = jnp.einsum("hij,hjk->hik", state, pair[:, 0], precision=highest)
            return state - moved + pair[:, 1]

        return lax.fori_loop(0, steps, one, jnp.zeros((heads,) + maps.shape[2:], jnp.float32))

    first = walk(place, lambda lap: lap, slice(0, heads))
    second = walk(count - 1 - place, lambda lap: count - 1 - lap, slice(heads, None))
    return jnp.concatenate([first, second]).astype(maps.dtype)


def layer_kernel(
    groups, heads, dim,
    x_hbm, wq_hbm, wk_hbm, wv_hbm, g_hbm, wb_hbm, b_hbm,
    dx_hbm, gq_hbm, gk_hbm, gv_hbm, tail_hbm,
    dx_ref, grads, tail_ref, x, w, wb, g, wb_ref, b_ref, qkv, units, scales, z, mid, maps, x_out, x_in, y_out, y_in, state,
    cols, cols_t, mine, blocks, tails, part_out, part_in, tail_out, tail_in,
    own, piece, landed,
    load, tok_send, tok_recv, map_send, map_recv, x_send, x_recv, f_send, f_recv,
    y_send, y_recv, s_recv, far_send, far_recv, sib_send, sib_recv, fwd_send, fwd_recv,
    part_send, part_recv, z_send, z_recv, save,
):
    me = lax.axis_index("seq")
    group = lax.axis_index("head")
    core, across, upper = me % 2, (me // 2) % 2, me // 4
    rows, width = g.shape
    part = cols.shape[-1]
    half = heads // 2
    f32, bf16 = jnp.float32, jnp.bfloat16

    def seq(o):
        index = me
        for bit in (1, 2, 4):
            if o & bit:
                index = index + bit - 2 * bit * ((me // bit) % 2)
        return index

    def remote(source, target, send, recv, device):
        return pltpu.make_async_remote_copy(
            src_ref=source,
            dst_ref=target,
            send_sem=send,
            recv_sem=recv,
            device_id=device if isinstance(device, dict) else {"seq": seq(device)},
            device_id_type=MESH,
        )

    pairs = (
        (x_hbm, x), (wk_hbm, w.at[1]), (wb_hbm, wb_ref), (b_hbm, b_ref), (g_hbm, g),
        (wq_hbm, w.at[0]), (wv_hbm, w.at[2]),
    )
    loads = [pltpu.make_async_copy(s, t, load.at[i]) for i, (s, t) in enumerate(pairs)]
    for copy in loads:
        copy.start()
    barrier = pltpu.get_barrier_semaphore()
    others = [{"seq": seq(o)} for o in range(1, 8)]
    others += [{"head": lax.rem(group + r, groups)} for r in range(1, groups)]
    for peer in others:
        pl.semaphore_signal(barrier, inc=1, device_id=peer, device_id_type=MESH)
    wb[...] = jnp.zeros_like(wb)
    pl.semaphore_wait(barrier, len(others))

    fars, partners = (2, 4), (4, 2)
    slots = [(0, 1, far, far ^ 1) for far in fars]

    def columns(index):
        return pl.ds(pl.multiple_of(index * part, part), part)

    tokens, later = {}, [(0, 3, 1), (1, 3, 1)]
    for s in (2, 3, 1):
        for b in range(2):
            for a in range(2):
                if (a, s, b) != (1, 1, 0):
                    owner = seq(slots[a][s] ^ (partners[a] if b else 0))
                    i = len(tokens)
                    tokens[a, s, b] = remote(
                        x_hbm.at[:, columns(owner)], cols.at[a, s, b],
                        tok_send.at[i], tok_recv.at[i], slots[a][s],
                    )
                    if (a, s, b) not in later:
                        tokens[a, s, b].start()

    loads[0].wait()
    loads[1].wait()
    qkv[1] = dot(x[...], w[1])
    for copy in loads[2:]:
        copy.wait()
    wb[pl.ds(0, heads), :] = wb_ref[...]
    z[:, :heads] = dot(x[...], wb[:16], (1, 1))[:, :heads] + b_ref[...]
    def put_map(unit, factor, offset):
        maps[core, unit, 0] = factor.astype(bf16)
        maps[core, unit, 1] = offset.astype(bf16)

    def project(i, n):
        def run():
            span = slice(n * width // 2, (n + 1) * width // 2)
            qkv[i, :, span] = dot(x[...], w[i, :, span])

        return run

    def put_unit(qp, kp):
        for i, pairs in enumerate((qp, kp)):
            for h, (unit, scale) in enumerate(pairs):
                units[i, :, h * dim : (h + 1) * dim] = unit
                scales[:, i * heads + h : i * heads + h + 1] = scale

    fillers = [project(i, n) for i in (0, 2) for n in range(2)]
    put_mid = summarise(
        heads, dim, qkv.at[0], qkv.at[1], qkv.at[2], z, g, put_map, fillers, put_unit
    )
    passed, taken = across, 1 - across
    kept, other = pl.ds(core * half, half), pl.ds((1 - core) * half, half)
    urgent = [
        (way * heads + n * half, j)
        for j, (way, n) in enumerate(
            [(passed, 1 - core), (taken, 1 - core), (passed, core), (taken, core)]
        )
    ]
    sibling = [
        remote(
            maps.at[core, pl.ds(unit, half)], maps.at[core, pl.ds(unit, half)],
            map_send.at[j], map_recv.at[j], 1,
        )
        for unit, j in urgent
    ]
    arriving = [
        remote(
            maps.at[1 - core, pl.ds(way * heads + n * half, half)],
            maps.at[1 - core, pl.ds(way * heads + n * half, half)],
            map_send.at[j], map_recv.at[j], 1,
        )
        for j, (way, n) in enumerate([(passed, core), (taken, core), (passed, 1 - core), (taken, 1 - core)])
    ]
    for copy in sibling:
        copy.start()
    put_mid(mid)
    arriving[0].wait_recv()

    def chip_total(way, n):
        unit = way * heads + core * half + n
        first = jnp.concatenate([maps[way, unit, 0], maps[way, unit, 1]], 0)
        factor = maps[1 - way, unit, 0]
        moved = dot(first, factor)
        both = first.astype(f32) - moved
        return both[:dim] + factor.astype(f32), both[dim:] + maps[1 - way, unit, 1].astype(f32)

    for n in range(half):
        factor, offset = chip_total(passed, n)
        x_out[0, n] = offset.astype(bf16)
        x_out[1, n] = factor.astype(bf16)
    over = [remote(x_out.at[j], x_in.at[j, kept], x_send.at[j], x_recv.at[j], 2) for j in range(2)]
    for copy in over:
        copy.start()
    arriving[1].wait_recv()
    totals = [chip_total(taken, n) for n in range(half)]
    forward = [
        remote(x_in.at[j, kept], x_in.at[j, kept], f_send.at[j], f_recv.at[j], 1) for j in range(2)
    ]

    def own_columns(a, b):
        return x[:, columns(seq(partners[a]) if b else me)]

    def turn_block(a, s, b):
        if s == 0:
            block = own_columns(a, b)
        else:
            block = cols[0, 1, 0] if (a, s, b) == (1, 1, 0) else cols[a, s, b]
        cols_t[a, b * part : (b + 1) * part, s * rows : (s + 1) * rows] = block.T

    def turn(a):
        for s in range(4):
            for b in range(2):
                if (a, s, b) not in later:
                    turn_block(a, s, b)

    for key, copy in tokens.items():
        if key[0] == 0 and key not in later:
            copy.wait_recv()
    turn(0)
    over[0].wait_recv()
    for n, (factor, offset) in enumerate(totals):
        entering = x_in[0, core * half + n]
        y_out[n] = (entering.astype(f32) - tight_mm((entering, None), split(factor)) + offset).astype(bf16)
    up = [remote(y_out, y_in.at[kept], y_send.at[j], y_recv, 4 + 2 * j) for j in range(2)]
    share = remote(y_in.at[kept], y_in.at[kept], y_send.at[2], s_recv, 1)

    @pl.when(upper == taken)
    def _():
        for copy in up:
            copy.start()

    forward[0].start()
    over[1].wait_recv()
    forward[1].start()
    for key in later:
        tokens[key].start()
    for key, copy in tokens.items():
        if key[0] == 1 and key not in later:
            copy.wait_recv()
    turn(1)
    for copy in forward + arriving[2:]:
        copy.wait_recv()
    state[...] = jnp.zeros_like(state)
    for h in range(heads):
        state[taken * heads + h] = x_in[0, h].astype(f32)
    bridge = []
    lead, inside = 1 - upper, 1 - core
    for h in range(heads):
        unit = inside * heads + h
        factor = maps[inside, unit, 0]
        before = state[unit]
        state[unit] = before - tight_mm(split(before), (factor, None)) + maps[inside, unit, 1].astype(f32)
        first = jnp.where(taken == lead, x_in[1, h].astype(f32), 0.0).astype(bf16)
        second = jnp.where(inside == lead, factor.astype(f32), 0.0).astype(bf16)
        bridge.append(split(first.astype(f32) + second.astype(f32) - dot(first, second)))
    up[0].wait_recv()
    share.start()
    share.wait_recv()
    for h in range(heads):
        unit = lead * heads + h
        state[unit] = state[unit] + (y_in[h].astype(f32) - tight_mm((y_in[h], None), bridge[h]))

    def put(i, h, span, value):
        a, n = h // half, h % half
        mine[span, i * width + h * dim : i * width + (h + 1) * dim] = value
        blocks[a, i, span, n * dim : (n + 1) * dim] = value

    def spread(a, i):
        if i < 3:
            slot = [blocks.at[a, i, pl.ds(s * rows, rows)] for s in range(4)]
        else:
            slot = [tails.at[s] for s in range(4)]
        return (
            remote(slot[0], slot[2], far_send.at[a, i], far_recv.at[a, i], fars[a]),
            remote(slot[0], slot[1], sib_send.at[a, i], sib_recv.at[a, i], 1),
            remote(slot[2], slot[3], fwd_send.at[a, i], fwd_recv.at[a, i], 1),
        )

    def unit_state(unit):
        return state[unit].astype(bf16)

    spreads = {(a, i): spread(a, i) for a in range(2) for i in range(3)}
    spreads[0, 3] = spread(0, 3)

    def send(key):
        for copy in spreads[key][:2]:
            copy.start()

    def valued():
        send((0, 2))
        send((1, 2))

    def strength(span, dz):
        last = strength_lanes(heads, dz)
        mine[span, 3 * width :] = last.astype(bf16)
        tails[0, :, span] = last.T[:16].astype(bf16)

    def unit_pairs(i):
        return [
            (units[i, :, h * dim : (h + 1) * dim], scales[:, i * heads + h : i * heads + h + 1])
            for h in range(heads)
        ]

    halves = [slice(0, rows // 2), slice(rows // 2, rows)]

    def input_part(index, rows):
        span = pl.ds(pl.multiple_of(index * width, width), width)
        total = dot(mine[rows, 3 * width :], wb[:, span])
        for i in range(3):
            total = total + dot(mine[rows, i * width : (i + 1) * width], w[i, span, :], (1, 1))
        return total

    side = 1 - 2 * (group // 2)
    edge = (group == 0) | (group == groups - 1)
    rim = jnp.where(edge, 1, 0)
    targets = [
        group + side * (1 + 2 * rim),
        group + side * (3 * rim - 1),
        group + side * (2 - rim),
    ]

    def landing(n, h):
        slot = jnp.where(edge, groups, group) if n == 0 else group
        device = group + side if n == 0 else targets[n]
        return remote(
            piece.at[n, halves[h]], landed.at[slot, halves[h]],
            z_send.at[n, h], z_recv.at[slot, h], {"head": device},
        )

    def first_piece(h):
        piece[0, halves[h]] = input_part(targets[0], halves[h]).astype(bf16)
        landing(0, h).start()

    gradients(
        heads, dim, unit_pairs(0), unit_pairs(1), z, g, mid, unit_state, put, strength,
        valued, lambda: first_piece(0),
    )
    for key in ((0, 0), (1, 0), (0, 1), (1, 1), (0, 3)):
        send(key)
    first_piece(1)
    piece[1] = input_part(targets[1], slice(0, rows)).astype(bf16)
    for h in range(2):
        landing(1, h).start()
    piece[2] = input_part(targets[2], slice(0, rows)).astype(bf16)

    @pl.when(edge)
    def _():
        for h in range(2):
            landing(2, h).start()

    own[...] = input_part(group, slice(0, rows))

    def arrived(slot, h):
        remote(
            piece.at[0, halves[h]], landed.at[slot, halves[h]],
            z_send.at[0, h], z_recv.at[slot, h], {"head": targets[0]},
        ).wait_recv()
        return landed[slot, halves[h]].astype(f32)

    def pass_on(h):
        @pl.when(jnp.logical_not(edge))
        def _():
            piece[2, halves[h]] = (piece[2, halves[h]].astype(f32) + arrived(groups, h)).astype(bf16)
            landing(2, h).start()

    order = [(0, 2), (1, 2), (0, 0), (1, 0), (0, 1), (1, 1), (0, 3)]
    trades = {
        (a, i): remote(
            part_out.at[a, i], part_in.at[a, i], part_send.at[a, i], part_recv.at[a, i], partners[a]
        )
        for a in range(2)
        for i in range(3)
    }
    tail_trade = remote(tail_out, tail_in, part_send.at[0, 3], part_recv.at[0, 3], partners[0])

    def process(a, i):
        spreads[a, i][1].wait_recv()
        spreads[a, i][2].wait_recv()
        if i < 3:
            value = dot(cols_t[a], blocks[a, i])
            part_out[a, i] = value[part:].astype(bf16)
            trades[a, i].start()
            grads[i, :, a * half * dim : (a + 1) * half * dim] = value[:part]
        else:
            sums = [dot(tails[0], own_columns(0, b)) for b in range(2)]
            for s in range(1, 4):
                sums = [t + dot(tails[s], cols[0, s, b]) for b, t in enumerate(sums)]
            held = jnp.sum(tails[...].astype(f32), 0)
            held = jnp.sum(held, -1, keepdims=True)
            row, col = iotas(16, part)
            held = jnp.sum(jnp.where(row == col, held, 0.0), 0, keepdims=True)
            row = lax.broadcasted_iota(jnp.int32, (16, part), 0)
            tail_out[...] = jnp.where(row == 8, held, sums[1])
            tail_trade.start()
            tail_ref[...] = jnp.where(row == 8, held, sums[0])

    for key in later:
        tokens[key].wait_recv()
        turn_block(*key)
    for n, key in enumerate(order):
        spreads[key][0].wait_recv()
        spreads[key][2].start()
        if n > 0:
            process(*order[n - 1])
        if n == 1:
            pass_on(0)
        if n == 3:
            pass_on(1)

    process(*order[-1])
    saves = []

    def keep(source, target):
        copy = pltpu.make_async_copy(source, target, save.at[len(saves)])
        copy.start()
        saves.append(copy)

    targets_hbm = (gq_hbm, gk_hbm, gv_hbm)
    for a, i in order:
        if i < 3:
            trades[a, i].wait_recv()
            span = slice(a * half * dim, (a + 1) * half * dim)
            grads[i, :, span] = grads[i, :, span] + part_in[a, i].astype(f32)
            keep(grads.at[i, :, span], targets_hbm[i].at[:, span])
        else:
            tail_trade.wait_recv()
            tail_ref[...] = tail_ref[...] + tail_in[...]
            keep(tail_ref, tail_hbm)

    for h in range(2):

        @pl.when(jnp.logical_not(edge))
        def _():
            own[halves[h]] = own[halves[h]] + arrived(group - side, h)

        total = own[halves[h]] + arrived(group + side, h) + arrived(group + 2 * side, h)
        dx_ref[halves[h]] = total.astype(bf16)
        keep(dx_ref.at[halves[h]], dx_hbm.at[halves[h]])

    share.wait_send()

    @pl.when(upper == taken)
    def _():
        for copy in up:
            copy.wait_send()

    for n in range(3):
        for h in range(2):
            landing(n, h).wait_send()
    for copy in sibling + list(tokens.values()) + over + forward + [tail_trade] + list(trades.values()):
        copy.wait_send()
    for copies in spreads.values():
        for copy in copies:
            copy.wait_send()
    for copy in saves:
        copy.wait()


def place_kernel(count, heads, *refs):
    sources, outs = refs[: count + 1], refs[count + 1 : 2 * count + 3]
    held, (strength, bias, sems) = refs[2 * count + 3 : -3], refs[-3:]
    fetch, store = [], []
    for i in range(count):
        size = sources[i].shape[0] // 2
        for n in range(2):
            span = pl.ds(n * size, size)
            j = 2 * i + n
            fetch.append(
                pltpu.make_async_copy(sources[i].at[span], held[i].at[span], sems.at[0, j])
            )
            store.append(pltpu.make_async_copy(held[i].at[span], outs[i].at[span], sems.at[1, j]))
    small = pltpu.make_async_copy(sources[count], held[count], sems.at[0, 2 * count])
    small.start()
    for copy in fetch:
        copy.start()
    small.wait()
    strength[...] = held[count][:heads, :]
    bias[...] = held[count][8:9, :heads] + held[count][8:9, heads : 2 * heads]
    store.append(pltpu.make_async_copy(strength, outs[count], sems.at[1, 2 * count]))
    store.append(pltpu.make_async_copy(bias, outs[count + 1], sems.at[1, 2 * count + 1]))
    for copy in store[-2:]:
        copy.start()
    for j in range(2 * count):
        fetch[j].wait()
        store[j].start()
    for copy in store:
        copy.wait()


def place(arrays, tail, heads):
    count = len(arrays)
    hbm = pl.BlockSpec(memory_space=pltpu.HBM)
    return pl.pallas_call(
        functools.partial(place_kernel, count, heads),
        out_shape=tuple(jax.ShapeDtypeStruct(a.shape, a.dtype) for a in arrays)
        + (
            jax.ShapeDtypeStruct((heads, tail.shape[1]), tail.dtype),
            jax.ShapeDtypeStruct((1, heads), tail.dtype),
        ),
        in_specs=[hbm] * (count + 1),
        out_specs=(hbm,) * (count + 2),
        scratch_shapes=[pltpu.VMEM(a.shape, a.dtype) for a in (*arrays, tail)]
        + [
            pltpu.VMEM((heads, tail.shape[1]), tail.dtype),
            pltpu.VMEM((1, heads), tail.dtype),
            pltpu.SemaphoreType.DMA((2, 2 * count + 2)),
        ],
        compiler_params=pltpu.CompilerParams(vmem_limit_bytes=60 * 1024 * 1024),
        name="place",
    )(*arrays, tail)


def whole_layer(tokens, weights, w_beta, b_beta, d_out):
    shards, groups = lax.axis_size("seq"), lax.axis_size("head")
    rows, features = tokens.shape
    heads = w_beta.shape[1]
    width = weights[0].shape[1]
    dim = width // heads
    half = heads // 2
    part = features // shards
    f32, bf16 = jnp.float32, jnp.bfloat16
    hbm = pl.BlockSpec(memory_space=pltpu.HBM)
    square = jax.ShapeDtypeStruct((part, width), f32)
    dma = pltpu.SemaphoreType.DMA
    outs = pl.pallas_call(
        functools.partial(layer_kernel, groups, heads, dim),
        out_shape=(
            jax.ShapeDtypeStruct((rows, features // groups), tokens.dtype),
            square,
            square,
            square,
            jax.ShapeDtypeStruct((16, part), f32),
        ),
        in_specs=[hbm] * 7,
        out_specs=(hbm,) * 5,
        scratch_shapes=[
            pltpu.VMEM((rows, features // groups), bf16),
            pltpu.VMEM((3, part, width), f32),
            pltpu.VMEM((16, part), f32),
            pltpu.VMEM((rows, features), bf16),
            pltpu.VMEM((3, features, width), bf16),
            pltpu.VMEM((LANES, features), bf16),
            pltpu.VMEM((rows, width), bf16),
            pltpu.VMEM((heads, features), bf16),
            pltpu.VMEM((1, heads), f32),
            pltpu.VMEM((3, rows, width), f32),
            pltpu.VMEM((2, rows, width), f32),
            pltpu.VMEM((rows, LANES), f32),
            pltpu.VMEM((rows, LANES), f32),
            pltpu.VMEM((heads, rows, 4 * dim), f32),
            pltpu.VMEM((2, 2 * heads, 2, dim, dim), bf16),
            pltpu.VMEM((2, half, dim, dim), bf16),
            pltpu.VMEM((2, heads, dim, dim), bf16),
            pltpu.VMEM((half, dim, dim), bf16),
            pltpu.VMEM((heads, dim, dim), bf16),
            pltpu.VMEM((2 * heads, dim, dim), f32),
            pltpu.VMEM((2, 4, 2, rows, part), bf16),
            pltpu.VMEM((2, 2 * part, 4 * rows), bf16),
            pltpu.VMEM((rows, 3 * width + LANES), bf16),
            pltpu.VMEM((2, 3, 4 * rows, width // 2), bf16),
            pltpu.VMEM((4, 16, rows), bf16),
            pltpu.VMEM((2, 3, part, width // 2), bf16),
            pltpu.VMEM((2, 3, part, width // 2), bf16),
            pltpu.VMEM((16, part), f32),
            pltpu.VMEM((16, part), f32),
            pltpu.VMEM((rows, features // groups), f32),
            pltpu.VMEM((3, rows, features // groups), bf16),
            pltpu.VMEM((groups + 1, rows, features // groups), bf16),
            dma((7,)),
            dma((11,)),
            dma((11,)),
            dma((4,)),
            dma((4,)),
            dma((2,)),
            dma((2,)),
            dma((2,)),
            dma((2,)),
            dma((3,)),
            dma,
            dma,
            dma((2, 4)),
            dma((2, 4)),
            dma((2, 4)),
            dma((2, 4)),
            dma((2, 4)),
            dma((2, 4)),
            dma((2, 4)),
            dma((2, 4)),
            dma((3, 2)),
            dma((groups + 1, 2)),
            dma((9,)),
        ],
        compiler_params=pltpu.CompilerParams(
            vmem_limit_bytes=60 * 1024 * 1024, collective_id=1, has_side_effects=True
        ),
        name="layer",
    )(tokens, *weights, d_out, w_beta.T, b_beta.reshape(1, heads))
    d_x, grad_q, grad_k, grad_v, tail, bias = place(outs[:4], outs[4], heads)
    return d_x, grad_q, grad_k, grad_v, tail.T, bias.reshape(heads)


def per_device(tokens, w_query, w_key, w_value, w_beta, b_beta, d_out):
    token_count, features = tokens.shape
    heads = w_beta.shape[1]
    width = w_query.shape[1]
    dim = width // heads
    f32 = jnp.float32
    shards, groups = lax.axis_size("seq"), lax.axis_size("head")
    weights = (w_query, w_key, w_value)
    fits = heads % 2 == 0 and 2 * heads <= 8 and width * groups == features and dim == LANES
    if shards == 8 and groups == 4 and fits and features // shards == token_count:
        return whole_layer(tokens, weights, w_beta, b_beta, d_out)
    q, k, v = (jnp.dot(tokens, w, preferred_element_type=f32) for w in weights)
    w_last = jnp.pad(w_beta, ((0, 0), (0, LANES - heads)))
    z = jnp.dot(tokens, w_last, preferred_element_type=f32) + jnp.pad(b_beta, (0, LANES - heads))
    params = pltpu.CompilerParams(vmem_limit_bytes=60 * 1024 * 1024)
    columns = lax.all_to_all(tokens, "seq", split_axis=1, concat_axis=0, tiled=True)
    maps, mid = pl.pallas_call(
        functools.partial(summary_kernel, heads, dim),
        out_shape=(
            jax.ShapeDtypeStruct((2 * heads, 2, dim, dim), jnp.bfloat16),
            jax.ShapeDtypeStruct((heads, token_count, 4 * dim), f32),
        ),
        compiler_params=params,
        name="summary",
    )(q, k, v, z, d_out)
    states = gathered_states(maps, heads)
    grads = pl.pallas_call(
        functools.partial(gradient_kernel, heads, dim),
        out_shape=jax.ShapeDtypeStruct((token_count, 3 * width + LANES), jnp.bfloat16),
        compiler_params=params,
        name="gradient",
    )(q, k, z, d_out, mid, states)
    whole = lax.all_gather(grads, "seq", axis=0, tiled=True)
    partial = jnp.dot(grads[:, 3 * width : 3 * width + heads], w_beta.T, preferred_element_type=f32)
    for i, w in enumerate(weights):
        partial = partial + jnp.dot(
            grads[:, i * width : (i + 1) * width], w.T, preferred_element_type=f32
        )
    d_x = lax.psum_scatter(
        partial.astype(jnp.bfloat16), "head", scatter_dimension=1, tiled=True
    )

    def weight_grad(block):
        return lax.dot_general(
            columns, block, (((0,), (0,)), ((), ())), preferred_element_type=f32
        )

    found = [weight_grad(whole[:, i * width : (i + 1) * width]) for i in range(3)]
    tail = whole[:, 3 * width :]
    grad_wbeta = weight_grad(tail)[:, :heads]
    sums = jnp.sum(tail.astype(f32), 0)
    return (d_x, *found, grad_wbeta, sums[:heads] + sums[heads : 2 * heads])


def solution(mesh):
    in_specs = (
        P("seq", None),
        P(None, "head"),
        P(None, "head"),
        P(None, "head"),
        P(None, "head"),
        P("head"),
        P("seq", "head"),
    )
    out_specs = (
        P("seq", "head"),
        P("seq", "head"),
        P("seq", "head"),
        P("seq", "head"),
        P("seq", "head"),
        P("head"),
    )
    return jax.shard_map(
        per_device, mesh=mesh, in_specs=in_specs, out_specs=out_specs, check_vma=False
    )
```

```python
import functools

import jax
import jax.numpy as jnp
from jax import lax
from jax.experimental import pallas as pl
from jax.experimental.pallas import tpu as pltpu
from jax.sharding import PartitionSpec as P

epsilon = 1e-06
LANES = 128
MESH = pl.DeviceIdType.MESH
highest = lax.Precision.HIGHEST


def split(a):
    high = a.astype(jnp.bfloat16)
    return high, (a - high.astype(jnp.float32)).astype(jnp.bfloat16)


def only(a):
    return a.astype(jnp.bfloat16), None


def mm(a, b, dims=(1, 0)):
    numbers = (((dims[0],), (dims[1],)), ((), ()))
    dot = functools.partial(
        lax.dot_general, dimension_numbers=numbers, preferred_element_type=jnp.float32
    )
    total = dot(a[0], b[0])
    if b[1] is not None:
        total = total + dot(a[0], b[1])
    if a[1] is not None:
        total = total + dot(a[1], b[0])
    return total


def square_mm(a, b):
    size = a[0].shape[0]
    left = jnp.concatenate(a, 1)
    right = jnp.concatenate(
        [jnp.concatenate(b, 1), jnp.concatenate([b[0], jnp.zeros_like(b[0])], 1)], 0
    )
    both = lax.dot_general(left, right, (((1,), (0,)), ((), ())), preferred_element_type=jnp.float32)
    return both[:, :size] + both[:, size:]


def tight_mm(a, b, dims=(1, 0)):
    inner, outer = dims[1], 1 - dims[1]
    size = b[0].shape[outer]
    left = a[0] if a[1] is None else jnp.concatenate(a, dims[0])
    right = b[0] if b[1] is None else jnp.concatenate(b, outer)
    if a[1] is not None:
        again = b[0]
        if b[1] is not None:
            again = jnp.concatenate([b[0], jnp.zeros_like(b[0])], outer)
        right = jnp.concatenate([right, again], inner)
    both = lax.dot_general(
        left, right, (((dims[0],), (dims[1],)), ((), ())), preferred_element_type=jnp.float32
    )
    return both if b[1] is None else both[:, :size] + both[:, size:]


def wide_mm(a, b, dims=(1, 0)):
    numbers = (((dims[0],), (dims[1],)), ((), ()))
    size = b[0].shape[1 - dims[1]]
    both = lax.dot_general(
        a[0], jnp.concatenate(b, 1 - dims[1]), numbers, preferred_element_type=jnp.float32
    )
    total = both[:, :size] + both[:, size:]
    if a[1] is not None:
        total = total + lax.dot_general(a[1], b[0], numbers, preferred_element_type=jnp.float32)
    return total


def deep_mm(a, b):
    numbers = (((1,), (1,)), ((), ()))
    dot = functools.partial(
        lax.dot_general, dimension_numbers=numbers, preferred_element_type=jnp.float32
    )
    return dot(jnp.concatenate(a, 1), jnp.concatenate([b[0], b[0]], 1)) + dot(a[0], b[1])


def iotas(rows, cols):
    return (
        lax.broadcasted_iota(jnp.int32, (rows, cols), 0),
        lax.broadcasted_iota(jnp.int32, (rows, cols), 1),
    )


def invert_unit_lower(systems, fillers=()):
    fillers = list(fillers)
    size = systems[0].shape[0]
    base = min(size, LANES)
    row, col = iotas(base, base)
    eye = jnp.where(row == col, 1.0, 0.0).astype(jnp.float32)

    def step_mask(s):
        return (row // (2 * s) == col // (2 * s)) & (row % (2 * s) >= s) & (col % (2 * s) < s)

    count = size // base
    diagonals = [
        n[i * base : (i + 1) * base, i * base : (i + 1) * base] for n in systems for i in range(count)
    ]
    inverses = [eye - jnp.where(step_mask(1), n, 0.0) for n in diagonals]
    pairs = [split(n) for n in diagonals]
    s = 2
    while s < base:
        mask = jnp.where(step_mask(s), 1.0, 0.0).astype(jnp.bfloat16)
        parts = [split(x) for x in inverses]
        inner = [square_mm((mask * n[0], mask * n[1]), x) for n, x in zip(pairs, parts)]
        if fillers:
            fillers.pop(0)()
        outer = [square_mm(x, split(y)) for x, y in zip(parts, inner)]
        inverses = [x - y for x, y in zip(inverses, outer)]
        s *= 2
    for filler in fillers:
        filler()
    grouped = [inverses[i * count : (i + 1) * count] for i in range(len(systems))]
    width = base
    while width < size:
        merged = []
        for n, blocks in zip(systems, grouped):
            joined = []
            for i in range(0, len(blocks), 2):
                first, second = blocks[i], blocks[i + 1]
                low = n[(i + 1) * width : (i + 2) * width, i * width : (i + 1) * width]
                corner = square_mm(split(second), split(square_mm(split(low), split(first))))
                joined.append(
                    jnp.concatenate(
                        [
                            jnp.concatenate([first, jnp.zeros_like(first)], 1),
                            jnp.concatenate([-corner, second], 1),
                        ],
                        0,
                    )
                )
            merged.append(joined)
        grouped = merged
        width *= 2
    return [g[0] for g in grouped]


def normalise(raw):
    scale = lax.rsqrt(jnp.sum(raw * raw, -1, keepdims=True) + epsilon)
    return raw * scale, scale


def dot(a, b, dims=(1, 0)):
    return lax.dot_general(
        a, b, (((dims[0],), (dims[1],)), ((), ())), preferred_element_type=jnp.float32
    )


def summarise(heads, dim, q_ref, k_ref, v_ref, z_ref, g_ref, put_map, fillers=(), put_unit=None):
    count = q_ref.shape[0]
    row, col = iotas(count, count)
    strict, inclusive = row > col, row >= col
    every = range(heads)
    cols = [slice(h * dim, (h + 1) * dim) for h in every]
    beta_all = 2.0 * jax.nn.sigmoid(z_ref[:, :heads])
    beta = [beta_all[:, h : h + 1] for h in every]
    kp = [normalise(k_ref[:, c]) for c in cols]
    kn = [x[0] for x in kp]
    ks = [split(x) for x in kn]
    gs = [(g_ref[:, c], None) for c in cols]
    gram = [jnp.where(strict, deep_mm(x, x), 0.0) for x in ks]
    systems = [b * n for b, n in zip(beta, gram)]
    late = {}

    def score():
        qp = [normalise(q_ref[:, c]) for c in cols]
        late["qs"] = [split(x[0]) for x in qp]
        if put_unit is not None:
            put_unit(qp, kp)
        late["scores"] = [
            split(jnp.where(inclusive, deep_mm(a, b), 0.0)) for a, b in zip(late["qs"], ks)
        ]

    def pull():
        late["back"] = [mm(p, g, (0, 0)) for p, g in zip(late["scores"], gs)]
        late["direct"] = [wide_mm(g, q, (0, 0)) for g, q in zip(gs, late["qs"])]

    fillers = list(fillers) + [score, pull]
    inverse = [split(t) for t in invert_unit_lower(systems, fillers)]
    gram = [split(n) for n in gram]
    back, direct = late["back"], late["direct"]
    forth_in = [jnp.concatenate([v_ref[:, c], k], 1) for c, k in zip(cols, kn)]
    forth = [split(mm(t, split(b * x))) for t, b, x in zip(inverse, beta, forth_in)]
    adjoint = [
        mm(t, split(jnp.concatenate([p, k], 1)), (0, 0)) for t, p, k in zip(inverse, back, kn)
    ]
    ends = [wide_mm(f, k, (0, 0)) for f, k in zip(forth, ks)]
    tails = [wide_mm(split(a), split(b * k), (0, 0)) for a, b, k in zip(adjoint, beta, kn)]
    for h in every:
        put_map(h, ends[h][dim:], ends[h][:dim])
        put_map(heads + h, tails[h][dim:], direct[h] - tails[h][:dim])

    def put_mid(mid_ref):
        for h in every:
            mid_ref[h, :, : 2 * dim] = forth_in[h] - mm(gram[h], forth[h])
            mid_ref[h, :, 2 * dim :] = adjoint[h]

    return put_mid


def summary_kernel(heads, dim, q_ref, k_ref, v_ref, z_ref, g_ref, map_ref, mid_ref):
    def put_map(unit, factor, offset):
        map_ref[unit, 0] = factor.astype(map_ref.dtype)
        map_ref[unit, 1] = offset.astype(map_ref.dtype)

    summarise(heads, dim, q_ref, k_ref, v_ref, z_ref, g_ref, put_map)(mid_ref)


def gradients(heads, dim, qp, kp, z_ref, g_ref, mid_ref, state, put, strength, valued, between):
    every = range(heads)
    count = z_ref.shape[0] // 2
    halves = (slice(0, count), slice(count, 2 * count))
    row, col = iotas(count, count)
    strict, inclusive = row > col, row >= col
    beta_all = 2.0 * jax.nn.sigmoid(z_ref[:, :heads])
    beta = [beta_all[:, h : h + 1] for h in every]
    ss = [(state(h), None) for h in every]
    ds = [(state(heads + h), None) for h in every]
    dx = [
        mid_ref[h, :, 2 * dim : 3 * dim] + tight_mm(split(mid_ref[h, :, 3 * dim :]), d, (1, 1))
        for h, d in zip(every, ds)
    ]
    dv = [b * x for b, x in zip(beta, dx)]
    for h in every:
        put(2, h, slice(0, 2 * count), dv[h].astype(jnp.bfloat16))
    valued()

    def pick(x, rows):
        return tuple(None if y is None else y[rows] for y in x)

    def part(rows):
        ks = [split(x[0][rows]) for x in kp]
        qs = [split(x[0][rows]) for x in qp]
        gs = [(g_ref[rows, h * dim : (h + 1) * dim], None) for h in every]
        plain = [
            mid_ref[h, rows, :dim] - tight_mm(split(mid_ref[h, rows, dim : 2 * dim]), s, (1, 1))
            for h, s in zip(every, ss)
        ]
        us = [split(b[rows] * x) for b, x in zip(beta, plain)]
        dz = [
            jnp.sum(x[rows] * p, -1, keepdims=True) * b[rows] * (1.0 - 0.5 * b[rows])
            for x, p, b in zip(dx, plain, beta)
        ]
        return ks, qs, gs, us, dz

    def through(grad, pair, rows):
        unit, scale = pair[0][rows], pair[1][rows]
        return scale * (grad - unit * jnp.sum(unit * grad, -1, keepdims=True))

    def finish(rows, dqn, dkn):
        for h in every:
            put(0, h, rows, through(dqn[h], qp[h], rows).astype(jnp.bfloat16))
            put(1, h, rows, through(dkn[h], kp[h], rows).astype(jnp.bfloat16))

    def below(a, b, mask):
        found = [tight_mm(x, y, (1, 1)) for x, y in zip(a, b)]
        return found if mask is None else [jnp.where(mask, x, 0.0) for x in found]

    dvs = [[split(x[rows]) for x in dv] for rows in halves]
    k0, q0, g0, u0, dz = part(halves[0])
    strength(halves[0], dz)
    k1 = [split(x[0][halves[1]]) for x in kp]
    q1 = [split(x[0][halves[1]]) for x in qp]
    g1 = [(g_ref[halves[1], h * dim : (h + 1) * dim], None) for h in every]
    inner0 = [split(x) for x in below(g0, u0, inclusive)]
    pair0 = below(dvs[0], u0, strict)
    inner1 = [split(x) for x in below(g1, u0, None)]
    pair1 = below(dvs[1], u0, None)
    dqn = [tight_mm(g, s) + tight_mm(i, k) for g, s, i, k in zip(g0, ss, inner0, k0)]
    dkn = [
        tight_mm(i, q, (0, 0)) + tight_mm(j, r, (0, 0)) + tight_mm(u, d) - tight_mm(x, s)
        - tight_mm(split(e + e.T), k) - tight_mm(split(f.T), l)
        for i, q, j, r, u, d, x, s, e, k, f, l in zip(
            inner0, q0, inner1, q1, u0, ds, dvs[0], ss, pair0, k0, pair1, k1
        )
    ]
    finish(halves[0], dqn, dkn)
    between()
    k1, q1, g1, u1, dz = part(halves[1])
    strength(halves[1], dz)
    inner2 = [split(x) for x in below(g1, u1, inclusive)]
    pair2 = below(dvs[1], u1, strict)
    dqn = [
        tight_mm(g, s) + tight_mm(j, k) + tight_mm(i, l)
        for g, s, j, k, i, l in zip(g1, ss, inner1, k0, inner2, k1)
    ]
    dkn = [
        tight_mm(i, q, (0, 0)) + tight_mm(u, d) - tight_mm(x, s) - tight_mm(split(f), k) - tight_mm(split(e + e.T), l)
        for i, q, u, d, x, s, f, k, e, l in zip(
            inner2, q1, u1, ds, dvs[1], ss, pair1, k0, pair2, k1
        )
    ]
    finish(halves[1], dqn, dkn)


def strength_lanes(heads, dz):
    lane = lax.broadcasted_iota(jnp.int32, (dz[0].shape[0], LANES), 1)
    last = jnp.zeros((dz[0].shape[0], LANES), jnp.float32)
    for h in range(heads):
        high, low = split(dz[h])
        last = jnp.where(lane == h, high.astype(jnp.float32), last)
        last = jnp.where(lane == heads + h, low.astype(jnp.float32), last)
    return last


def gradient_kernel(heads, dim, q_ref, k_ref, z_ref, g_ref, mid_ref, state_ref, out_ref):
    width = heads * dim

    def put(i, h, rows, value):
        out_ref[rows, i * width + h * dim : i * width + (h + 1) * dim] = value

    def state(unit):
        return state_ref[unit]

    def strength(rows, dz):
        out_ref[rows, 3 * width :] = strength_lanes(heads, dz).astype(jnp.bfloat16)

    cols = [slice(h * dim, (h + 1) * dim) for h in range(heads)]
    qp = [normalise(q_ref[:, c]) for c in cols]
    kp = [normalise(k_ref[:, c]) for c in cols]
    gradients(
        heads, dim, qp, kp, z_ref, g_ref, mid_ref, state, put, strength,
        lambda: None, lambda: None,
    )


def gathered_states(maps, heads):
    count = lax.axis_size("seq")
    place = lax.axis_index("seq")
    gathered = lax.all_gather(maps, "seq").astype(jnp.float32)

    def walk(steps, pick, rows):
        def one(lap, state):
            pair = lax.dynamic_index_in_dim(gathered, pick(lap), 0, False)[rows]
            moved = jnp.einsum("hij,hjk->hik", state, pair[:, 0], precision=highest)
            return state - moved + pair[:, 1]

        return lax.fori_loop(0, steps, one, jnp.zeros((heads,) + maps.shape[2:], jnp.float32))

    first = walk(place, lambda lap: lap, slice(0, heads))
    second = walk(count - 1 - place, lambda lap: count - 1 - lap, slice(heads, None))
    return jnp.concatenate([first, second]).astype(maps.dtype)


def layer_kernel(
    groups, heads, dim,
    x_hbm, wq_hbm, wk_hbm, wv_hbm, g_hbm, wb_hbm, b_hbm,
    dx_hbm, gq_hbm, gk_hbm, gv_hbm, tail_hbm,
    dx_ref, grads, tail_ref, x, w, wb, g, wb_ref, b_ref, qkv, units, scales, z, mid, maps, x_out, x_in, y_out, y_in, state,
    cols, cols_t, mine, blocks, tails, part_out, part_in, tail_out, tail_in,
    own, piece, landed,
    load, tok_send, tok_recv, map_send, map_recv, x_send, x_recv, f_send, f_recv,
    y_send, y_recv, s_recv, far_send, far_recv, sib_send, sib_recv, fwd_send, fwd_recv,
    part_send, part_recv, z_send, z_recv, save,
):
    me = lax.axis_index("seq")
    group = lax.axis_index("head")
    core, across, upper = me % 2, (me // 2) % 2, me // 4
    rows, width = g.shape
    part = cols.shape[-1]
    half = heads // 2
    f32, bf16 = jnp.float32, jnp.bfloat16

    def seq(o):
        index = me
        for bit in (1, 2, 4):
            if o & bit:
                index = index + bit - 2 * bit * ((me // bit) % 2)
        return index

    def remote(source, target, send, recv, device):
        return pltpu.make_async_remote_copy(
            src_ref=source,
            dst_ref=target,
            send_sem=send,
            recv_sem=recv,
            device_id=device if isinstance(device, dict) else {"seq": seq(device)},
            device_id_type=MESH,
        )

    pairs = (
        (x_hbm, x), (wk_hbm, w.at[1]), (wb_hbm, wb_ref), (b_hbm, b_ref), (g_hbm, g),
        (wq_hbm, w.at[0]), (wv_hbm, w.at[2]),
    )
    loads = [pltpu.make_async_copy(s, t, load.at[i]) for i, (s, t) in enumerate(pairs)]
    for copy in loads:
        copy.start()
    barrier = pltpu.get_barrier_semaphore()
    others = [{"seq": seq(o)} for o in range(1, 8)]
    others += [{"head": lax.rem(group + r, groups)} for r in range(1, groups)]
    for peer in others:
        pl.semaphore_signal(barrier, inc=1, device_id=peer, device_id_type=MESH)
    wb[...] = jnp.zeros_like(wb)
    pl.semaphore_wait(barrier, len(others))

    fars, partners = (2, 4), (4, 2)
    slots = [(0, 1, far, far ^ 1) for far in fars]

    def columns(index):
        return pl.ds(pl.multiple_of(index * part, part), part)

    tokens, later = {}, [(0, 3, 1), (1, 3, 1)]
    for s in (2, 3, 1):
        for b in range(2):
            for a in range(2):
                if (a, s, b) != (1, 1, 0):
                    owner = seq(slots[a][s] ^ (partners[a] if b else 0))
                    i = len(tokens)
                    tokens[a, s, b] = remote(
                        x_hbm.at[:, columns(owner)], cols.at[a, s, b],
                        tok_send.at[i], tok_recv.at[i], slots[a][s],
                    )
                    if (a, s, b) not in later:
                        tokens[a, s, b].start()

    loads[0].wait()
    loads[1].wait()
    qkv[1] = dot(x[...], w[1])
    for copy in loads[2:]:
        copy.wait()
    wb[pl.ds(0, heads), :] = wb_ref[...]
    z[:, :heads] = dot(x[...], wb[:16], (1, 1))[:, :heads] + b_ref[...]
    def put_map(unit, factor, offset):
        maps[core, unit, 0] = factor.astype(bf16)
        maps[core, unit, 1] = offset.astype(bf16)

    def project(i, n):
        def run():
            span = slice(n * width // 2, (n + 1) * width // 2)
            qkv[i, :, span] = dot(x[...], w[i, :, span])

        return run

    def put_unit(qp, kp):
        for i, pairs in enumerate((qp, kp)):
            for h, (unit, scale) in enumerate(pairs):
                units[i, :, h * dim : (h + 1) * dim] = unit
                scales[:, i * heads + h : i * heads + h + 1] = scale

    fillers = [project(i, n) for i in (0, 2) for n in range(2)]
    put_mid = summarise(
        heads, dim, qkv.at[0], qkv.at[1], qkv.at[2], z, g, put_map, fillers, put_unit
    )
    passed, taken = across, 1 - across
    kept, other = pl.ds(core * half, half), pl.ds((1 - core) * half, half)
    urgent = [
        (way * heads + n * half, j)
        for j, (way, n) in enumerate(
            [(passed, 1 - core), (taken, 1 - core), (passed, core), (taken, core)]
        )
    ]
    sibling = [
        remote(
            maps.at[core, pl.ds(unit, half)], maps.at[core, pl.ds(unit, half)],
            map_send.at[j], map_recv.at[j], 1,
        )
        for unit, j in urgent
    ]
    arriving = [
        remote(
            maps.at[1 - core, pl.ds(way * heads + n * half, half)],
            maps.at[1 - core, pl.ds(way * heads + n * half, half)],
            map_send.at[j], map_recv.at[j], 1,
        )
        for j, (way, n) in enumerate([(passed, core), (taken, core), (passed, 1 - core), (taken, 1 - core)])
    ]
    for copy in sibling:
        copy.start()
    put_mid(mid)
    arriving[0].wait_recv()

    def chip_total(way, n):
        unit = way * heads + core * half + n
        first = jnp.concatenate([maps[way, unit, 0], maps[way, unit, 1]], 0)
        factor = maps[1 - way, unit, 0]
        moved = dot(first, factor)
        both = first.astype(f32) - moved
        return both[:dim] + factor.astype(f32), both[dim:] + maps[1 - way, unit, 1].astype(f32)

    for n in range(half):
        factor, offset = chip_total(passed, n)
        x_out[0, n] = offset.astype(bf16)
        x_out[1, n] = factor.astype(bf16)
    over = [remote(x_out.at[j], x_in.at[j, kept], x_send.at[j], x_recv.at[j], 2) for j in range(2)]
    for copy in over:
        copy.start()
    arriving[1].wait_recv()
    totals = [chip_total(taken, n) for n in range(half)]
    forward = [
        remote(x_in.at[j, kept], x_in.at[j, kept], f_send.at[j], f_recv.at[j], 1) for j in range(2)
    ]

    def own_columns(a, b):
        return x[:, columns(seq(partners[a]) if b else me)]

    def turn_block(a, s, b):
        if s == 0:
            block = own_columns(a, b)
        else:
            block = cols[0, 1, 0] if (a, s, b) == (1, 1, 0) else cols[a, s, b]
        cols_t[a, b * part : (b + 1) * part, s * rows : (s + 1) * rows] = block.T

    def turn(a):
        for s in range(4):
            for b in range(2):
                if (a, s, b) not in later:
                    turn_block(a, s, b)

    for key, copy in tokens.items():
        if key[0] == 0 and key not in later:
            copy.wait_recv()
    turn(0)
    over[0].wait_recv()
    for n, (factor, offset) in enumerate(totals):
        entering = x_in[0, core * half + n]
        y_out[n] = (entering.astype(f32) - tight_mm((entering, None), split(factor)) + offset).astype(bf16)
    up = [remote(y_out, y_in.at[kept], y_send.at[j], y_recv, 4 + 2 * j) for j in range(2)]
    share = remote(y_in.at[kept], y_in.at[kept], y_send.at[2], s_recv, 1)

    @pl.when(upper == taken)
    def _():
        for copy in up:
            copy.start()

    forward[0].start()
    over[1].wait_recv()
    forward[1].start()
    for key in later:
        tokens[key].start()
    for key, copy in tokens.items():
        if key[0] == 1 and key not in later:
            copy.wait_recv()
    turn(1)
    for copy in forward + arriving[2:]:
        copy.wait_recv()
    state[...] = jnp.zeros_like(state)
    for h in range(heads):
        state[taken * heads + h] = x_in[0, h].astype(f32)
    bridge = []
    lead, inside = 1 - upper, 1 - core
    for h in range(heads):
        unit = inside * heads + h
        factor = maps[inside, unit, 0]
        before = state[unit]
        state[unit] = before - tight_mm(split(before), (factor, None)) + maps[inside, unit, 1].astype(f32)
        first = jnp.where(taken == lead, x_in[1, h].astype(f32), 0.0).astype(bf16)
        second = jnp.where(inside == lead, factor.astype(f32), 0.0).astype(bf16)
        bridge.append(split(first.astype(f32) + second.astype(f32) - dot(first, second)))
    up[0].wait_recv()
    share.start()
    share.wait_recv()
    for h in range(heads):
        unit = lead * heads + h
        state[unit] = state[unit] + (y_in[h].astype(f32) - tight_mm((y_in[h], None), bridge[h]))

    def put(i, h, span, value):
        a, n = h // half, h % half
        mine[span, i * width + h * dim : i * width + (h + 1) * dim] = value
        blocks[a, i, span, n * dim : (n + 1) * dim] = value

    def spread(a, i):
        if i < 3:
            slot = [blocks.at[a, i, pl.ds(s * rows, rows)] for s in range(4)]
        else:
            slot = [tails.at[s] for s in range(4)]
        return (
            remote(slot[0], slot[2], far_send.at[a, i], far_recv.at[a, i], fars[a]),
            remote(slot[0], slot[1], sib_send.at[a, i], sib_recv.at[a, i], 1),
            remote(slot[2], slot[3], fwd_send.at[a, i], fwd_recv.at[a, i], 1),
        )

    def unit_state(unit):
        return state[unit].astype(bf16)

    spreads = {(a, i): spread(a, i) for a in range(2) for i in range(3)}
    spreads[0, 3] = spread(0, 3)

    def send(key):
        for copy in spreads[key][:2]:
            copy.start()

    def valued():
        send((0, 2))
        send((1, 2))

    def strength(span, dz):
        last = strength_lanes(heads, dz)
        mine[span, 3 * width :] = last.astype(bf16)
        tails[0, :, span] = last.T[:16].astype(bf16)

    def unit_pairs(i):
        return [
            (units[i, :, h * dim : (h + 1) * dim], scales[:, i * heads + h : i * heads + h + 1])
            for h in range(heads)
        ]

    halves = [slice(0, rows // 2), slice(rows // 2, rows)]

    def input_part(index, rows):
        span = pl.ds(pl.multiple_of(index * width, width), width)
        total = dot(mine[rows, 3 * width :], wb[:, span])
        for i in range(3):
            total = total + dot(mine[rows, i * width : (i + 1) * width], w[i, span, :], (1, 1))
        return total

    side = 1 - 2 * (group // 2)
    edge = (group == 0) | (group == groups - 1)
    rim = jnp.where(edge, 1, 0)
    targets = [
        group + side * (1 + 2 * rim),
        group + side * (3 * rim - 1),
        group + side * (2 - rim),
    ]

    def landing(n, h):
        slot = jnp.where(edge, groups, group) if n == 0 else group
        device = group + side if n == 0 else targets[n]
        return remote(
            piece.at[n, halves[h]], landed.at[slot, halves[h]],
            z_send.at[n, h], z_recv.at[slot, h], {"head": device},
        )

    def first_piece(h):
        piece[0, halves[h]] = input_part(targets[0], halves[h]).astype(bf16)
        landing(0, h).start()

    gradients(
        heads, dim, unit_pairs(0), unit_pairs(1), z, g, mid, unit_state, put, strength,
        valued, lambda: first_piece(0),
    )
    for key in ((0, 0), (1, 0), (0, 1), (1, 1), (0, 3)):
        send(key)
    first_piece(1)
    piece[1] = input_part(targets[1], slice(0, rows)).astype(bf16)
    for h in range(2):
        landing(1, h).start()
    piece[2] = input_part(targets[2], slice(0, rows)).astype(bf16)

    @pl.when(edge)
    def _():
        for h in range(2):
            landing(2, h).start()

    def arrived(slot, h):
        remote(
            piece.at[0, halves[h]], landed.at[slot, halves[h]],
            z_send.at[0, h], z_recv.at[slot, h], {"head": targets[0]},
        ).wait_recv()
        return landed[slot, halves[h]].astype(f32)

    def pass_on(h):
        @pl.when(jnp.logical_not(edge))
        def _():
            piece[2, halves[h]] = (piece[2, halves[h]].astype(f32) + arrived(groups, h)).astype(bf16)
            landing(2, h).start()

    order = [(0, 2), (1, 2), (0, 0), (1, 0), (0, 1), (1, 1), (0, 3)]
    trades = {
        (a, i): remote(
            part_out.at[a, i], part_in.at[a, i], part_send.at[a, i], part_recv.at[a, i], partners[a]
        )
        for a in range(2)
        for i in range(3)
    }
    tail_trade = remote(tail_out, tail_in, part_send.at[0, 3], part_recv.at[0, 3], partners[0])

    def process(a, i):
        spreads[a, i][1].wait_recv()
        spreads[a, i][2].wait_recv()
        if i < 3:
            value = dot(cols_t[a], blocks[a, i])
            part_out[a, i] = value[part:].astype(bf16)
            trades[a, i].start()
            grads[i, :, a * half * dim : (a + 1) * half * dim] = value[:part]
        else:
            sums = [dot(tails[0], own_columns(0, b)) for b in range(2)]
            for s in range(1, 4):
                sums = [t + dot(tails[s], cols[0, s, b]) for b, t in enumerate(sums)]
            held = jnp.sum(tails[...].astype(f32), 0)
            held = jnp.sum(held, -1, keepdims=True)
            row, col = iotas(16, part)
            held = jnp.sum(jnp.where(row == col, held, 0.0), 0, keepdims=True)
            row = lax.broadcasted_iota(jnp.int32, (16, part), 0)
            tail_out[...] = jnp.where(row == 8, held, sums[1])
            tail_trade.start()
            tail_ref[...] = jnp.where(row == 8, held, sums[0])

    for key in later:
        tokens[key].wait_recv()
        turn_block(*key)
    for n, key in enumerate(order):
        spreads[key][0].wait_recv()
        spreads[key][2].start()
        if n > 0:
            process(*order[n - 1])
        if n == 1:
            pass_on(0)
        if n == 3:
            pass_on(1)

    process(*order[-1])
    own[...] = input_part(group, slice(0, rows))
    saves = []

    def keep(source, target):
        copy = pltpu.make_async_copy(source, target, save.at[len(saves)])
        copy.start()
        saves.append(copy)

    targets_hbm = (gq_hbm, gk_hbm, gv_hbm)
    for a, i in order:
        if i < 3:
            trades[a, i].wait_recv()
            span = slice(a * half * dim, (a + 1) * half * dim)
            grads[i, :, span] = grads[i, :, span] + part_in[a, i].astype(f32)
            keep(grads.at[i, :, span], targets_hbm[i].at[:, span])
        else:
            tail_trade.wait_recv()
            tail_ref[...] = tail_ref[...] + tail_in[...]
            keep(tail_ref, tail_hbm)

    for h in range(2):

        @pl.when(jnp.logical_not(edge))
        def _():
            own[halves[h]] = own[halves[h]] + arrived(group - side, h)

        total = own[halves[h]] + arrived(group + side, h) + arrived(group + 2 * side, h)
        dx_ref[halves[h]] = total.astype(bf16)
        keep(dx_ref.at[halves[h]], dx_hbm.at[halves[h]])

    share.wait_send()

    @pl.when(upper == taken)
    def _():
        for copy in up:
            copy.wait_send()

    for n in range(3):
        for h in range(2):
            landing(n, h).wait_send()
    for copy in sibling + list(tokens.values()) + over + forward + [tail_trade] + list(trades.values()):
        copy.wait_send()
    for copies in spreads.values():
        for copy in copies:
            copy.wait_send()
    for copy in saves:
        copy.wait()


def place_kernel(count, heads, *refs):
    sources, outs = refs[: count + 1], refs[count + 1 : 2 * count + 3]
    held, (strength, bias, sems) = refs[2 * count + 3 : -3], refs[-3:]
    fetch, store = [], []
    for i in range(count):
        size = sources[i].shape[0] // 2
        for n in range(2):
            span = pl.ds(n * size, size)
            j = 2 * i + n
            fetch.append(
                pltpu.make_async_copy(sources[i].at[span], held[i].at[span], sems.at[0, j])
            )
            store.append(pltpu.make_async_copy(held[i].at[span], outs[i].at[span], sems.at[1, j]))
    small = pltpu.make_async_copy(sources[count], held[count], sems.at[0, 2 * count])
    small.start()
    for copy in fetch:
        copy.start()
    small.wait()
    strength[...] = held[count][:heads, :]
    bias[...] = held[count][8:9, :heads] + held[count][8:9, heads : 2 * heads]
    store.append(pltpu.make_async_copy(strength, outs[count], sems.at[1, 2 * count]))
    store.append(pltpu.make_async_copy(bias, outs[count + 1], sems.at[1, 2 * count + 1]))
    for copy in store[-2:]:
        copy.start()
    for j in range(2 * count):
        fetch[j].wait()
        store[j].start()
    for copy in store:
        copy.wait()


def place(arrays, tail, heads):
    count = len(arrays)
    hbm = pl.BlockSpec(memory_space=pltpu.HBM)
    return pl.pallas_call(
        functools.partial(place_kernel, count, heads),
        out_shape=tuple(jax.ShapeDtypeStruct(a.shape, a.dtype) for a in arrays)
        + (
            jax.ShapeDtypeStruct((heads, tail.shape[1]), tail.dtype),
            jax.ShapeDtypeStruct((1, heads), tail.dtype),
        ),
        in_specs=[hbm] * (count + 1),
        out_specs=(hbm,) * (count + 2),
        scratch_shapes=[pltpu.VMEM(a.shape, a.dtype) for a in (*arrays, tail)]
        + [
            pltpu.VMEM((heads, tail.shape[1]), tail.dtype),
            pltpu.VMEM((1, heads), tail.dtype),
            pltpu.SemaphoreType.DMA((2, 2 * count + 2)),
        ],
        compiler_params=pltpu.CompilerParams(vmem_limit_bytes=60 * 1024 * 1024),
        name="place",
    )(*arrays, tail)


def whole_layer(tokens, weights, w_beta, b_beta, d_out):
    shards, groups = lax.axis_size("seq"), lax.axis_size("head")
    rows, features = tokens.shape
    heads = w_beta.shape[1]
    width = weights[0].shape[1]
    dim = width // heads
    half = heads // 2
    part = features // shards
    f32, bf16 = jnp.float32, jnp.bfloat16
    hbm = pl.BlockSpec(memory_space=pltpu.HBM)
    square = jax.ShapeDtypeStruct((part, width), f32)
    dma = pltpu.SemaphoreType.DMA
    outs = pl.pallas_call(
        functools.partial(layer_kernel, groups, heads, dim),
        out_shape=(
            jax.ShapeDtypeStruct((rows, features // groups), tokens.dtype),
            square,
            square,
            square,
            jax.ShapeDtypeStruct((16, part), f32),
        ),
        in_specs=[hbm] * 7,
        out_specs=(hbm,) * 5,
        scratch_shapes=[
            pltpu.VMEM((rows, features // groups), bf16),
            pltpu.VMEM((3, part, width), f32),
            pltpu.VMEM((16, part), f32),
            pltpu.VMEM((rows, features), bf16),
            pltpu.VMEM((3, features, width), bf16),
            pltpu.VMEM((LANES, features), bf16),
            pltpu.VMEM((rows, width), bf16),
            pltpu.VMEM((heads, features), bf16),
            pltpu.VMEM((1, heads), f32),
            pltpu.VMEM((3, rows, width), f32),
            pltpu.VMEM((2, rows, width), f32),
            pltpu.VMEM((rows, LANES), f32),
            pltpu.VMEM((rows, LANES), f32),
            pltpu.VMEM((heads, rows, 4 * dim), f32),
            pltpu.VMEM((2, 2 * heads, 2, dim, dim), bf16),
            pltpu.VMEM((2, half, dim, dim), bf16),
            pltpu.VMEM((2, heads, dim, dim), bf16),
            pltpu.VMEM((half, dim, dim), bf16),
            pltpu.VMEM((heads, dim, dim), bf16),
            pltpu.VMEM((2 * heads, dim, dim), f32),
            pltpu.VMEM((2, 4, 2, rows, part), bf16),
            pltpu.VMEM((2, 2 * part, 4 * rows), bf16),
            pltpu.VMEM((rows, 3 * width + LANES), bf16),
            pltpu.VMEM((2, 3, 4 * rows, width // 2), bf16),
            pltpu.VMEM((4, 16, rows), bf16),
            pltpu.VMEM((2, 3, part, width // 2), bf16),
            pltpu.VMEM((2, 3, part, width // 2), bf16),
            pltpu.VMEM((16, part), f32),
            pltpu.VMEM((16, part), f32),
            pltpu.VMEM((rows, features // groups), f32),
            pltpu.VMEM((3, rows, features // groups), bf16),
            pltpu.VMEM((groups + 1, rows, features // groups), bf16),
            dma((7,)),
            dma((11,)),
            dma((11,)),
            dma((4,)),
            dma((4,)),
            dma((2,)),
            dma((2,)),
            dma((2,)),
            dma((2,)),
            dma((3,)),
            dma,
            dma,
            dma((2, 4)),
            dma((2, 4)),
            dma((2, 4)),
            dma((2, 4)),
            dma((2, 4)),
            dma((2, 4)),
            dma((2, 4)),
            dma((2, 4)),
            dma((3, 2)),
            dma((groups + 1, 2)),
            dma((9,)),
        ],
        compiler_params=pltpu.CompilerParams(
            vmem_limit_bytes=60 * 1024 * 1024, collective_id=1, has_side_effects=True
        ),
        name="layer",
    )(tokens, *weights, d_out, w_beta.T, b_beta.reshape(1, heads))
    d_x, grad_q, grad_k, grad_v, tail, bias = place(outs[:4], outs[4], heads)
    return d_x, grad_q, grad_k, grad_v, tail.T, bias.reshape(heads)


def per_device(tokens, w_query, w_key, w_value, w_beta, b_beta, d_out):
    token_count, features = tokens.shape
    heads = w_beta.shape[1]
    width = w_query.shape[1]
    dim = width // heads
    f32 = jnp.float32
    shards, groups = lax.axis_size("seq"), lax.axis_size("head")
    weights = (w_query, w_key, w_value)
    fits = heads % 2 == 0 and 2 * heads <= 8 and width * groups == features and dim == LANES
    if shards == 8 and groups == 4 and fits and features // shards == token_count:
        return whole_layer(tokens, weights, w_beta, b_beta, d_out)
    q, k, v = (jnp.dot(tokens, w, preferred_element_type=f32) for w in weights)
    w_last = jnp.pad(w_beta, ((0, 0), (0, LANES - heads)))
    z = jnp.dot(tokens, w_last, preferred_element_type=f32) + jnp.pad(b_beta, (0, LANES - heads))
    params = pltpu.CompilerParams(vmem_limit_bytes=60 * 1024 * 1024)
    columns = lax.all_to_all(tokens, "seq", split_axis=1, concat_axis=0, tiled=True)
    maps, mid = pl.pallas_call(
        functools.partial(summary_kernel, heads, dim),
        out_shape=(
            jax.ShapeDtypeStruct((2 * heads, 2, dim, dim), jnp.bfloat16),
            jax.ShapeDtypeStruct((heads, token_count, 4 * dim), f32),
        ),
        compiler_params=params,
        name="summary",
    )(q, k, v, z, d_out)
    states = gathered_states(maps, heads)
    grads = pl.pallas_call(
        functools.partial(gradient_kernel, heads, dim),
        out_shape=jax.ShapeDtypeStruct((token_count, 3 * width + LANES), jnp.bfloat16),
        compiler_params=params,
        name="gradient",
    )(q, k, z, d_out, mid, states)
    whole = lax.all_gather(grads, "seq", axis=0, tiled=True)
    partial = jnp.dot(grads[:, 3 * width : 3 * width + heads], w_beta.T, preferred_element_type=f32)
    for i, w in enumerate(weights):
        partial = partial + jnp.dot(
            grads[:, i * width : (i + 1) * width], w.T, preferred_element_type=f32
        )
    d_x = lax.psum_scatter(
        partial.astype(jnp.bfloat16), "head", scatter_dimension=1, tiled=True
    )

    def weight_grad(block):
        return lax.dot_general(
            columns, block, (((0,), (0,)), ((), ())), preferred_element_type=f32
        )

    found = [weight_grad(whole[:, i * width : (i + 1) * width]) for i in range(3)]
    tail = whole[:, 3 * width :]
    grad_wbeta = weight_grad(tail)[:, :heads]
    sums = jnp.sum(tail.astype(f32), 0)
    return (d_x, *found, grad_wbeta, sums[:heads] + sums[heads : 2 * heads])


def solution(mesh):
    in_specs = (
        P("seq", None),
        P(None, "head"),
        P(None, "head"),
        P(None, "head"),
        P(None, "head"),
        P("head"),
        P("seq", "head"),
    )
    out_specs = (
        P("seq", "head"),
        P("seq", "head"),
        P("seq", "head"),
        P("seq", "head"),
        P("seq", "head"),
        P("head"),
    )
    return jax.shard_map(
        per_device, mesh=mesh, in_specs=in_specs, out_specs=out_specs, check_vma=False
    )
```

```python
import functools

import jax
import jax.numpy as jnp
from jax import lax
from jax.experimental import pallas as pl
from jax.experimental.pallas import tpu as pltpu
from jax.sharding import PartitionSpec as P

epsilon = 1e-06
LANES = 128
MESH = pl.DeviceIdType.MESH
highest = lax.Precision.HIGHEST


def split(a):
    high = a.astype(jnp.bfloat16)
    return high, (a - high.astype(jnp.float32)).astype(jnp.bfloat16)


def only(a):
    return a.astype(jnp.bfloat16), None


def mm(a, b, dims=(1, 0)):
    numbers = (((dims[0],), (dims[1],)), ((), ()))
    dot = functools.partial(
        lax.dot_general, dimension_numbers=numbers, preferred_element_type=jnp.float32
    )
    total = dot(a[0], b[0])
    if b[1] is not None:
        total = total + dot(a[0], b[1])
    if a[1] is not None:
        total = total + dot(a[1], b[0])
    return total


def square_mm(a, b):
    size = a[0].shape[0]
    left = jnp.concatenate(a, 1)
    right = jnp.concatenate(
        [jnp.concatenate(b, 1), jnp.concatenate([b[0], jnp.zeros_like(b[0])], 1)], 0
    )
    both = lax.dot_general(left, right, (((1,), (0,)), ((), ())), preferred_element_type=jnp.float32)
    return both[:, :size] + both[:, size:]


def tight_mm(a, b, dims=(1, 0)):
    inner, outer = dims[1], 1 - dims[1]
    size = b[0].shape[outer]
    left = a[0] if a[1] is None else jnp.concatenate(a, dims[0])
    right = b[0] if b[1] is None else jnp.concatenate(b, outer)
    if a[1] is not None:
        again = b[0]
        if b[1] is not None:
            again = jnp.concatenate([b[0], jnp.zeros_like(b[0])], outer)
        right = jnp.concatenate([right, again], inner)
    both = lax.dot_general(
        left, right, (((dims[0],), (dims[1],)), ((), ())), preferred_element_type=jnp.float32
    )
    return both if b[1] is None else both[:, :size] + both[:, size:]


def wide_mm(a, b, dims=(1, 0)):
    numbers = (((dims[0],), (dims[1],)), ((), ()))
    size = b[0].shape[1 - dims[1]]
    both = lax.dot_general(
        a[0], jnp.concatenate(b, 1 - dims[1]), numbers, preferred_element_type=jnp.float32
    )
    total = both[:, :size] + both[:, size:]
    if a[1] is not None:
        total = total + lax.dot_general(a[1], b[0], numbers, preferred_element_type=jnp.float32)
    return total


def deep_mm(a, b):
    numbers = (((1,), (1,)), ((), ()))
    dot = functools.partial(
        lax.dot_general, dimension_numbers=numbers, preferred_element_type=jnp.float32
    )
    return dot(jnp.concatenate(a, 1), jnp.concatenate([b[0], b[0]], 1)) + dot(a[0], b[1])


def iotas(rows, cols):
    return (
        lax.broadcasted_iota(jnp.int32, (rows, cols), 0),
        lax.broadcasted_iota(jnp.int32, (rows, cols), 1),
    )


def invert_unit_lower(systems, fillers=()):
    fillers = list(fillers)
    size = systems[0].shape[0]
    base = min(size, LANES)
    row, col = iotas(base, base)
    eye = jnp.where(row == col, 1.0, 0.0).astype(jnp.float32)

    def step_mask(s):
        return (row // (2 * s) == col // (2 * s)) & (row % (2 * s) >= s) & (col % (2 * s) < s)

    count = size // base
    diagonals = [
        n[i * base : (i + 1) * base, i * base : (i + 1) * base] for n in systems for i in range(count)
    ]
    inverses = [eye - jnp.where(step_mask(1), n, 0.0) for n in diagonals]
    pairs = [split(n) for n in diagonals]
    s = 2
    while s < base:
        mask = jnp.where(step_mask(s), 1.0, 0.0).astype(jnp.bfloat16)
        parts = [split(x) for x in inverses]
        inner = [square_mm((mask * n[0], mask * n[1]), x) for n, x in zip(pairs, parts)]
        if fillers:
            fillers.pop(0)()
        outer = [square_mm(x, split(y)) for x, y in zip(parts, inner)]
        inverses = [x - y for x, y in zip(inverses, outer)]
        s *= 2
    for filler in fillers:
        filler()
    grouped = [inverses[i * count : (i + 1) * count] for i in range(len(systems))]
    width = base
    while width < size:
        merged = []
        for n, blocks in zip(systems, grouped):
            joined = []
            for i in range(0, len(blocks), 2):
                first, second = blocks[i], blocks[i + 1]
                low = n[(i + 1) * width : (i + 2) * width, i * width : (i + 1) * width]
                corner = square_mm(split(second), split(square_mm(split(low), split(first))))
                joined.append(
                    jnp.concatenate(
                        [
                            jnp.concatenate([first, jnp.zeros_like(first)], 1),
                            jnp.concatenate([-corner, second], 1),
                        ],
                        0,
                    )
                )
            merged.append(joined)
        grouped = merged
        width *= 2
    return [g[0] for g in grouped]


def normalise(raw):
    scale = lax.rsqrt(jnp.sum(raw * raw, -1, keepdims=True) + epsilon)
    return raw * scale, scale


def dot(a, b, dims=(1, 0)):
    return lax.dot_general(
        a, b, (((dims[0],), (dims[1],)), ((), ())), preferred_element_type=jnp.float32
    )


def summarise(heads, dim, q_ref, k_ref, v_ref, z_ref, g_ref, put_map, fillers=(), put_unit=None):
    count = q_ref.shape[0]
    row, col = iotas(count, count)
    strict, inclusive = row > col, row >= col
    every = range(heads)
    cols = [slice(h * dim, (h + 1) * dim) for h in every]
    beta_all = 2.0 * jax.nn.sigmoid(z_ref[:, :heads])
    beta = [beta_all[:, h : h + 1] for h in every]
    kp = [normalise(k_ref[:, c]) for c in cols]
    kn = [x[0] for x in kp]
    ks = [split(x) for x in kn]
    gs = [(g_ref[:, c], None) for c in cols]
    gram = [jnp.where(strict, deep_mm(x, x), 0.0) for x in ks]
    systems = [b * n for b, n in zip(beta, gram)]
    late = {}

    def score():
        qp = [normalise(q_ref[:, c]) for c in cols]
        late["qs"] = [split(x[0]) for x in qp]
        if put_unit is not None:
            put_unit(qp, kp)
        late["scores"] = [
            split(jnp.where(inclusive, deep_mm(a, b), 0.0)) for a, b in zip(late["qs"], ks)
        ]

    def pull():
        late["back"] = [mm(p, g, (0, 0)) for p, g in zip(late["scores"], gs)]
        late["direct"] = [wide_mm(g, q, (0, 0)) for g, q in zip(gs, late["qs"])]

    fillers = list(fillers) + [score, pull]
    inverse = [split(t) for t in invert_unit_lower(systems, fillers)]
    gram = [split(n) for n in gram]
    back, direct = late["back"], late["direct"]
    forth_in = [jnp.concatenate([v_ref[:, c], k], 1) for c, k in zip(cols, kn)]
    forth = [split(mm(t, split(b * x))) for t, b, x in zip(inverse, beta, forth_in)]
    adjoint = [
        mm(t, split(jnp.concatenate([p, k], 1)), (0, 0)) for t, p, k in zip(inverse, back, kn)
    ]
    ends = [wide_mm(f, k, (0, 0)) for f, k in zip(forth, ks)]
    tails = [wide_mm(split(a), split(b * k), (0, 0)) for a, b, k in zip(adjoint, beta, kn)]
    for h in every:
        put_map(h, ends[h][dim:], ends[h][:dim])
        put_map(heads + h, tails[h][dim:], direct[h] - tails[h][:dim])

    def put_mid(mid_ref):
        for h in every:
            mid_ref[h, :, : 2 * dim] = forth_in[h] - mm(gram[h], forth[h])
            mid_ref[h, :, 2 * dim :] = adjoint[h]

    return put_mid


def summary_kernel(heads, dim, q_ref, k_ref, v_ref, z_ref, g_ref, map_ref, mid_ref):
    def put_map(unit, factor, offset):
        map_ref[unit, 0] = factor.astype(map_ref.dtype)
        map_ref[unit, 1] = offset.astype(map_ref.dtype)

    summarise(heads, dim, q_ref, k_ref, v_ref, z_ref, g_ref, put_map)(mid_ref)


def gradients(heads, dim, qp, kp, z_ref, g_ref, mid_ref, state, put, strength, valued, between):
    every = range(heads)
    count = z_ref.shape[0] // 2
    halves = (slice(0, count), slice(count, 2 * count))
    row, col = iotas(count, count)
    strict, inclusive = row > col, row >= col
    beta_all = 2.0 * jax.nn.sigmoid(z_ref[:, :heads])
    beta = [beta_all[:, h : h + 1] for h in every]
    ss = [(state(h), None) for h in every]
    ds = [(state(heads + h), None) for h in every]
    dx = [
        mid_ref[h, :, 2 * dim : 3 * dim] + tight_mm(split(mid_ref[h, :, 3 * dim :]), d, (1, 1))
        for h, d in zip(every, ds)
    ]
    dv = [b * x for b, x in zip(beta, dx)]
    for h in every:
        put(2, h, slice(0, 2 * count), dv[h].astype(jnp.bfloat16))
    valued()

    def pick(x, rows):
        return tuple(None if y is None else y[rows] for y in x)

    def part(rows):
        ks = [split(x[0][rows]) for x in kp]
        qs = [split(x[0][rows]) for x in qp]
        gs = [(g_ref[rows, h * dim : (h + 1) * dim], None) for h in every]
        plain = [
            mid_ref[h, rows, :dim] - tight_mm(split(mid_ref[h, rows, dim : 2 * dim]), s, (1, 1))
            for h, s in zip(every, ss)
        ]
        us = [split(b[rows] * x) for b, x in zip(beta, plain)]
        dz = [
            jnp.sum(x[rows] * p, -1, keepdims=True) * b[rows] * (1.0 - 0.5 * b[rows])
            for x, p, b in zip(dx, plain, beta)
        ]
        return ks, qs, gs, us, dz

    def through(grad, pair, rows):
        unit, scale = pair[0][rows], pair[1][rows]
        return scale * (grad - unit * jnp.sum(unit * grad, -1, keepdims=True))

    def finish(rows, dqn, dkn):
        for h in every:
            put(0, h, rows, through(dqn[h], qp[h], rows).astype(jnp.bfloat16))
            put(1, h, rows, through(dkn[h], kp[h], rows).astype(jnp.bfloat16))

    def below(a, b, mask):
        found = [tight_mm(x, y, (1, 1)) for x, y in zip(a, b)]
        return found if mask is None else [jnp.where(mask, x, 0.0) for x in found]

    dvs = [[split(x[rows]) for x in dv] for rows in halves]
    k0, q0, g0, u0, dz = part(halves[0])
    strength(halves[0], dz)
    k1 = [split(x[0][halves[1]]) for x in kp]
    q1 = [split(x[0][halves[1]]) for x in qp]
    g1 = [(g_ref[halves[1], h * dim : (h + 1) * dim], None) for h in every]
    inner0 = [split(x) for x in below(g0, u0, inclusive)]
    pair0 = below(dvs[0], u0, strict)
    inner1 = [split(x) for x in below(g1, u0, None)]
    pair1 = below(dvs[1], u0, None)
    dqn = [tight_mm(g, s) + tight_mm(i, k) for g, s, i, k in zip(g0, ss, inner0, k0)]
    dkn = [
        tight_mm(i, q, (0, 0)) + tight_mm(j, r, (0, 0)) + tight_mm(u, d) - tight_mm(x, s)
        - tight_mm(split(e + e.T), k) - tight_mm(split(f.T), l)
        for i, q, j, r, u, d, x, s, e, k, f, l in zip(
            inner0, q0, inner1, q1, u0, ds, dvs[0], ss, pair0, k0, pair1, k1
        )
    ]
    finish(halves[0], dqn, dkn)
    between()
    k1, q1, g1, u1, dz = part(halves[1])
    strength(halves[1], dz)
    inner2 = [split(x) for x in below(g1, u1, inclusive)]
    pair2 = below(dvs[1], u1, strict)
    dqn = [
        tight_mm(g, s) + tight_mm(j, k) + tight_mm(i, l)
        for g, s, j, k, i, l in zip(g1, ss, inner1, k0, inner2, k1)
    ]
    dkn = [
        tight_mm(i, q, (0, 0)) + tight_mm(u, d) - tight_mm(x, s) - tight_mm(split(f), k) - tight_mm(split(e + e.T), l)
        for i, q, u, d, x, s, f, k, e, l in zip(
            inner2, q1, u1, ds, dvs[1], ss, pair1, k0, pair2, k1
        )
    ]
    finish(halves[1], dqn, dkn)


def strength_lanes(heads, dz):
    lane = lax.broadcasted_iota(jnp.int32, (dz[0].shape[0], LANES), 1)
    last = jnp.zeros((dz[0].shape[0], LANES), jnp.float32)
    for h in range(heads):
        high, low = split(dz[h])
        last = jnp.where(lane == h, high.astype(jnp.float32), last)
        last = jnp.where(lane == heads + h, low.astype(jnp.float32), last)
    return last


def gradient_kernel(heads, dim, q_ref, k_ref, z_ref, g_ref, mid_ref, state_ref, out_ref):
    width = heads * dim

    def put(i, h, rows, value):
        out_ref[rows, i * width + h * dim : i * width + (h + 1) * dim] = value

    def state(unit):
        return state_ref[unit]

    def strength(rows, dz):
        out_ref[rows, 3 * width :] = strength_lanes(heads, dz).astype(jnp.bfloat16)

    cols = [slice(h * dim, (h + 1) * dim) for h in range(heads)]
    qp = [normalise(q_ref[:, c]) for c in cols]
    kp = [normalise(k_ref[:, c]) for c in cols]
    gradients(
        heads, dim, qp, kp, z_ref, g_ref, mid_ref, state, put, strength,
        lambda: None, lambda: None,
    )


def gathered_states(maps, heads):
    count = lax.axis_size("seq")
    place = lax.axis_index("seq")
    gathered = lax.all_gather(maps, "seq").astype(jnp.float32)

    def walk(steps, pick, rows):
        def one(lap, state):
            pair = lax.dynamic_index_in_dim(gathered, pick(lap), 0, False)[rows]
            moved = jnp.einsum("hij,hjk->hik", state, pair[:, 0], precision=highest)
            return state - moved + pair[:, 1]

        return lax.fori_loop(0, steps, one, jnp.zeros((heads,) + maps.shape[2:], jnp.float32))

    first = walk(place, lambda lap: lap, slice(0, heads))
    second = walk(count - 1 - place, lambda lap: count - 1 - lap, slice(heads, None))
    return jnp.concatenate([first, second]).astype(maps.dtype)


def layer_kernel(
    groups, heads, dim,
    x_hbm, wq_hbm, wk_hbm, wv_hbm, g_hbm, wb_hbm, b_hbm,
    dx_hbm, gq_hbm, gk_hbm, gv_hbm, tail_hbm,
    dx_ref, grads, tail_ref, x, w, wb, g, wb_ref, b_ref, qkv, units, scales, z, mid, maps, x_out, x_in, y_out, y_in, state,
    cols, cols_t, mine, blocks, tails, part_out, part_in, tail_out, tail_in,
    own, piece, landed,
    load, tok_send, tok_recv, map_send, map_recv, x_send, x_recv, f_send, f_recv,
    y_send, y_recv, s_recv, far_send, far_recv, sib_send, sib_recv, fwd_send, fwd_recv,
    part_send, part_recv, z_send, z_recv, save,
):
    me = lax.axis_index("seq")
    group = lax.axis_index("head")
    core, across, upper = me % 2, (me // 2) % 2, me // 4
    rows, width = g.shape
    part = cols.shape[-1]
    half = heads // 2
    f32, bf16 = jnp.float32, jnp.bfloat16

    def seq(o):
        index = me
        for bit in (1, 2, 4):
            if o & bit:
                index = index + bit - 2 * bit * ((me // bit) % 2)
        return index

    def remote(source, target, send, recv, device):
        return pltpu.make_async_remote_copy(
            src_ref=source,
            dst_ref=target,
            send_sem=send,
            recv_sem=recv,
            device_id=device if isinstance(device, dict) else {"seq": seq(device)},
            device_id_type=MESH,
        )

    pairs = (
        (x_hbm, x), (wk_hbm, w.at[1]), (wb_hbm, wb_ref), (b_hbm, b_ref), (g_hbm, g),
        (wq_hbm, w.at[0]), (wv_hbm, w.at[2]),
    )
    loads = [pltpu.make_async_copy(s, t, load.at[i]) for i, (s, t) in enumerate(pairs)]
    for copy in loads:
        copy.start()
    barrier = pltpu.get_barrier_semaphore()
    others = [{"seq": seq(o)} for o in range(1, 8)]
    others += [{"head": lax.rem(group + r, groups)} for r in range(1, groups)]
    for peer in others:
        pl.semaphore_signal(barrier, inc=1, device_id=peer, device_id_type=MESH)
    wb[...] = jnp.zeros_like(wb)
    pl.semaphore_wait(barrier, len(others))

    fars, partners = (2, 4), (4, 2)
    slots = [(0, 1, far, far ^ 1) for far in fars]

    def columns(index):
        return pl.ds(pl.multiple_of(index * part, part), part)

    tokens, later = {}, [(0, 3, 1), (1, 3, 1)]
    for s in (2, 3, 1):
        for b in range(2):
            for a in range(2):
                if (a, s, b) != (1, 1, 0):
                    owner = seq(slots[a][s] ^ (partners[a] if b else 0))
                    i = len(tokens)
                    tokens[a, s, b] = remote(
                        x_hbm.at[:, columns(owner)], cols.at[a, s, b],
                        tok_send.at[i], tok_recv.at[i], slots[a][s],
                    )
                    if (a, s, b) not in later:
                        tokens[a, s, b].start()

    loads[0].wait()
    loads[1].wait()
    qkv[1] = dot(x[...], w[1])
    for copy in loads[2:]:
        copy.wait()
    wb[pl.ds(0, heads), :] = wb_ref[...]
    z[:, :heads] = dot(x[...], wb[:16], (1, 1))[:, :heads] + b_ref[...]
    def put_map(unit, factor, offset):
        maps[core, unit, 0] = factor.astype(bf16)
        maps[core, unit, 1] = offset.astype(bf16)

    def project(i, n):
        def run():
            span = slice(n * width // 2, (n + 1) * width // 2)
            qkv[i, :, span] = dot(x[...], w[i, :, span])

        return run

    def put_unit(qp, kp):
        for i, pairs in enumerate((qp, kp)):
            for h, (unit, scale) in enumerate(pairs):
                units[i, :, h * dim : (h + 1) * dim] = unit
                scales[:, i * heads + h : i * heads + h + 1] = scale

    fillers = [project(i, n) for i in (0, 2) for n in range(2)]
    put_mid = summarise(
        heads, dim, qkv.at[0], qkv.at[1], qkv.at[2], z, g, put_map, fillers, put_unit
    )
    passed, taken = across, 1 - across
    kept, other = pl.ds(core * half, half), pl.ds((1 - core) * half, half)
    urgent = [
        (way * heads + n * half, j)
        for j, (way, n) in enumerate(
            [(passed, 1 - core), (taken, 1 - core), (passed, core), (taken, core)]
        )
    ]
    sibling = [
        remote(
            maps.at[core, pl.ds(unit, half)], maps.at[core, pl.ds(unit, half)],
            map_send.at[j], map_recv.at[j], 1,
        )
        for unit, j in urgent
    ]
    arriving = [
        remote(
            maps.at[1 - core, pl.ds(way * heads + n * half, half)],
            maps.at[1 - core, pl.ds(way * heads + n * half, half)],
            map_send.at[j], map_recv.at[j], 1,
        )
        for j, (way, n) in enumerate([(passed, core), (taken, core), (passed, 1 - core), (taken, 1 - core)])
    ]
    for copy in sibling:
        copy.start()
    put_mid(mid)
    arriving[0].wait_recv()

    def chip_part(way, n, j):
        unit = way * heads + core * half + n
        first, second = maps[way, unit, j], maps[1 - way, unit, j]
        return first.astype(f32) - dot(first, maps[1 - way, unit, 0]) + second.astype(f32)

    over = [remote(x_out.at[j], x_in.at[j, kept], x_send.at[j], x_recv.at[j], 2) for j in range(2)]
    for j in range(2):
        for n in range(half):
            x_out[j, n] = chip_part(passed, n, 1 - j).astype(bf16)
        over[j].start()
    arriving[1].wait_recv()
    totals = [(chip_part(taken, n, 0), chip_part(taken, n, 1)) for n in range(half)]
    forward = [
        remote(x_in.at[j, kept], x_in.at[j, kept], f_send.at[j], f_recv.at[j], 1) for j in range(2)
    ]

    def own_columns(a, b):
        return x[:, columns(seq(partners[a]) if b else me)]

    def turn_block(a, s, b):
        if s == 0:
            block = own_columns(a, b)
        else:
            block = cols[0, 1, 0] if (a, s, b) == (1, 1, 0) else cols[a, s, b]
        cols_t[a, b * part : (b + 1) * part, s * rows : (s + 1) * rows] = block.T

    def turn(a):
        for s in range(4):
            for b in range(2):
                if (a, s, b) not in later:
                    turn_block(a, s, b)

    for key, copy in tokens.items():
        if key[0] == 0 and key not in later:
            copy.wait_recv()
    turn(0)
    over[0].wait_recv()
    for n, (factor, offset) in enumerate(totals):
        entering = x_in[0, core * half + n]
        y_out[n] = (entering.astype(f32) - tight_mm((entering, None), split(factor)) + offset).astype(bf16)
    up = [remote(y_out, y_in.at[kept], y_send.at[j], y_recv, 4 + 2 * j) for j in range(2)]
    share = remote(y_in.at[kept], y_in.at[kept], y_send.at[2], s_recv, 1)

    @pl.when(upper == taken)
    def _():
        for copy in up[::-1]:
            copy.start()

    forward[0].start()
    over[1].wait_recv()
    forward[1].start()
    for key in later:
        tokens[key].start()
    for key, copy in tokens.items():
        if key[0] == 1 and key not in later:
            copy.wait_recv()
    turn(1)
    for copy in forward + arriving[2:]:
        copy.wait_recv()
    state[...] = jnp.zeros_like(state)
    for h in range(heads):
        state[taken * heads + h] = x_in[0, h].astype(f32)
    bridge = []
    lead, inside = 1 - upper, 1 - core
    for h in range(heads):
        unit = inside * heads + h
        factor = maps[inside, unit, 0]
        before = state[unit]
        state[unit] = before - tight_mm(split(before), (factor, None)) + maps[inside, unit, 1].astype(f32)
        first = jnp.where(taken == lead, x_in[1, h].astype(f32), 0.0).astype(bf16)
        second = jnp.where(inside == lead, factor.astype(f32), 0.0).astype(bf16)
        bridge.append(split(first.astype(f32) + second.astype(f32) - dot(first, second)))
    up[0].wait_recv()
    share.start()
    share.wait_recv()
    for h in range(heads):
        unit = lead * heads + h
        state[unit] = state[unit] + (y_in[h].astype(f32) - tight_mm((y_in[h], None), bridge[h]))

    def put(i, h, span, value):
        a, n = h // half, h % half
        mine[span, i * width + h * dim : i * width + (h + 1) * dim] = value
        blocks[a, i, span, n * dim : (n + 1) * dim] = value

    def spread(a, i):
        if i < 3:
            slot = [blocks.at[a, i, pl.ds(s * rows, rows)] for s in range(4)]
        else:
            slot = [tails.at[s] for s in range(4)]
        return (
            remote(slot[0], slot[2], far_send.at[a, i], far_recv.at[a, i], fars[a]),
            remote(slot[0], slot[1], sib_send.at[a, i], sib_recv.at[a, i], 1),
            remote(slot[2], slot[3], fwd_send.at[a, i], fwd_recv.at[a, i], 1),
        )

    def unit_state(unit):
        return state[unit].astype(bf16)

    spreads = {(a, i): spread(a, i) for a in range(2) for i in range(3)}
    spreads[0, 3] = spread(0, 3)

    def send(key):
        for copy in spreads[key][:2]:
            copy.start()

    def valued():
        send((0, 2))
        send((1, 2))

    def strength(span, dz):
        last = strength_lanes(heads, dz)
        mine[span, 3 * width :] = last.astype(bf16)
        tails[0, :, span] = last.T[:16].astype(bf16)

    def unit_pairs(i):
        return [
            (units[i, :, h * dim : (h + 1) * dim], scales[:, i * heads + h : i * heads + h + 1])
            for h in range(heads)
        ]

    halves = [slice(0, rows // 2), slice(rows // 2, rows)]

    def input_part(index, rows):
        span = pl.ds(pl.multiple_of(index * width, width), width)
        total = dot(mine[rows, 3 * width :], wb[:, span])
        for i in range(3):
            total = total + dot(mine[rows, i * width : (i + 1) * width], w[i, span, :], (1, 1))
        return total

    side = 1 - 2 * (group // 2)
    edge = (group == 0) | (group == groups - 1)
    rim = jnp.where(edge, 1, 0)
    targets = [
        group + side * (1 + 2 * rim),
        group + side * (3 * rim - 1),
        group + side * (2 - rim),
    ]

    def landing(n, h):
        slot = jnp.where(edge, groups, group) if n == 0 else group
        device = group + side if n == 0 else targets[n]
        return remote(
            piece.at[n, halves[h]], landed.at[slot, halves[h]],
            z_send.at[n, h], z_recv.at[slot, h], {"head": device},
        )

    def first_piece(h):
        piece[0, halves[h]] = input_part(targets[0], halves[h]).astype(bf16)
        landing(0, h).start()

    gradients(
        heads, dim, unit_pairs(0), unit_pairs(1), z, g, mid, unit_state, put, strength,
        valued, lambda: first_piece(0),
    )
    for key in ((0, 0), (1, 0), (0, 1), (1, 1), (0, 3)):
        send(key)
    first_piece(1)
    piece[1] = input_part(targets[1], slice(0, rows)).astype(bf16)
    for h in range(2):
        landing(1, h).start()
    piece[2] = input_part(targets[2], slice(0, rows)).astype(bf16)

    @pl.when(edge)
    def _():
        for h in range(2):
            landing(2, h).start()

    def arrived(slot, h):
        remote(
            piece.at[0, halves[h]], landed.at[slot, halves[h]],
            z_send.at[0, h], z_recv.at[slot, h], {"head": targets[0]},
        ).wait_recv()
        return landed[slot, halves[h]].astype(f32)

    def pass_on(h):
        @pl.when(jnp.logical_not(edge))
        def _():
            piece[2, halves[h]] = (piece[2, halves[h]].astype(f32) + arrived(groups, h)).astype(bf16)
            landing(2, h).start()

    order = [(0, 2), (1, 2), (0, 0), (1, 0), (0, 1), (1, 1), (0, 3)]
    trades = {
        (a, i): remote(
            part_out.at[a, i], part_in.at[a, i], part_send.at[a, i], part_recv.at[a, i], partners[a]
        )
        for a in range(2)
        for i in range(3)
    }
    tail_trade = remote(tail_out, tail_in, part_send.at[0, 3], part_recv.at[0, 3], partners[0])

    def process(a, i):
        spreads[a, i][1].wait_recv()
        spreads[a, i][2].wait_recv()
        if i < 3:
            value = dot(cols_t[a], blocks[a, i])
            part_out[a, i] = value[part:].astype(bf16)
            trades[a, i].start()
            grads[i, :, a * half * dim : (a + 1) * half * dim] = value[:part]
        else:
            sums = [dot(tails[0], own_columns(0, b)) for b in range(2)]
            for s in range(1, 4):
                sums = [t + dot(tails[s], cols[0, s, b]) for b, t in enumerate(sums)]
            held = jnp.sum(tails[...].astype(f32), 0)
            held = jnp.sum(held, -1, keepdims=True)
            row, col = iotas(16, part)
            held = jnp.sum(jnp.where(row == col, held, 0.0), 0, keepdims=True)
            row = lax.broadcasted_iota(jnp.int32, (16, part), 0)
            tail_out[...] = jnp.where(row == 8, held, sums[1])
            tail_trade.start()
            tail_ref[...] = jnp.where(row == 8, held, sums[0])

    for key in later:
        tokens[key].wait_recv()
        turn_block(*key)
    for n, key in enumerate(order):
        spreads[key][0].wait_recv()
        spreads[key][2].start()
        if n > 0:
            process(*order[n - 1])
        if n == 1:
            pass_on(0)
        if n == 3:
            pass_on(1)

    process(*order[-1])
    own[...] = input_part(group, slice(0, rows))
    saves = []

    def keep(source, target):
        copy = pltpu.make_async_copy(source, target, save.at[len(saves)])
        copy.start()
        saves.append(copy)

    targets_hbm = (gq_hbm, gk_hbm, gv_hbm)
    for a, i in order:
        if i < 3:
            trades[a, i].wait_recv()
            span = slice(a * half * dim, (a + 1) * half * dim)
            grads[i, :, span] = grads[i, :, span] + part_in[a, i].astype(f32)
            keep(grads.at[i, :, span], targets_hbm[i].at[:, span])
        else:
            tail_trade.wait_recv()
            tail_ref[...] = tail_ref[...] + tail_in[...]
            keep(tail_ref, tail_hbm)

    for h in range(2):

        @pl.when(jnp.logical_not(edge))
        def _():
            own[halves[h]] = own[halves[h]] + arrived(group - side, h)

        total = own[halves[h]] + arrived(group + side, h) + arrived(group + 2 * side, h)
        dx_ref[halves[h]] = total.astype(bf16)
        keep(dx_ref.at[halves[h]], dx_hbm.at[halves[h]])

    share.wait_send()

    @pl.when(upper == taken)
    def _():
        for copy in up:
            copy.wait_send()

    for n in range(3):
        for h in range(2):
            landing(n, h).wait_send()
    for copy in sibling + list(tokens.values()) + over + forward + [tail_trade] + list(trades.values()):
        copy.wait_send()
    for copies in spreads.values():
        for copy in copies:
            copy.wait_send()
    for copy in saves:
        copy.wait()


def place_kernel(count, heads, *refs):
    sources, outs = refs[: count + 1], refs[count + 1 : 2 * count + 3]
    held, (strength, bias, sems) = refs[2 * count + 3 : -3], refs[-3:]
    fetch, store = [], []
    for i in range(count):
        size = sources[i].shape[0] // 2
        for n in range(2):
            span = pl.ds(n * size, size)
            j = 2 * i + n
            fetch.append(
                pltpu.make_async_copy(sources[i].at[span], held[i].at[span], sems.at[0, j])
            )
            store.append(pltpu.make_async_copy(held[i].at[span], outs[i].at[span], sems.at[1, j]))
    small = pltpu.make_async_copy(sources[count], held[count], sems.at[0, 2 * count])
    small.start()
    for copy in fetch:
        copy.start()
    small.wait()
    strength[...] = held[count][:heads, :]
    bias[...] = held[count][8:9, :heads] + held[count][8:9, heads : 2 * heads]
    store.append(pltpu.make_async_copy(strength, outs[count], sems.at[1, 2 * count]))
    store.append(pltpu.make_async_copy(bias, outs[count + 1], sems.at[1, 2 * count + 1]))
    for copy in store[-2:]:
        copy.start()
    for j in range(2 * count):
        fetch[j].wait()
        store[j].start()
    for copy in store:
        copy.wait()


def place(arrays, tail, heads):
    count = len(arrays)
    hbm = pl.BlockSpec(memory_space=pltpu.HBM)
    return pl.pallas_call(
        functools.partial(place_kernel, count, heads),
        out_shape=tuple(jax.ShapeDtypeStruct(a.shape, a.dtype) for a in arrays)
        + (
            jax.ShapeDtypeStruct((heads, tail.shape[1]), tail.dtype),
            jax.ShapeDtypeStruct((1, heads), tail.dtype),
        ),
        in_specs=[hbm] * (count + 1),
        out_specs=(hbm,) * (count + 2),
        scratch_shapes=[pltpu.VMEM(a.shape, a.dtype) for a in (*arrays, tail)]
        + [
            pltpu.VMEM((heads, tail.shape[1]), tail.dtype),
            pltpu.VMEM((1, heads), tail.dtype),
            pltpu.SemaphoreType.DMA((2, 2 * count + 2)),
        ],
        compiler_params=pltpu.CompilerParams(vmem_limit_bytes=60 * 1024 * 1024),
        name="place",
    )(*arrays, tail)


def whole_layer(tokens, weights, w_beta, b_beta, d_out):
    shards, groups = lax.axis_size("seq"), lax.axis_size("head")
    rows, features = tokens.shape
    heads = w_beta.shape[1]
    width = weights[0].shape[1]
    dim = width // heads
    half = heads // 2
    part = features // shards
    f32, bf16 = jnp.float32, jnp.bfloat16
    hbm = pl.BlockSpec(memory_space=pltpu.HBM)
    square = jax.ShapeDtypeStruct((part, width), f32)
    dma = pltpu.SemaphoreType.DMA
    outs = pl.pallas_call(
        functools.partial(layer_kernel, groups, heads, dim),
        out_shape=(
            jax.ShapeDtypeStruct((rows, features // groups), tokens.dtype),
            square,
            square,
            square,
            jax.ShapeDtypeStruct((16, part), f32),
        ),
        in_specs=[hbm] * 7,
        out_specs=(hbm,) * 5,
        scratch_shapes=[
            pltpu.VMEM((rows, features // groups), bf16),
            pltpu.VMEM((3, part, width), f32),
            pltpu.VMEM((16, part), f32),
            pltpu.VMEM((rows, features), bf16),
            pltpu.VMEM((3, features, width), bf16),
            pltpu.VMEM((LANES, features), bf16),
            pltpu.VMEM((rows, width), bf16),
            pltpu.VMEM((heads, features), bf16),
            pltpu.VMEM((1, heads), f32),
            pltpu.VMEM((3, rows, width), f32),
            pltpu.VMEM((2, rows, width), f32),
            pltpu.VMEM((rows, LANES), f32),
            pltpu.VMEM((rows, LANES), f32),
            pltpu.VMEM((heads, rows, 4 * dim), f32),
            pltpu.VMEM((2, 2 * heads, 2, dim, dim), bf16),
            pltpu.VMEM((2, half, dim, dim), bf16),
            pltpu.VMEM((2, heads, dim, dim), bf16),
            pltpu.VMEM((half, dim, dim), bf16),
            pltpu.VMEM((heads, dim, dim), bf16),
            pltpu.VMEM((2 * heads, dim, dim), f32),
            pltpu.VMEM((2, 4, 2, rows, part), bf16),
            pltpu.VMEM((2, 2 * part, 4 * rows), bf16),
            pltpu.VMEM((rows, 3 * width + LANES), bf16),
            pltpu.VMEM((2, 3, 4 * rows, width // 2), bf16),
            pltpu.VMEM((4, 16, rows), bf16),
            pltpu.VMEM((2, 3, part, width // 2), bf16),
            pltpu.VMEM((2, 3, part, width // 2), bf16),
            pltpu.VMEM((16, part), f32),
            pltpu.VMEM((16, part), f32),
            pltpu.VMEM((rows, features // groups), f32),
            pltpu.VMEM((3, rows, features // groups), bf16),
            pltpu.VMEM((groups + 1, rows, features // groups), bf16),
            dma((7,)),
            dma((11,)),
            dma((11,)),
            dma((4,)),
            dma((4,)),
            dma((2,)),
            dma((2,)),
            dma((2,)),
            dma((2,)),
            dma((3,)),
            dma,
            dma,
            dma((2, 4)),
            dma((2, 4)),
            dma((2, 4)),
            dma((2, 4)),
            dma((2, 4)),
            dma((2, 4)),
            dma((2, 4)),
            dma((2, 4)),
            dma((3, 2)),
            dma((groups + 1, 2)),
            dma((9,)),
        ],
        compiler_params=pltpu.CompilerParams(
            vmem_limit_bytes=60 * 1024 * 1024, collective_id=1, has_side_effects=True
        ),
        name="layer",
    )(tokens, *weights, d_out, w_beta.T, b_beta.reshape(1, heads))
    d_x, grad_q, grad_k, grad_v, tail, bias = place(outs[:4], outs[4], heads)
    return d_x, grad_q, grad_k, grad_v, tail.T, bias.reshape(heads)


def per_device(tokens, w_query, w_key, w_value, w_beta, b_beta, d_out):
    token_count, features = tokens.shape
    heads = w_beta.shape[1]
    width = w_query.shape[1]
    dim = width // heads
    f32 = jnp.float32
    shards, groups = lax.axis_size("seq"), lax.axis_size("head")
    weights = (w_query, w_key, w_value)
    fits = heads % 2 == 0 and 2 * heads <= 8 and width * groups == features and dim == LANES
    if shards == 8 and groups == 4 and fits and features // shards == token_count:
        return whole_layer(tokens, weights, w_beta, b_beta, d_out)
    q, k, v = (jnp.dot(tokens, w, preferred_element_type=f32) for w in weights)
    w_last = jnp.pad(w_beta, ((0, 0), (0, LANES - heads)))
    z = jnp.dot(tokens, w_last, preferred_element_type=f32) + jnp.pad(b_beta, (0, LANES - heads))
    params = pltpu.CompilerParams(vmem_limit_bytes=60 * 1024 * 1024)
    columns = lax.all_to_all(tokens, "seq", split_axis=1, concat_axis=0, tiled=True)
    maps, mid = pl.pallas_call(
        functools.partial(summary_kernel, heads, dim),
        out_shape=(
            jax.ShapeDtypeStruct((2 * heads, 2, dim, dim), jnp.bfloat16),
            jax.ShapeDtypeStruct((heads, token_count, 4 * dim), f32),
        ),
        compiler_params=params,
        name="summary",
    )(q, k, v, z, d_out)
    states = gathered_states(maps, heads)
    grads = pl.pallas_call(
        functools.partial(gradient_kernel, heads, dim),
        out_shape=jax.ShapeDtypeStruct((token_count, 3 * width + LANES), jnp.bfloat16),
        compiler_params=params,
        name="gradient",
    )(q, k, z, d_out, mid, states)
    whole = lax.all_gather(grads, "seq", axis=0, tiled=True)
    partial = jnp.dot(grads[:, 3 * width : 3 * width + heads], w_beta.T, preferred_element_type=f32)
    for i, w in enumerate(weights):
        partial = partial + jnp.dot(
            grads[:, i * width : (i + 1) * width], w.T, preferred_element_type=f32
        )
    d_x = lax.psum_scatter(
        partial.astype(jnp.bfloat16), "head", scatter_dimension=1, tiled=True
    )

    def weight_grad(block):
        return lax.dot_general(
            columns, block, (((0,), (0,)), ((), ())), preferred_element_type=f32
        )

    found = [weight_grad(whole[:, i * width : (i + 1) * width]) for i in range(3)]
    tail = whole[:, 3 * width :]
    grad_wbeta = weight_grad(tail)[:, :heads]
    sums = jnp.sum(tail.astype(f32), 0)
    return (d_x, *found, grad_wbeta, sums[:heads] + sums[heads : 2 * heads])


def solution(mesh):
    in_specs = (
        P("seq", None),
        P(None, "head"),
        P(None, "head"),
        P(None, "head"),
        P(None, "head"),
        P("head"),
        P("seq", "head"),
    )
    out_specs = (
        P("seq", "head"),
        P("seq", "head"),
        P("seq", "head"),
        P("seq", "head"),
        P("seq", "head"),
        P("head"),
    )
    return jax.shard_map(
        per_device, mesh=mesh, in_specs=in_specs, out_specs=out_specs, check_vma=False
    )
```
